256 devices in a mesh: tile: 8 (over x, core), dev: 32 (over z, y).
Axes of the slice: x: 4, y: 4, z: 8, core: 2. Of those that a mesh axis runs over, the one named last changes fastest.
Arguments:
- features: bfloat16 [2048, 64, 128], P(('tile', 'dev')), may hold values from -6 to 6
- morton_pos: int32 [2048], P(('tile', 'dev')), may hold values from 0 to 255, as said below
- neighbours: int32 [2048, 27], P(('tile', 'dev')), may hold values from 0 to 24, as said below
- rim: int32 [1024], P(('tile', 'dev')), may hold values from 0 to 7, as said below
- cotangent: bfloat16 [2048, 64, 128], P(('tile', 'dev')), may hold values from -6 to 6
- weight_one: bfloat16 [3456, 128], replicated, may hold values from -0.109375 to 0.109375
- weight_two: bfloat16 [3456, 128], replicated, may hold values from -0.109375 to 0.109375
Outputs:
- output: bfloat16 [2048, 64, 128], P(('tile', 'dev'))
- input_grad: bfloat16 [2048, 64, 128], P(('tile', 'dev'))
- grad_one: float32 [3456, 128], replicated
- grad_two: float32 [3456, 128], replicated
The draws below stay inside these ranges and needn't reach their ends.
Inputs may be any that keep to these rules, and one draw needn't show every extreme that they name: `morton_pos`: within each super-tile the positions form a permutation of its 256 Morton rows; the 8 scan rows of one device go to at most 2 rows of any one device (position // 8), a bound reached in every draw. `neighbours`: lists come from block coordinates of a sparse map, each device owning a box of 6 x 6 x 2 block cells, tile stepping along x and dev along y: block a's neighbour at offset o is b exactly when b's neighbour at offset 26 - o is a; every block that a neighbouring device reads is in that device's rim list; the four corner columns of every box are empty, so no block reads a device diagonal to its own. `rim`: 4 different blocks of the device.
All inputs are finite; a program needn't handle non-finite values.
Results may differ from the reference program's by a relative error of at most 0.0033.
Values may be sent and summed in bfloat16 or wider, within the bound.
A program may use at most 128 MiB of HBM per device.

```python
import math
import jax
import jax.numpy as jnp
import numpy as np
from jax import lax

CH = 128
EDGE = 4
VOX = 64
KCOLS = 3456
BLK = 8
RIM = 4
BOX_XY = 6
BOX_Z = 2
CAP = 2
BLOCKS = 2048
N_TILE = 8
N_DEV = 32


def layout(key):
    cells = BOX_XY * BOX_XY * BOX_Z
    index = np.arange(cells)
    cell_x = index // (BOX_XY * BOX_Z)
    cell_y = index // BOX_Z % BOX_XY
    edge_x = (cell_x == 0) | (cell_x == BOX_XY - 1)
    edge_y = (cell_y == 0) | (cell_y == BOX_XY - 1)
    on_face = (edge_x | edge_y) & ~(edge_x & edge_y)
    inside = ~(edge_x | edge_y)
    face_cells = jnp.asarray(index[on_face], jnp.int32)
    inner_cells = jnp.asarray(index[inside], jnp.int32)
    devices = N_TILE * N_DEV
    device_keys = jax.random.split(jax.random.fold_in(key, 11), devices)

    def place(device_key):
        keys = jax.random.split(device_key, 4)
        chosen_face = jax.random.permutation(keys[0], face_cells)[:RIM]
        chosen_inner = jax.random.permutation(keys[1], inner_cells)[:BLK - RIM]
        chosen = jnp.concatenate([chosen_face, chosen_inner])
        order = jax.random.permutation(keys[2], BLK)
        cell_of_slot = chosen[order]
        slot_of_chosen = jnp.zeros((BLK,), jnp.int32).at[order].set(jnp.arange(BLK, dtype=jnp.int32))
        rim_order = jax.random.permutation(keys[3], RIM)
        rim_slots = slot_of_chosen[rim_order]
        rim_of_face = jnp.zeros((RIM,), jnp.int32).at[rim_order].set(jnp.arange(RIM, dtype=jnp.int32))
        slot_grid = jnp.full((cells,), -1, jnp.int32).at[cell_of_slot].set(jnp.arange(BLK, dtype=jnp.int32))
        rim_grid = jnp.full((cells,), -1, jnp.int32).at[chosen_face].set(rim_of_face)
        return (cell_of_slot, rim_slots, slot_grid, rim_grid)
    cell_of_slot, rim_slots, slot_grid, rim_grid = jax.vmap(place)(device_keys)
    offsets = np.arange(27)
    off_x = jnp.asarray(offsets // 9 - 1, jnp.int32)[None, None, :]
    off_y = jnp.asarray(offsets // 3 % 3 - 1, jnp.int32)[None, None, :]
    off_z = jnp.asarray(offsets % 3 - 1, jnp.int32)[None, None, :]
    device = jnp.arange(devices, dtype=jnp.int32)[:, None, None]
    tile_of = device // N_DEV
    dev_of = device % N_DEV
    cell = cell_of_slot[:, :, None]
    near_x = cell // (BOX_XY * BOX_Z) + off_x
    near_y = cell // BOX_Z % BOX_XY + off_y
    near_z = cell % BOX_Z + off_z
    step_x = jnp.where(near_x < 0, -1, jnp.where(near_x >= BOX_XY, 1, 0))
    step_y = jnp.where(near_y < 0, -1, jnp.where(near_y >= BOX_XY, 1, 0))
    local_x = near_x - step_x * BOX_XY
    local_y = near_y - step_y * BOX_XY
    tile_new = tile_of + step_x
    dev_new = dev_of + step_y
    valid = (near_z >= 0) & (near_z < BOX_Z) & (tile_new >= 0) & (tile_new < N_TILE) & (dev_new >= 0) & (dev_new < N_DEV) & ((step_x == 0) | (step_y == 0))
    other = jnp.clip(tile_new, 0, N_TILE - 1) * N_DEV + jnp.clip(dev_new, 0, N_DEV - 1)
    other_cell = (local_x * BOX_XY + local_y) * BOX_Z + jnp.clip(near_z, 0, BOX_Z - 1)
    slot_there = slot_grid[other, other_cell]
    rim_there = rim_grid[other, other_cell]
    sides = jnp.where(step_x == -1, 0, jnp.where(step_x == 1, 1, jnp.where(step_y == -1, 2, 3)))
    is_local = (step_x == 0) & (step_y == 0)
    value = jnp.where(is_local, slot_there, BLK + sides * RIM + rim_there)
    value = jnp.where(valid & (slot_there >= 0), value, BLK + 4 * RIM)
    neighbours = value.reshape(devices * BLK, 27).astype(jnp.int32)
    tile_keys = jax.random.split(jax.random.fold_in(key, 23), N_TILE)

    def regroup(tile_key):
        keys = jax.random.split(tile_key, 4)
        spare = jnp.repeat(jnp.arange(1, N_DEV, dtype=jnp.int32), CAP)
        picked = jax.random.permutation(keys[0], spare)[:BLK - CAP]
        peers = jnp.arange(N_DEV, dtype=jnp.int32)
        counts = jnp.sum((picked[:, None] == peers[None, :]).astype(jnp.int32), axis=0)
        counts = counts + jnp.where(peers == 0, CAP, 0)
        shuffle = jax.random.permutation(keys[1], N_DEV)
        matrix = counts[(shuffle[None, :] - peers[:, None]) % N_DEV]
        offset = jnp.cumsum(matrix, axis=0) - matrix
        row_keys = jax.random.split(keys[2], N_DEV)
        dest_keys = jax.random.split(keys[3], N_DEV)

        def arrange_one(dest_key):
            return jax.random.permutation(dest_key, BLK)
        arrange = jax.vmap(arrange_one)(dest_keys)

        def source(src, row_key):
            counts_here = matrix[src]
            dest = jnp.repeat(peers, counts_here, total_repeat_length=BLK)
            start = jnp.cumsum(counts_here) - counts_here
            spot = jnp.arange(BLK, dtype=jnp.int32) - start[dest] + offset[src, dest]
            position = dest * BLK + arrange[dest, spot]
            return position[jax.random.permutation(row_key, BLK)]
        return jax.vmap(source)(peers, row_keys).reshape(-1)
    morton = jax.vmap(regroup)(tile_keys).reshape(-1).astype(jnp.int32)
    return (morton, neighbours, rim_slots.reshape(-1).astype(jnp.int32))


def draw_morton_pos(key, part):
    return layout(key)[0]


def draw_neighbours(key, part):
    return layout(key)[1]


def draw_rim(key, part):
    return layout(key)[2]


def level_of(rng, extent, cuts, low, top_value):
    factor_of, own = 1.0, jax.random.fold_in(rng, 6)
    for axis_at, parts in cuts:
        steps = jnp.exp(jax.random.uniform(jax.random.fold_in(own, axis_at), (parts,), jnp.float32, low / len(cuts), top_value / len(cuts)))
        factor_of = factor_of * jnp.repeat(steps, extent[axis_at] // parts).reshape([-1 if axis == axis_at else 1 for axis in range(len(extent))])
    return factor_of


def bell_draw(rng, dims, deviation, reach, cuts=(), held_as=jnp.bfloat16):
    values = deviation * jax.random.normal(rng, dims, jnp.float32)
    if cuts:
        values = values * level_of(rng, dims, cuts, -0.22, 0.18)
    return jnp.clip(values, -reach, reach).astype(held_as)


def setup_inputs(seed: int = 0) -> dict:
    key_of = jax.random.split(jax.random.key(seed), 8)
    features = bell_draw(key_of[0], (BLOCKS, VOX, CH), 1.0, 6.0, ((0, 256),))
    morton_pos = draw_morton_pos(jax.random.fold_in(key_of[7], 71), 0)
    neighbours = draw_neighbours(jax.random.fold_in(key_of[7], 71), 0)
    rim = draw_rim(jax.random.fold_in(key_of[7], 71), 0)
    cotangent = bell_draw(key_of[4], (BLOCKS, VOX, CH), 1.0, 6.0, ((0, 256),))
    weight_one = bell_draw(key_of[5], (KCOLS, CH), KCOLS ** -0.5, 0.109375)
    weight_two = bell_draw(key_of[6], (KCOLS, CH), KCOLS ** -0.5, 0.109375)
    return dict(features=features, morton_pos=morton_pos, neighbours=neighbours, rim=rim, cotangent=cotangent, weight_one=weight_one, weight_two=weight_two)


def padded_cube(blocks):
    count = blocks.shape[0]
    channels = blocks.shape[-1]
    cube = blocks.reshape(count, 3, 3, 3, EDGE, EDGE, EDGE, channels)
    for axis_pass in range(3):
        cube = jnp.concatenate([cube[:, 0][:, :, :, EDGE - 1:], cube[:, 1], cube[:, 2][:, :, :, :1]], axis=3)
    return cube

def patch_columns(blocks):
    count = blocks.shape[0]
    channels = blocks.shape[-1]
    cube = padded_cube(blocks)
    pieces = [cube[:, offset_x:offset_x + EDGE, offset_y:offset_y + EDGE, offset_z:offset_z + EDGE] for offset_x in range(3) for offset_y in range(3) for offset_z in range(3)]
    return jnp.concatenate(pieces, axis=-1).reshape(count * EDGE ** 3, 27 * channels)

def global_rows(neighbours, rim):
    device = (jnp.arange(BLOCKS, dtype=jnp.int32) // BLK)[:, None]
    tile_of = device // N_DEV
    dev_of = device % N_DEV
    slot = jnp.clip(neighbours - BLK, 0, 4 * RIM - 1)
    sides = slot // RIM
    place = slot % RIM
    tile_new = tile_of + jnp.where(sides == 0, -1, jnp.where(sides == 1, 1, 0))
    dev_new = dev_of + jnp.where(sides == 2, -1, jnp.where(sides == 3, 1, 0))
    valid = (tile_new >= 0) & (tile_new < N_TILE) & (dev_new >= 0) & (dev_new < N_DEV)
    other = jnp.clip(tile_new, 0, N_TILE - 1) * N_DEV + jnp.clip(dev_new, 0, N_DEV - 1)
    remote = other * BLK + rim[other * RIM + place]
    result = jnp.where(neighbours < BLK, device * BLK + neighbours, jnp.where((neighbours < BLK + 4 * RIM) & valid, remote, BLOCKS))
    return result.astype(jnp.int32)

def reference(features, morton_pos, neighbours, rim, cotangent, weight_one, weight_two):
    per_tile = N_DEV * BLK
    scan_rows = jnp.arange(BLOCKS, dtype=jnp.int32)
    target = (scan_rows // per_tile * per_tile + morton_pos).astype(jnp.int32)
    morton = jnp.zeros_like(features).at[target].set(features)
    table_rows = global_rows(neighbours, rim).reshape(-1, BLK, 27)

    def forward(table, weight):
        padded = jnp.concatenate([table, jnp.zeros((1, VOX, CH), table.dtype)])

        def one_group(rows):
            return jnp.dot(patch_columns(padded[rows]), weight, preferred_element_type=jnp.float32)
        return lax.map(one_group, table_rows).reshape(BLOCKS, VOX, CH)

    def backward(table, grad, weight):
        padded = jnp.concatenate([table, jnp.zeros((1, VOX, CH), table.dtype)])
        grads = grad.reshape(-1, BLK * VOX, CH)

        def step(carry, inputs):
            total, wgrad = carry
            rows, local_grad = inputs
            blocks = padded[rows]
            columns = patch_columns(blocks)
            wgrad = wgrad + lax.dot_general(columns, local_grad, (((0,), (0,)), ((), ())), preferred_element_type=jnp.float32)
            back_cols = lax.dot_general(local_grad, weight, (((1,), (1,)), ((), ())), preferred_element_type=jnp.float32)
            primal = jnp.zeros(blocks.shape, jnp.float32)
            unused, pullback = jax.vjp(patch_columns, primal)
            back_blocks = pullback(back_cols)[0]
            total = total.at[rows.reshape(-1)].add(back_blocks.reshape(-1, VOX, CH))
            return ((total, wgrad), None)
        start = (jnp.zeros((BLOCKS + 1, VOX, CH), jnp.float32), jnp.zeros((27 * CH, CH), jnp.float32))
        (total, wgrad), unused = lax.scan(step, start, (table_rows, grads))
        return (total[:BLOCKS], wgrad)
    pre_one = forward(morton, weight_one)
    hidden = jax.nn.silu(pre_one).astype(jnp.bfloat16)
    pre_two = forward(hidden, weight_two)
    output = (morton.astype(jnp.float32) + pre_two).astype(jnp.bfloat16)
    hidden_grad, grad_two = backward(hidden, cotangent, weight_two)
    gate = jax.nn.sigmoid(pre_one)
    pre_grad = (hidden_grad * gate * (1.0 + pre_one * (1.0 - gate))).astype(jnp.bfloat16)
    morton_part, grad_one = backward(morton, pre_grad, weight_one)
    morton_grad = (morton_part + cotangent.astype(jnp.float32)).astype(jnp.bfloat16)
    input_grad = morton_grad[target]
    scale = 1.0 / math.sqrt(BLOCKS * VOX)
    return (output, input_grad, grad_one * scale, grad_two * scale)
```

```python
import functools
import math

import jax
import jax.numpy as jnp
import numpy as np
from jax import lax
from jax.experimental import pallas as pl
from jax.experimental.pallas import tpu as pltpu
from jax.sharding import PartitionSpec as P

EDGE = 4
PLANE = EDGE * EDGE
BLK = 8
VOX = 64
CH = 128
RIM = 4
HALF = 27 * CH // 2
QUARTER = HALF // 4
TILES = QUARTER // 16
F32 = jnp.float32
BF16 = jnp.bfloat16
I32 = jnp.int32


def shift_matrix():
    result = np.zeros((9 * PLANE, 9 * PLANE), np.float32)
    for ky in range(3):
        for kz in range(3):
            for j in range(EDGE):
                for k in range(EDGE):
                    y, z = j + ky - 1, k + kz - 1
                    dy, dz = y // EDGE + 1, z // EDGE + 1
                    source = ((dy * 3 + dz) * EDGE + y % EDGE) * EDGE + z % EDGE
                    result[((ky * 3 + kz) * EDGE + j) * EDGE + k, source] = 1.0
    return result


def dot(left, right):
    return jnp.dot(left, right, preferred_element_type=F32)


def unit_kernel(
    n_tile,
    n_dev,
    scale,
    pos,
    nbr,
    rim,
    feat,
    cot,
    w1,
    w2,
    smat,
    out_output,
    out_grad,
    out_sums,
    idxv,
    idxs,
    slotv,
    slots,
    labels,
    packed,
    arrived,
    repacked,
    returned,
    tab_m,
    tab_c,
    tab_h,
    tab_p,
    own,
    rims,
    wt1,
    wt2,
    planes,
    y_m,
    y_c,
    y_x,
    pre_one,
    hidden_grad,
    grads,
    core_in,
    x_out,
    x_in,
    own_sum,
    z_out,
    z_in,
    final,
    sem_local,
    sem_a2a,
    sem_lab,
    sem_back,
    sem_halo_s,
    sem_halo_r,
    sem_sum_s,
    sem_sum_r,
):
    tile = lax.axis_index("tile")
    dev = lax.axis_index("dev")
    core = lax.rem(tile, 2)
    chip_x = tile // 2
    n_x = n_tile // 2

    def remote(src, dst, send, recv, **where):
        return pltpu.make_async_remote_copy(
            src_ref=src,
            dst_ref=dst,
            send_sem=send,
            recv_sem=recv,
            device_id=where,
            device_id_type=pl.DeviceIdType.MESH,
        )

    def await_bytes(ref, sem):
        pltpu.make_async_copy(ref, ref, sem).wait()

    barrier = pltpu.get_barrier_semaphore()

    @pl.loop(1, n_dev)
    def _(d):
        pl.semaphore_signal(barrier, inc=1, device_id={"dev": lax.rem(dev + d, n_dev)})

    @pl.loop(1, n_tile)
    def _(d):
        pl.semaphore_signal(barrier, inc=1, device_id={"tile": lax.rem(tile + d, n_tile)})

    sub = lax.broadcasted_iota(I32, (8, CH), 0)
    lane = lax.broadcasted_iota(I32, (8, CH), 1)
    posv = jnp.zeros((8, CH), I32)
    for r in range(BLK):
        posv = jnp.where(sub == r, pos[r], posv)
    owner = posv // BLK
    count = jnp.zeros((8, CH), I32)
    for r in range(BLK):
        count = count + jnp.where((owner == pos[r] // BLK) & (sub > r), 1, 0)
    slot_of_row = lax.rem(owner - dev + n_dev, n_dev) * 2 + count
    hit = lane == slot_of_row
    row_of_slot = jnp.min(jnp.where(hit, sub, BLK - 1), axis=0, keepdims=True)
    label_of_slot = jnp.min(jnp.where(hit, lax.rem(posv, BLK), BLK), axis=0, keepdims=True)
    idxv[0] = jnp.broadcast_to(row_of_slot, (8, CH))
    idxv[1] = jnp.minimum(slot_of_row, 2 * n_dev - 1)
    labels[0] = jnp.broadcast_to(label_of_slot, (8, CH))
    to_scalars = pltpu.make_async_copy(idxv, idxs, sem_local.at[0])
    to_scalars.start()

    def pack_rims(rows, which):
        for h in range(RIM):
            rims[which, h] = rows[rim[h]]

    def halo_copies(which, table):
        result = []
        for q, where in enumerate(
            (
                dict(tile=lax.rem(tile + 1, n_tile)),
                dict(tile=lax.rem(tile + n_tile - 1, n_tile)),
                dict(dev=lax.rem(dev + 1, n_dev)),
                dict(dev=lax.rem(dev + n_dev - 1, n_dev)),
            )
        ):
            result.append(
                remote(
                    rims.at[which],
                    table.at[pl.ds(BLK + q * RIM, RIM)],
                    sem_halo_s.at[which, q],
                    sem_halo_r.at[which, q],
                    **where,
                )
            )
        return result

    def finish_halo(copies, table):
        for copy in copies:
            copy.wait()
        edges = (tile == 0, tile == n_tile - 1, dev == 0, dev == n_dev - 1)
        for q, edge in enumerate(edges):

            @pl.when(edge)
            def _(q=q):
                table[BLK + q * RIM : BLK + (q + 1) * RIM] = jnp.zeros((RIM, VOX, CH), BF16)

    for table in (tab_m, tab_c, tab_h, tab_p):
        table[BLK + 4 * RIM] = jnp.zeros((VOX, CH), BF16)
    tab_c[0:BLK] = cot[...]
    pack_rims(cot, 0)
    to_scalars.wait()

    @pl.loop(0, n_dev)
    def _(d):
        for c in range(2):
            packed[d, c] = feat[idxs[0, 0, 2 * d + c]]

    arrived[0] = packed[0]

    pl.semaphore_wait(barrier, n_dev + n_tile - 2)

    @pl.loop(1, n_dev)
    def _(d):
        where = lax.rem(dev + d, n_dev)
        remote(labels.at[0], labels.at[d], sem_lab.at[0], sem_lab.at[1], dev=where).start()
        remote(packed.at[d], arrived.at[d], sem_a2a.at[0], sem_a2a.at[1], dev=where).start()

    halo_c = halo_copies(0, tab_c)
    for copy in halo_c:
        copy.start()

    def flip_weights(source, target):
        for o in range(27):
            piece = source[o * CH : (o + 1) * CH, :].astype(F32)
            target[(26 - o) * CH : (27 - o) * CH, :] = piece.T.astype(BF16)

    def expand(table, y):
        @pl.loop(0, BLK)
        def _(b):
            for i in range(6):
                dx = 0 if i == 0 else (2 if i == 5 else 1)
                row = (i + EDGE - 1) % EDGE
                for t in range(9):
                    entry = nbr[b, dx * 9 + t]
                    planes[t * PLANE : (t + 1) * PLANE, i * CH : (i + 1) * CH] = table[
                        entry, row * PLANE : (row + 1) * PLANE, :
                    ]
            moved = dot(smat[...], planes[...]).astype(BF16)
            for i in range(6):
                for t in range(9):
                    y[b, i, :, t * CH : (t + 1) * CH] = moved[
                        t * PLANE : (t + 1) * PLANE, i * CH : (i + 1) * CH
                    ]

    def columns(y, kx):
        return y[:, kx : kx + EDGE].reshape(BLK * VOX, 9 * CH)

    def conv(y, w):
        return (
            dot(columns(y, 0), w[0 : 9 * CH, :])
            + dot(columns(y, 1), w[9 * CH : 18 * CH, :])
            + dot(columns(y, 2), w[18 * CH : 27 * CH, :])
        )

    flip_weights(w2, wt2)
    flip_weights(w1, wt1)
    finish_halo(halo_c, tab_c)
    expand(tab_c, y_c)
    hidden_grad[...] = conv(y_c, wt2)

    await_bytes(labels.at[pl.ds(1, n_dev - 1)], sem_lab.at[1])
    label_at = jnp.zeros((8, CH), I32)
    for d in range(n_dev):
        label_at = jnp.where(lane // 2 == d, labels[d], label_at)
    label_at = jnp.where(lane < 2 * n_dev, label_at, BLK)
    slotv[0] = jnp.minimum(label_at, BLK - 1)
    slotv[1] = jnp.broadcast_to(
        jnp.max(jnp.where(label_at == sub, lane, 0), axis=1, keepdims=True), (8, CH)
    )
    to_slots = pltpu.make_async_copy(slotv, slots, sem_local.at[0])
    to_slots.start()
    to_slots.wait()
    await_bytes(arrived.at[pl.ds(1, n_dev - 1)], sem_a2a.at[1])
    for s in range(BLK):
        linear = slots[1, s, 0]
        own[0, s] = arrived[linear // 2, lax.rem(linear, 2)]
    tab_m[0:BLK] = own[0]
    pack_rims(own.at[0], 1)
    halo_m = halo_copies(1, tab_m)
    for copy in halo_m:
        copy.start()
    finish_halo(halo_m, tab_m)
    expand(tab_m, y_m)
    pre = conv(y_m, w1)
    gate = jax.nn.sigmoid(pre)
    hidden = (pre * gate).astype(BF16)
    pre_grad = (hidden_grad[...] * gate * (1.0 + pre * (1.0 - gate))).astype(BF16)
    tab_h[0:BLK] = hidden.reshape(BLK, VOX, CH)
    tab_p[0:BLK] = pre_grad.reshape(BLK, VOX, CH)
    own[1] = hidden.reshape(BLK, VOX, CH)
    own[2] = pre_grad.reshape(BLK, VOX, CH)
    pack_rims(own.at[1], 2)
    pack_rims(own.at[2], 3)
    halo_h = halo_copies(2, tab_h)
    halo_p = halo_copies(3, tab_p)
    for copy in halo_h + halo_p:
        copy.start()

    partner = dict(tile=tile + 1 - 2 * core)

    def half_rows(which):
        return pl.ds(pl.multiple_of(which * HALF, 16), HALF)

    def core_copy(q):
        return remote(
            grads.at[q, half_rows(1 - core)],
            core_in.at[q],
            sem_sum_s.at[q, 0],
            sem_sum_r.at[q, 0],
            **partner,
        )

    hidden_t = own[1].reshape(BLK * VOX, CH).astype(F32).T.astype(BF16)
    for kx in range(3):
        part = dot(hidden_t, columns(y_c, kx))
        for t in range(9):
            o = 26 - (kx * 9 + t)
            grads[1, o * CH : (o + 1) * CH, :] = part[:, t * CH : (t + 1) * CH]
    core_copy(1).start()
    pre_grad_t = own[2].reshape(BLK * VOX, CH).astype(F32).T.astype(BF16)
    for kx in range(3):
        part = dot(pre_grad_t, columns(y_m, kx))
        for t in range(9):
            o = kx * 9 + t
            grads[0, o * CH : (o + 1) * CH, :] = part[:, t * CH : (t + 1) * CH].T
    core_copy(0).start()

    def x_copy(q, e):
        other = lax.rem(chip_x + e, n_x)
        return remote(
            x_out.at[q, other],
            x_in.at[q, e - 1],
            sem_sum_s.at[q, 1],
            sem_sum_r.at[q, 1],
            tile=other * 2 + core,
        )

    def both_cores(q, chunk):
        start = pl.multiple_of(core * HALF + chunk * QUARTER, 16)
        start_in = pl.multiple_of(chunk * QUARTER, 16)
        return grads[q, pl.ds(start, QUARTER), :] + core_in[q, pl.ds(start_in, QUARTER), :]

    def start_x(q):
        core_copy(q).wait_recv()
        for j in range(n_x):
            x_out[q, j] = both_cores(q, j).astype(BF16)
        for e in range(1, n_x):
            x_copy(q, e).start()

    def start_z(q):
        await_bytes(x_in.at[q], sem_sum_r.at[q, 1])
        total = both_cores(q, chip_x)
        for e in range(n_x - 1):
            total = total + x_in[q, e].astype(F32)
        own_sum[q, 0:QUARTER] = total
        own_sum[q, QUARTER:] = jnp.zeros((n_dev * 16 - QUARTER, CH), F32)
        z_out[q, 0:TILES] = total.astype(BF16).reshape(TILES, 16, CH)
        z_out[q, TILES:] = jnp.zeros((n_dev - TILES, 16, CH), BF16)

        @pl.loop(1, n_dev)
        def _(d):
            where = lax.rem(dev + d, n_dev)
            remote(
                z_out.at[q, where], z_in.at[q, d - 1], sem_sum_s.at[q, 2], sem_sum_r.at[q, 2], dev=where
            ).start()

    def start_gather_z(q):
        await_bytes(z_in.at[q], sem_sum_r.at[q, 2])
        total = own_sum[q, pl.ds(pl.multiple_of(dev * 16, 16), 16), :]
        for d in range(n_dev - 1):
            total = total + z_in[q, d].astype(F32)
        final[q, core, chip_x, dev] = (total * scale).astype(BF16)

        @pl.loop(1, n_dev)
        def _(d):
            where = lax.rem(dev + d, n_dev)
            mine = final.at[q, core, chip_x, dev]
            remote(mine, mine, sem_sum_s.at[q, 3], sem_sum_r.at[q, 3], dev=where).start()

    def gather_x_copy(q, e):
        mine = final.at[q, core, chip_x, pl.ds(0, TILES)]
        return remote(
            mine, mine, sem_sum_s.at[q, 4], sem_sum_r.at[q, 4], tile=lax.rem(chip_x + e, n_x) * 2 + core
        )

    def start_gather_x(q):
        await_bytes(z_in.at[q], sem_sum_r.at[q, 3])
        for e in range(1, n_x):
            gather_x_copy(q, e).start()

    def gather_core_copy(q):
        mine = final.at[q, core, :, pl.ds(0, TILES)]
        return remote(mine, mine, sem_sum_s.at[q, 5], sem_sum_r.at[q, 5], **partner)

    def start_gather_core(q):
        await_bytes(x_in.at[q], sem_sum_r.at[q, 4])
        gather_core_copy(q).start()

    start_x(1)
    start_x(0)
    finish_halo(halo_h, tab_h)
    expand(tab_h, y_x)
    pre_two = conv(y_x, w2)
    out_output[...] = (
        (own[0].reshape(BLK * VOX, CH).astype(F32) + pre_two).astype(BF16).reshape(BLK, VOX, CH)
    )
    start_z(1)
    start_z(0)
    finish_halo(halo_p, tab_p)
    expand(tab_p, y_x)
    back = conv(y_x, wt1) + cot[...].reshape(BLK * VOX, CH).astype(F32)
    own[1] = back.astype(BF16).reshape(BLK, VOX, CH)

    @pl.loop(0, n_dev)
    def _(d):
        for c in range(2):
            repacked[d, c] = own[1, slots[0, 0, 2 * d + c]]

    returned[0] = repacked[0]

    @pl.loop(1, n_dev)
    def _(d):
        where = lax.rem(dev - d + n_dev, n_dev)
        remote(repacked.at[d], returned.at[d], sem_back.at[0], sem_back.at[1], dev=where).start()

    start_gather_z(1)
    start_gather_z(0)
    start_gather_x(1)
    start_gather_x(0)
    start_gather_core(1)
    start_gather_core(0)
    await_bytes(returned.at[pl.ds(1, n_dev - 1)], sem_back.at[1])
    for r in range(BLK):
        linear = idxs[1, r, 0]
        out_grad[r] = returned[linear // 2, lax.rem(linear, 2)]
    gather_core_copy(1).wait_recv()
    gather_core_copy(0).wait_recv()
    out_sums[...] = final[...]

    await_bytes(labels.at[pl.ds(1, n_dev - 1)], sem_lab.at[0])
    await_bytes(packed.at[pl.ds(1, n_dev - 1)], sem_a2a.at[0])
    await_bytes(repacked.at[pl.ds(1, n_dev - 1)], sem_back.at[0])
    for q in range(2):
        core_copy(q).wait_send()
        await_bytes(x_in.at[q], sem_sum_s.at[q, 1])
        await_bytes(z_in.at[q], sem_sum_s.at[q, 2])
        await_bytes(z_in.at[q], sem_sum_s.at[q, 3])
        await_bytes(x_in.at[q], sem_sum_s.at[q, 4])
        gather_core_copy(q).wait_send()


def per_device(
    n_tile, n_dev, features, morton_pos, neighbours, rim, cotangent, weight_one, weight_two
):
    blocks, voxels, channels = features.shape
    scale = 1.0 / math.sqrt(blocks * voxels * n_tile * n_dev)
    n_x = n_tile // 2
    smem = pl.BlockSpec(memory_space=pltpu.SMEM)
    vmem = pl.BlockSpec(memory_space=pltpu.VMEM)
    dma = pltpu.SemaphoreType.DMA
    block_table = pltpu.VMEM((BLK + 4 * RIM + 1, VOX, CH), BF16)
    wide = pltpu.VMEM((BLK, 6, PLANE, 9 * CH), BF16)
    flat = pltpu.VMEM((BLK * VOX, CH), F32)
    slab = pltpu.VMEM((n_dev, 2, VOX, CH), BF16)
    output, input_grad, sums = pl.pallas_call(
        functools.partial(unit_kernel, n_tile, n_dev, scale),
        out_shape=(
            jax.ShapeDtypeStruct(features.shape, BF16),
            jax.ShapeDtypeStruct(features.shape, BF16),
            jax.ShapeDtypeStruct((2, 2, n_x, n_dev, 16, CH), BF16),
        ),
        in_specs=[smem, smem, smem, vmem, vmem, vmem, vmem, vmem],
        out_specs=(vmem, vmem, vmem),
        scratch_shapes=[
            pltpu.VMEM((2, 8, CH), I32),
            pltpu.SMEM((2, 8, CH), I32),
            pltpu.VMEM((2, 8, CH), I32),
            pltpu.SMEM((2, 8, CH), I32),
            pltpu.VMEM((n_dev, 8, CH), I32),
            slab,
            slab,
            slab,
            slab,
            block_table,
            block_table,
            block_table,
            block_table,
            pltpu.VMEM((3, BLK, VOX, CH), BF16),
            pltpu.VMEM((4, RIM, VOX, CH), BF16),
            pltpu.VMEM((27 * CH, CH), BF16),
            pltpu.VMEM((27 * CH, CH), BF16),
            pltpu.VMEM((9 * PLANE, 6 * CH), BF16),
            wide,
            wide,
            wide,
            flat,
            flat,
            pltpu.VMEM((2, 27 * CH, CH), F32),
            pltpu.VMEM((2, HALF, CH), F32),
            pltpu.VMEM((2, n_x, QUARTER, CH), BF16),
            pltpu.VMEM((2, n_x - 1, QUARTER, CH), BF16),
            pltpu.VMEM((2, n_dev * 16, CH), F32),
            pltpu.VMEM((2, n_dev, 16, CH), BF16),
            pltpu.VMEM((2, n_dev - 1, 16, CH), BF16),
            pltpu.VMEM((2, 2, n_x, n_dev, 16, CH), BF16),
            dma((1,)),
            dma((2,)),
            dma((2,)),
            dma((2,)),
            dma((4, 4)),
            dma((4, 4)),
            dma((2, 6)),
            dma((2, 6)),
        ],
        compiler_params=pltpu.CompilerParams(
            collective_id=0, has_side_effects=True, vmem_limit_bytes=48 * 1024 * 1024
        ),
    )(
        morton_pos,
        neighbours,
        rim,
        features,
        cotangent,
        weight_one,
        weight_two,
        jnp.asarray(shift_matrix(), BF16),
    )
    kernels = sums[:, :, :, :TILES].astype(F32).reshape(2, 27 * CH, CH)
    return (output, input_grad, kernels[0], kernels[1])


def solution(mesh):
    placed = (
        P(("tile", "dev"), None, None),
        P(("tile", "dev")),
        P(("tile", "dev"), None),
        P(("tile", "dev")),
        P(("tile", "dev"), None, None),
        P(),
        P(),
    )
    return jax.shard_map(
        functools.partial(per_device, mesh.shape["tile"], mesh.shape["dev"]),
        mesh=mesh,
        in_specs=placed,
        out_specs=(P(("tile", "dev"), None, None), P(("tile", "dev"), None, None), P(), P()),
        check_vma=False,
    )
```

```python
import functools
import math

import jax
import jax.numpy as jnp
import numpy as np
from jax import lax
from jax.experimental import pallas as pl
from jax.experimental.pallas import tpu as pltpu
from jax.sharding import PartitionSpec as P

EDGE = 4
PLANE = EDGE * EDGE
BLK = 8
VOX = 64
CH = 128
RIM = 4
HALF = 27 * CH // 2
QUARTER = HALF // 4
TILES = QUARTER // 16
PIECE = 7 * 16
F32 = jnp.float32
BF16 = jnp.bfloat16
I32 = jnp.int32


def shift_matrix():
    result = np.zeros((9 * PLANE, 9 * PLANE), np.float32)
    for ky in range(3):
        for kz in range(3):
            for j in range(EDGE):
                for k in range(EDGE):
                    y, z = j + ky - 1, k + kz - 1
                    dy, dz = y // EDGE + 1, z // EDGE + 1
                    source = ((dy * 3 + dz) * EDGE + y % EDGE) * EDGE + z % EDGE
                    result[((ky * 3 + kz) * EDGE + j) * EDGE + k, source] = 1.0
    return result


def dot(left, right):
    return jnp.dot(left, right, preferred_element_type=F32)


def unit_kernel(
    n_tile,
    n_dev,
    scale,
    pos_in,
    nbr_in,
    rim_in,
    feat_in,
    cot_in,
    w1_in,
    w2_in,
    smat_in,
    out_output,
    out_grad,
    out_sums,
    pos,
    nbr,
    rim,
    feat,
    cot,
    w1,
    w2,
    smat,
    idxv,
    idxs,
    slotv,
    slots,
    labels,
    packed,
    arrived,
    repacked,
    returned,
    tab_m,
    tab_c,
    tab_h,
    tab_p,
    own,
    rims,
    wt1,
    wt2,
    planes,
    y_m,
    y_c,
    y_x,
    pre_one,
    hidden_grad,
    grads,
    core_in,
    x_out,
    x_in,
    y_out,
    y_in,
    own_sum,
    z_out,
    z_in,
    final,
    sem_in,
    sem_local,
    sem_a2a,
    sem_lab,
    sem_back,
    sem_halo_s,
    sem_halo_r,
    sem_sum_s,
    sem_sum_r,
    sem_first,
):
    tile = lax.axis_index("tile")
    dev = lax.axis_index("dev")
    core = lax.rem(tile, 2)
    chip_x = tile // 2
    n_x = n_tile // 2

    def remote(src, dst, send, recv, **where):
        return pltpu.make_async_remote_copy(
            src_ref=src,
            dst_ref=dst,
            send_sem=send,
            recv_sem=recv,
            device_id=where,
            device_id_type=pl.DeviceIdType.MESH,
        )

    def await_bytes(ref, sem):
        pltpu.make_async_copy(ref, ref, sem).wait()

    operands = (pos_in, rim_in, feat_in, cot_in, w2_in, w1_in, smat_in, nbr_in)
    places = (pos, rim, feat, cot, w2, w1, smat, nbr)
    loads = [
        pltpu.make_async_copy(source, place, sem_in.at[i])
        for i, (source, place) in enumerate(zip(operands, places))
    ]
    load_pos, load_rim, load_feat, load_cot, load_w2, load_w1, load_smat, load_nbr = loads
    for load in loads:
        load.start()
    barrier = pltpu.get_barrier_semaphore()

    @pl.loop(1, n_dev)
    def _(d):
        pl.semaphore_signal(barrier, inc=1, device_id={"dev": lax.rem(dev + d, n_dev)})

    @pl.loop(1, n_tile)
    def _(d):
        pl.semaphore_signal(barrier, inc=1, device_id={"tile": lax.rem(tile + d, n_tile)})

    sub = lax.broadcasted_iota(I32, (8, CH), 0)
    lane = lax.broadcasted_iota(I32, (8, CH), 1)
    load_pos.wait()
    posv = jnp.zeros((8, CH), I32)
    for r in range(BLK):
        posv = jnp.where(sub == r, pos[r], posv)
    owner = posv // BLK
    count = jnp.zeros((8, CH), I32)
    for r in range(BLK):
        count = count + jnp.where((owner == pos[r] // BLK) & (sub > r), 1, 0)
    slot_of_row = lax.rem(owner - dev + n_dev, n_dev) * 2 + count
    hit = lane == slot_of_row
    row_of_slot = jnp.min(jnp.where(hit, sub, BLK - 1), axis=0, keepdims=True)
    label_of_slot = jnp.min(jnp.where(hit, lax.rem(posv, BLK), BLK), axis=0, keepdims=True)
    idxv[0] = jnp.broadcast_to(row_of_slot, (8, CH))
    idxv[1] = jnp.minimum(slot_of_row, 2 * n_dev - 1)
    labels[0] = jnp.broadcast_to(label_of_slot, (8, CH))
    to_scalars = pltpu.make_async_copy(idxv, idxs, sem_local.at[0])
    to_scalars.start()

    def pack_rims(rows, which):
        for h in range(RIM):
            rims[which, h] = rows[rim[h]]

    def halo_copies(which, table):
        result = []
        for q, where in enumerate(
            (
                dict(tile=lax.rem(tile + 1, n_tile)),
                dict(tile=lax.rem(tile + n_tile - 1, n_tile)),
                dict(dev=lax.rem(dev + 1, n_dev)),
                dict(dev=lax.rem(dev + n_dev - 1, n_dev)),
            )
        ):
            result.append(
                remote(
                    rims.at[which],
                    table.at[pl.ds(BLK + q * RIM, RIM)],
                    sem_halo_s.at[which, q],
                    sem_halo_r.at[which, q],
                    **where,
                )
            )
        return result

    def finish_halo(copies, table):
        for copy in copies:
            copy.wait()
        edges = (tile == 0, tile == n_tile - 1, dev == 0, dev == n_dev - 1)
        for q, edge in enumerate(edges):

            @pl.when(edge)
            def _(q=q):
                table[BLK + q * RIM : BLK + (q + 1) * RIM] = jnp.zeros((RIM, VOX, CH), BF16)

    for table in (tab_m, tab_c, tab_h, tab_p):
        table[BLK + 4 * RIM] = jnp.zeros((VOX, CH), BF16)
    load_rim.wait()
    load_cot.wait()
    tab_c[0:BLK] = cot[...]
    pack_rims(cot, 0)
    load_feat.wait()
    to_scalars.wait()

    @pl.loop(0, n_dev)
    def _(d):
        for c in range(2):
            packed[d, c] = feat[idxs[0, 0, 2 * d + c]]

    arrived[0] = packed[0]

    pl.semaphore_wait(barrier, n_dev + n_tile - 2)

    @pl.loop(1, n_dev)
    def _(d):
        where = lax.rem(dev + d, n_dev)
        remote(labels.at[0], labels.at[d], sem_lab.at[0], sem_lab.at[1], dev=where).start()
        remote(packed.at[d], arrived.at[d], sem_a2a.at[0], sem_a2a.at[1], dev=where).start()

    halo_c = halo_copies(0, tab_c)
    for copy in halo_c:
        copy.start()

    def flip_weights(source, target):
        for o in range(27):
            piece = source[o * CH : (o + 1) * CH, :].astype(F32)
            target[(26 - o) * CH : (27 - o) * CH, :] = piece.T.astype(BF16)

    def expand(table, y):
        @pl.loop(0, BLK)
        def _(b):
            for i in range(6):
                dx = 0 if i == 0 else (2 if i == 5 else 1)
                row = (i + EDGE - 1) % EDGE
                for t in range(9):
                    entry = nbr[b, dx * 9 + t]
                    planes[t * PLANE : (t + 1) * PLANE, i * CH : (i + 1) * CH] = table[
                        entry, row * PLANE : (row + 1) * PLANE, :
                    ]
            moved = dot(smat[...], planes[...]).astype(BF16)
            for i in range(6):
                for t in range(9):
                    y[b, i, :, t * CH : (t + 1) * CH] = moved[
                        t * PLANE : (t + 1) * PLANE, i * CH : (i + 1) * CH
                    ]

    def columns(y, kx):
        return y[:, kx : kx + EDGE].reshape(BLK * VOX, 9 * CH)

    def conv(y, w):
        return (
            dot(columns(y, 0), w[0 : 9 * CH, :])
            + dot(columns(y, 1), w[9 * CH : 18 * CH, :])
            + dot(columns(y, 2), w[18 * CH : 27 * CH, :])
        )

    load_w2.wait()
    flip_weights(w2, wt2)
    load_w1.wait()
    flip_weights(w1, wt1)
    load_smat.wait()
    load_nbr.wait()
    finish_halo(halo_c, tab_c)
    expand(tab_c, y_c)
    hidden_grad[...] = conv(y_c, wt2)

    await_bytes(labels.at[pl.ds(1, n_dev - 1)], sem_lab.at[1])
    label_at = jnp.zeros((8, CH), I32)
    for d in range(n_dev):
        label_at = jnp.where(lane // 2 == d, labels[d], label_at)
    label_at = jnp.where(lane < 2 * n_dev, label_at, BLK)
    slotv[0] = jnp.minimum(label_at, BLK - 1)
    slotv[1] = jnp.broadcast_to(
        jnp.max(jnp.where(label_at == sub, lane, 0), axis=1, keepdims=True), (8, CH)
    )
    to_slots = pltpu.make_async_copy(slotv, slots, sem_local.at[0])
    to_slots.start()
    to_slots.wait()
    await_bytes(arrived.at[pl.ds(1, n_dev - 1)], sem_a2a.at[1])
    for s in range(BLK):
        linear = slots[1, s, 0]
        own[0, s] = arrived[linear // 2, lax.rem(linear, 2)]
    tab_m[0:BLK] = own[0]
    pack_rims(own.at[0], 1)
    halo_m = halo_copies(1, tab_m)
    for copy in halo_m:
        copy.start()
    finish_halo(halo_m, tab_m)
    expand(tab_m, y_m)
    pre = conv(y_m, w1)
    gate = jax.nn.sigmoid(pre)
    hidden = (pre * gate).astype(BF16)
    pre_grad = (hidden_grad[...] * gate * (1.0 + pre * (1.0 - gate))).astype(BF16)
    tab_h[0:BLK] = hidden.reshape(BLK, VOX, CH)
    tab_p[0:BLK] = pre_grad.reshape(BLK, VOX, CH)
    own[1] = hidden.reshape(BLK, VOX, CH)
    own[2] = pre_grad.reshape(BLK, VOX, CH)
    pack_rims(own.at[1], 2)
    pack_rims(own.at[2], 3)
    halo_h = halo_copies(2, tab_h)
    halo_p = halo_copies(3, tab_p)
    for copy in halo_h + halo_p:
        copy.start()

    partner = dict(tile=tile + 1 - 2 * core)

    def half_rows(which):
        return pl.ds(pl.multiple_of(which * HALF, 16), HALF)

    def core_copy(q):
        return remote(
            grads.at[q, half_rows(1 - core)],
            core_in.at[q],
            sem_sum_s.at[q, 0],
            sem_sum_r.at[q, 0],
            **partner,
        )

    hidden_t = own[1].reshape(BLK * VOX, CH).astype(F32).T.astype(BF16)
    for kx in range(3):
        part = dot(hidden_t, columns(y_c, kx))
        for t in range(9):
            o = 26 - (kx * 9 + t)
            grads[1, o * CH : (o + 1) * CH, :] = part[:, t * CH : (t + 1) * CH]
    core_copy(1).start()
    pre_grad_t = own[2].reshape(BLK * VOX, CH).astype(F32).T.astype(BF16)
    for kx in range(3):
        part = dot(pre_grad_t, columns(y_m, kx))
        for t in range(9):
            o = kx * 9 + t
            grads[0, o * CH : (o + 1) * CH, :] = part[:, t * CH : (t + 1) * CH].T
    core_copy(0).start()

    y = lax.rem(dev, 4)
    z = dev // 4
    n_z = n_dev // 4

    def peer(dim, e):
        if dim == "x":
            other = lax.rem(chip_x + e, n_x)
            return other, dict(tile=other * 2 + core)
        if dim == "y":
            other = lax.rem(y + e, 4)
            return other, dict(dev=z * 4 + other)
        other = lax.rem(z + e, n_z)
        return other, dict(dev=other * 4 + y)

    dims = (("x", "y"), ("y", "x"))
    place = dict(x=chip_x, y=y)

    def sem(q, stage):
        return sem_sum_s.at[q, stage], sem_sum_r.at[q, stage]

    def both_cores(q, chunk):
        start = pl.multiple_of(core * HALF + chunk * QUARTER, 16)
        start_in = pl.multiple_of(chunk * QUARTER, 16)
        return grads[q, pl.ds(start, QUARTER), :] + core_in[q, pl.ds(start_in, QUARTER), :]

    def start_first(q):
        core_copy(q).wait_recv()
        for j in range(4):
            x_out[q, j] = both_cores(q, j).astype(BF16)
        for e in (2, 1, 3):
            other, where = peer(dims[q][0], e)
            remote(x_out.at[q, other], x_in.at[q, e - 1], *sem(q, 1), **where).start()

    def start_second(q):
        await_bytes(x_in.at[q], sem_sum_r.at[q, 1])
        total = both_cores(q, place[dims[q][0]])
        for e in range(3):
            total = total + x_in[q, e].astype(F32)
        own_sum[q, 0:QUARTER] = total
        own_sum[q, QUARTER:] = jnp.zeros((4 * PIECE - QUARTER, CH), F32)
        for j in range(4):
            y_out[q, j] = own_sum[q, j * PIECE : (j + 1) * PIECE].astype(BF16)
        for e in (2, 1, 3):
            other, where = peer(dims[q][1], e)
            remote(y_out.at[q, other], y_in.at[q, e - 1], *sem(q, 2), **where).start()

    def start_third(q):
        await_bytes(y_in.at[q], sem_sum_r.at[q, 2])
        start = pl.multiple_of(place[dims[q][1]] * PIECE, 16)
        total = own_sum[q, pl.ds(start, PIECE), :]
        for e in range(3):
            total = total + y_in[q, e].astype(F32)
        z_out[q, 0:7] = total.reshape(7, 16, CH)
        z_out[q, 7] = jnp.zeros((16, CH), F32)
        for e in (4, 3, 5, 2, 6, 1, 7):
            other, where = peer("z", e)
            remote(z_out.at[q, other], z_in.at[q, e - 1], *sem(q, 3), **where).start()

    def start_gather_third(q):
        await_bytes(z_in.at[q], sem_sum_r.at[q, 3])
        total = z_out[q, z]
        for e in range(7):
            total = total + z_in[q, e]
        mine = final.at[q, core, place[dims[q][0]], place[dims[q][1]], z]
        mine[...] = (total * scale).astype(BF16)
        for e in (4, 3, 5, 2, 6, 1, 7):
            _, where = peer("z", e)
            remote(mine, mine, *sem(q, 4), **where).start()

    def start_gather_second(q):
        await_bytes(final.at[q, core, 0, 0, pl.ds(0, 7)], sem_sum_r.at[q, 4])
        mine = final.at[q, core, place[dims[q][0]], place[dims[q][1]], pl.ds(0, 7)]
        for e in (2, 1, 3):
            _, where = peer(dims[q][1], e)
            remote(mine, mine, *sem(q, 5), **where).start()

    def gather_core_copy(q, chunk):
        piece = final.at[q, core, chunk, :, pl.ds(0, 7)]
        return remote(piece, piece, *sem(q, 7), **partner)

    def gather_first_copy(q, e):
        mine = final.at[q, core, place[dims[q][0]], :, pl.ds(0, 7)]
        _, where = peer(dims[q][0], e)
        return remote(mine, mine, sem_sum_s.at[q, 6], sem_first.at[q, e - 1], **where)

    def start_gather_first(q):
        await_bytes(final.at[q, core, 0, pl.ds(0, 3), pl.ds(0, 7)], sem_sum_r.at[q, 5])
        for e in (2, 1, 3):
            gather_first_copy(q, e).start()
        gather_core_copy(q, place[dims[q][0]]).start()

    def start_gather_core(q):
        for e in (1, 3, 2):
            gather_first_copy(q, e).wait_recv()
            gather_core_copy(q, lax.rem(place[dims[q][0]] + 4 - e, 4)).start()

    start_first(1)
    start_first(0)
    finish_halo(halo_h, tab_h)
    expand(tab_h, y_x)
    pre_two = conv(y_x, w2)
    out_output[...] = (
        (own[0].reshape(BLK * VOX, CH).astype(F32) + pre_two).astype(BF16).reshape(BLK, VOX, CH)
    )
    finish_halo(halo_p, tab_p)
    expand(tab_p, y_x)
    back = conv(y_x, wt1) + cot[...].reshape(BLK * VOX, CH).astype(F32)
    own[1] = back.astype(BF16).reshape(BLK, VOX, CH)

    @pl.loop(0, n_dev)
    def _(d):
        for c in range(2):
            repacked[d, c] = own[1, slots[0, 0, 2 * d + c]]

    returned[0] = repacked[0]

    @pl.loop(1, n_dev)
    def _(d):
        where = lax.rem(dev - d + n_dev, n_dev)
        remote(repacked.at[d], returned.at[d], sem_back.at[0], sem_back.at[1], dev=where).start()

    for stage in (
        start_second,
        start_third,
        start_gather_third,
        start_gather_second,
        start_gather_first,
        start_gather_core,
    ):
        stage(1)
        stage(0)
    await_bytes(returned.at[pl.ds(1, n_dev - 1)], sem_back.at[1])
    for r in range(BLK):
        linear = idxs[1, r, 0]
        out_grad[r] = returned[linear // 2, lax.rem(linear, 2)]

    await_bytes(labels.at[pl.ds(1, n_dev - 1)], sem_lab.at[0])
    await_bytes(packed.at[pl.ds(1, n_dev - 1)], sem_a2a.at[0])
    await_bytes(repacked.at[pl.ds(1, n_dev - 1)], sem_back.at[0])
    for q in range(2):
        await_bytes(final.at[q, 1 - core, :, :, pl.ds(0, 7)], sem_sum_r.at[q, 7])
        for c in range(2):
            for j in range(4):
                out_sums[q, c, j] = final[q, c, j, :, 0:7].reshape(28, 16, CH)[0:TILES]
    for q in range(2):
        core_copy(q).wait_send()
        await_bytes(x_in.at[q], sem_sum_s.at[q, 1])
        await_bytes(y_in.at[q], sem_sum_s.at[q, 2])
        await_bytes(z_in.at[q], sem_sum_s.at[q, 3])
        await_bytes(final.at[q, core, 0, 0, pl.ds(0, 7)], sem_sum_s.at[q, 4])
        await_bytes(final.at[q, core, 0, pl.ds(0, 3), pl.ds(0, 7)], sem_sum_s.at[q, 5])
        await_bytes(final.at[q, core, pl.ds(0, 3), :, pl.ds(0, 7)], sem_sum_s.at[q, 6])
        await_bytes(final.at[q, core, :, :, pl.ds(0, 7)], sem_sum_s.at[q, 7])


def per_device(
    n_tile, n_dev, features, morton_pos, neighbours, rim, cotangent, weight_one, weight_two
):
    blocks, voxels, channels = features.shape
    scale = 1.0 / math.sqrt(blocks * voxels * n_tile * n_dev)
    n_x = n_tile // 2
    hbm = pl.BlockSpec(memory_space=pltpu.HBM)
    vmem = pl.BlockSpec(memory_space=pltpu.VMEM)
    dma = pltpu.SemaphoreType.DMA
    block_table = pltpu.VMEM((BLK + 4 * RIM + 1, VOX, CH), BF16)
    wide = pltpu.VMEM((BLK, 6, PLANE, 9 * CH), BF16)
    flat = pltpu.VMEM((BLK * VOX, CH), F32)
    slab = pltpu.VMEM((n_dev, 2, VOX, CH), BF16)
    output, input_grad, sums = pl.pallas_call(
        functools.partial(unit_kernel, n_tile, n_dev, scale),
        out_shape=(
            jax.ShapeDtypeStruct(features.shape, BF16),
            jax.ShapeDtypeStruct(features.shape, BF16),
            jax.ShapeDtypeStruct((2, 2, 4, TILES, 16, CH), BF16),
        ),
        in_specs=[hbm] * 8,
        out_specs=(vmem, vmem, vmem),
        scratch_shapes=[
            pltpu.SMEM(morton_pos.shape, I32),
            pltpu.SMEM(neighbours.shape, I32),
            pltpu.SMEM(rim.shape, I32),
            pltpu.VMEM(features.shape, BF16),
            pltpu.VMEM(cotangent.shape, BF16),
            pltpu.VMEM(weight_one.shape, BF16),
            pltpu.VMEM(weight_two.shape, BF16),
            pltpu.VMEM((9 * PLANE, 9 * PLANE), BF16),
            pltpu.VMEM((2, 8, CH), I32),
            pltpu.SMEM((2, 8, CH), I32),
            pltpu.VMEM((2, 8, CH), I32),
            pltpu.SMEM((2, 8, CH), I32),
            pltpu.VMEM((n_dev, 8, CH), I32),
            slab,
            slab,
            slab,
            slab,
            block_table,
            block_table,
            block_table,
            block_table,
            pltpu.VMEM((3, BLK, VOX, CH), BF16),
            pltpu.VMEM((4, RIM, VOX, CH), BF16),
            pltpu.VMEM((27 * CH, CH), BF16),
            pltpu.VMEM((27 * CH, CH), BF16),
            pltpu.VMEM((9 * PLANE, 6 * CH), BF16),
            wide,
            wide,
            wide,
            flat,
            flat,
            pltpu.VMEM((2, 27 * CH, CH), F32),
            pltpu.VMEM((2, HALF, CH), F32),
            pltpu.VMEM((2, 4, QUARTER, CH), BF16),
            pltpu.VMEM((2, 3, QUARTER, CH), BF16),
            pltpu.VMEM((2, 4, PIECE, CH), BF16),
            pltpu.VMEM((2, 3, PIECE, CH), BF16),
            pltpu.VMEM((2, 4 * PIECE, CH), F32),
            pltpu.VMEM((2, 8, 16, CH), F32),
            pltpu.VMEM((2, 7, 16, CH), F32),
            pltpu.VMEM((2, 2, 4, 4, 8, 16, CH), BF16),
            dma((8,)),
            dma((1,)),
            dma((2,)),
            dma((2,)),
            dma((2,)),
            dma((4, 4)),
            dma((4, 4)),
            dma((2, 8)),
            dma((2, 8)),
            dma((2, 3)),
        ],
        compiler_params=pltpu.CompilerParams(
            collective_id=0, has_side_effects=True, vmem_limit_bytes=62 * 1024 * 1024
        ),
    )(
        morton_pos,
        neighbours,
        rim,
        features,
        cotangent,
        weight_one,
        weight_two,
        jnp.asarray(shift_matrix(), BF16),
    )
    kernels = sums.astype(F32).reshape(2, 27 * CH, CH)
    return (output, input_grad, kernels[0], kernels[1])


def solution(mesh):
    placed = (
        P(("tile", "dev"), None, None),
        P(("tile", "dev")),
        P(("tile", "dev"), None),
        P(("tile", "dev")),
        P(("tile", "dev"), None, None),
        P(),
        P(),
    )
    return jax.shard_map(
        functools.partial(per_device, mesh.shape["tile"], mesh.shape["dev"]),
        mesh=mesh,
        in_specs=placed,
        out_specs=(P(("tile", "dev"), None, None), P(("tile", "dev"), None, None), P(), P()),
        check_vma=False,
    )
```

```python
import functools
import math

import jax
import jax.numpy as jnp
import numpy as np
from jax import lax
from jax.experimental import pallas as pl
from jax.experimental.pallas import tpu as pltpu
from jax.sharding import PartitionSpec as P

EDGE = 4
PLANE = EDGE * EDGE
BLK = 8
VOX = 64
CH = 128
RIM = 4
HALF = 27 * CH // 2
QUARTER = HALF // 4
TILES = QUARTER // 16
PIECE = 7 * 16
F32 = jnp.float32
BF16 = jnp.bfloat16
I32 = jnp.int32


def shift_matrix():
    result = np.zeros((9 * PLANE, 9 * PLANE), np.float32)
    for ky in range(3):
        for kz in range(3):
            for j in range(EDGE):
                for k in range(EDGE):
                    y, z = j + ky - 1, k + kz - 1
                    dy, dz = y // EDGE + 1, z // EDGE + 1
                    source = ((dy * 3 + dz) * EDGE + y % EDGE) * EDGE + z % EDGE
                    result[((ky * 3 + kz) * EDGE + j) * EDGE + k, source] = 1.0
    return result


def dot(left, right):
    return jnp.dot(left, right, preferred_element_type=F32)


def unit_kernel(
    n_tile,
    n_dev,
    scale,
    pos_in,
    nbr_in,
    rim_in,
    feat_in,
    cot_in,
    w1_in,
    w2_in,
    smat_in,
    out_output,
    out_grad,
    out_sums,
    pos,
    nbr,
    rim,
    feat,
    cot,
    w1,
    w2,
    smat,
    idxv,
    idxs,
    slotv,
    slots,
    labels,
    packed,
    arrived,
    repacked,
    returned,
    tab_m,
    tab_c,
    tab_h,
    tab_p,
    own,
    rims,
    wt1,
    wt2,
    planes,
    y_m,
    y_c,
    y_x,
    pre_one,
    hidden_grad,
    grads,
    core_in,
    x_out,
    x_in,
    y_out,
    y_in,
    own_sum,
    z_out,
    z_in,
    final,
    sem_in,
    sem_local,
    sem_a2a,
    sem_lab,
    sem_back,
    sem_halo_s,
    sem_halo_r,
    sem_sum_s,
    sem_sum_r,
    sem_first,
):
    tile = lax.axis_index("tile")
    dev = lax.axis_index("dev")
    core = lax.rem(tile, 2)
    chip_x = tile // 2
    n_x = n_tile // 2

    def remote(src, dst, send, recv, **where):
        return pltpu.make_async_remote_copy(
            src_ref=src,
            dst_ref=dst,
            send_sem=send,
            recv_sem=recv,
            device_id=where,
            device_id_type=pl.DeviceIdType.MESH,
        )

    def await_bytes(ref, sem):
        pltpu.make_async_copy(ref, ref, sem).wait()

    operands = (pos_in, rim_in, feat_in, cot_in, w2_in, w1_in, smat_in, nbr_in)
    places = (pos, rim, feat, cot, w2, w1, smat, nbr)
    loads = [
        pltpu.make_async_copy(source, place, sem_in.at[i])
        for i, (source, place) in enumerate(zip(operands, places))
    ]
    load_pos, load_rim, load_feat, load_cot, load_w2, load_w1, load_smat, load_nbr = loads
    for load in loads:
        load.start()
    barrier = pltpu.get_barrier_semaphore()

    @pl.loop(1, n_dev)
    def _(d):
        pl.semaphore_signal(barrier, inc=1, device_id={"dev": lax.rem(dev + d, n_dev)})

    @pl.loop(1, n_tile)
    def _(d):
        pl.semaphore_signal(barrier, inc=1, device_id={"tile": lax.rem(tile + d, n_tile)})

    sub = lax.broadcasted_iota(I32, (8, CH), 0)
    lane = lax.broadcasted_iota(I32, (8, CH), 1)
    load_pos.wait()
    posv = jnp.zeros((8, CH), I32)
    for r in range(BLK):
        posv = jnp.where(sub == r, pos[r], posv)
    owner = posv // BLK
    count = jnp.zeros((8, CH), I32)
    for r in range(BLK):
        count = count + jnp.where((owner == pos[r] // BLK) & (sub > r), 1, 0)
    slot_of_row = lax.rem(owner - dev + n_dev, n_dev) * 2 + count
    hit = lane == slot_of_row
    row_of_slot = jnp.min(jnp.where(hit, sub, BLK - 1), axis=0, keepdims=True)
    label_of_slot = jnp.min(jnp.where(hit, lax.rem(posv, BLK), BLK), axis=0, keepdims=True)
    idxv[0] = jnp.broadcast_to(row_of_slot, (8, CH))
    idxv[1] = jnp.minimum(slot_of_row, 2 * n_dev - 1)
    labels[0] = label_of_slot
    to_scalars = pltpu.make_async_copy(idxv, idxs, sem_local.at[0])
    to_scalars.start()

    def pack_rims(rows, which):
        for h in range(RIM):
            rims[which, h] = rows[rim[h]]

    def halo_copies(which, table):
        result = []
        for q, where in enumerate(
            (
                dict(tile=lax.rem(tile + 1, n_tile)),
                dict(tile=lax.rem(tile + n_tile - 1, n_tile)),
                dict(dev=lax.rem(dev + 1, n_dev)),
                dict(dev=lax.rem(dev + n_dev - 1, n_dev)),
            )
        ):
            result.append(
                remote(
                    rims.at[which],
                    table.at[pl.ds(BLK + q * RIM, RIM)],
                    sem_halo_s.at[which, q],
                    sem_halo_r.at[which, q],
                    **where,
                )
            )
        return result

    def finish_halo(copies, table):
        for copy in copies:
            copy.wait()
        edges = (tile == 0, tile == n_tile - 1, dev == 0, dev == n_dev - 1)
        for q, edge in enumerate(edges):

            @pl.when(edge)
            def _(q=q):
                table[BLK + q * RIM : BLK + (q + 1) * RIM] = jnp.zeros((RIM, VOX, CH), BF16)

    for table in (tab_m, tab_c, tab_h, tab_p):
        table[BLK + 4 * RIM] = jnp.zeros((VOX, CH), BF16)
    load_rim.wait()
    load_cot.wait()
    tab_c[0:BLK] = cot[...]
    pack_rims(cot, 0)
    load_feat.wait()
    to_scalars.wait()

    @pl.loop(0, n_dev)
    def _(d):
        for c in range(2):
            packed[d, c] = feat[idxs[0, 0, 2 * d + c]]

    arrived[0] = packed[0]

    pl.semaphore_wait(barrier, n_dev + n_tile - 2)

    @pl.loop(1, n_dev)
    def _(d):
        where = lax.rem(dev + d, n_dev)
        remote(labels.at[0], labels.at[d], sem_lab.at[0], sem_lab.at[1], dev=where).start()
        remote(packed.at[d], arrived.at[d], sem_a2a.at[0], sem_a2a.at[1], dev=where).start()

    halo_c = halo_copies(0, tab_c)
    for copy in halo_c:
        copy.start()

    def flip_weights(source, target):
        for o in range(27):
            piece = source[o * CH : (o + 1) * CH, :].astype(F32)
            target[(26 - o) * CH : (27 - o) * CH, :] = piece.T.astype(BF16)

    def expand(table, y):
        @pl.loop(0, BLK)
        def _(b):
            for i in range(6):
                dx = 0 if i == 0 else (2 if i == 5 else 1)
                row = (i + EDGE - 1) % EDGE
                for t in range(9):
                    entry = nbr[b, dx * 9 + t]
                    planes[t * PLANE : (t + 1) * PLANE, i * CH : (i + 1) * CH] = table[
                        entry, row * PLANE : (row + 1) * PLANE, :
                    ]
            moved = dot(smat[...], planes[...]).astype(BF16)
            for i in range(6):
                for t in range(9):
                    y[b, i, :, t * CH : (t + 1) * CH] = moved[
                        t * PLANE : (t + 1) * PLANE, i * CH : (i + 1) * CH
                    ]

    def columns(y, kx):
        return y[:, kx : kx + EDGE].reshape(BLK * VOX, 9 * CH)

    def conv(y, w):
        return (
            dot(columns(y, 0), w[0 : 9 * CH, :])
            + dot(columns(y, 1), w[9 * CH : 18 * CH, :])
            + dot(columns(y, 2), w[18 * CH : 27 * CH, :])
        )

    load_w2.wait()
    flip_weights(w2, wt2)
    load_w1.wait()
    flip_weights(w1, wt1)
    load_smat.wait()
    load_nbr.wait()
    finish_halo(halo_c, tab_c)
    expand(tab_c, y_c)
    hidden_grad[...] = conv(y_c, wt2)

    await_bytes(labels.at[pl.ds(1, n_dev - 1)], sem_lab.at[1])
    label_at = jnp.zeros((8, CH), I32)
    for d in range(n_dev):
        label_at = jnp.where(lane // 2 == d, labels[d], label_at)
    label_at = jnp.where(lane < 2 * n_dev, label_at, BLK)
    slotv[0] = jnp.minimum(label_at, BLK - 1)
    slotv[1] = jnp.broadcast_to(
        jnp.max(jnp.where(label_at == sub, lane, 0), axis=1, keepdims=True), (8, CH)
    )
    to_slots = pltpu.make_async_copy(slotv, slots, sem_local.at[0])
    to_slots.start()
    to_slots.wait()
    await_bytes(arrived.at[pl.ds(1, n_dev - 1)], sem_a2a.at[1])
    for s in range(BLK):
        linear = slots[1, s, 0]
        own[0, s] = arrived[linear // 2, lax.rem(linear, 2)]
    tab_m[0:BLK] = own[0]
    pack_rims(own.at[0], 1)
    halo_m = halo_copies(1, tab_m)
    for copy in halo_m:
        copy.start()
    finish_halo(halo_m, tab_m)
    expand(tab_m, y_m)
    pre = conv(y_m, w1)
    gate = jax.nn.sigmoid(pre)
    hidden = (pre * gate).astype(BF16)
    pre_grad = (hidden_grad[...] * gate * (1.0 + pre * (1.0 - gate))).astype(BF16)
    tab_h[0:BLK] = hidden.reshape(BLK, VOX, CH)
    tab_p[0:BLK] = pre_grad.reshape(BLK, VOX, CH)
    own[1] = hidden.reshape(BLK, VOX, CH)
    own[2] = pre_grad.reshape(BLK, VOX, CH)
    pack_rims(own.at[1], 2)
    pack_rims(own.at[2], 3)
    halo_h = halo_copies(2, tab_h)
    halo_p = halo_copies(3, tab_p)
    for copy in halo_h + halo_p:
        copy.start()

    partner = dict(tile=tile + 1 - 2 * core)

    def half_rows(which):
        return pl.ds(pl.multiple_of(which * HALF, 16), HALF)

    def core_copy(q):
        return remote(
            grads.at[q, half_rows(1 - core)],
            core_in.at[q],
            sem_sum_s.at[q, 0],
            sem_sum_r.at[q, 0],
            **partner,
        )

    hidden_t = own[1].reshape(BLK * VOX, CH).astype(F32).T.astype(BF16)
    for kx in range(3):
        part = dot(hidden_t, columns(y_c, kx))
        for t in range(9):
            o = 26 - (kx * 9 + t)
            grads[1, o * CH : (o + 1) * CH, :] = part[:, t * CH : (t + 1) * CH]
    core_copy(1).start()
    pre_grad_t = own[2].reshape(BLK * VOX, CH).astype(F32).T.astype(BF16)
    for kx in range(3):
        part = dot(pre_grad_t, columns(y_m, kx))
        for t in range(9):
            o = kx * 9 + t
            grads[0, o * CH : (o + 1) * CH, :] = part[:, t * CH : (t + 1) * CH].T
    core_copy(0).start()

    y = lax.rem(dev, 4)
    z = dev // 4
    n_z = n_dev // 4

    def peer(dim, e):
        if dim == "x":
            other = lax.rem(chip_x + e, n_x)
            return other, dict(tile=other * 2 + core)
        if dim == "y":
            other = lax.rem(y + e, 4)
            return other, dict(dev=z * 4 + other)
        other = lax.rem(z + e, n_z)
        return other, dict(dev=other * 4 + y)

    dims = (("x", "y"), ("y", "x"))
    place = dict(x=chip_x, y=y)

    def sem(q, stage):
        return sem_sum_s.at[q, stage], sem_sum_r.at[q, stage]

    def both_cores(q, chunk):
        start = pl.multiple_of(core * HALF + chunk * QUARTER, 16)
        start_in = pl.multiple_of(chunk * QUARTER, 16)
        return grads[q, pl.ds(start, QUARTER), :] + core_in[q, pl.ds(start_in, QUARTER), :]

    def start_first(q):
        core_copy(q).wait_recv()
        for j in range(4):
            x_out[q, j] = both_cores(q, j).astype(BF16)
        for e in (2, 1, 3):
            other, where = peer(dims[q][0], e)
            remote(x_out.at[q, other], x_in.at[q, e - 1], *sem(q, 1), **where).start()

    def start_second(q):
        await_bytes(x_in.at[q], sem_sum_r.at[q, 1])
        total = both_cores(q, place[dims[q][0]])
        for e in range(3):
            total = total + x_in[q, e].astype(F32)
        own_sum[q, 0:QUARTER] = total
        own_sum[q, QUARTER:] = jnp.zeros((4 * PIECE - QUARTER, CH), F32)
        for j in range(4):
            y_out[q, j] = own_sum[q, j * PIECE : (j + 1) * PIECE].astype(BF16)
        for e in (2, 1, 3):
            other, where = peer(dims[q][1], e)
            remote(y_out.at[q, other], y_in.at[q, e - 1], *sem(q, 2), **where).start()

    def start_third(q):
        await_bytes(y_in.at[q], sem_sum_r.at[q, 2])
        start = pl.multiple_of(place[dims[q][1]] * PIECE, 16)
        total = own_sum[q, pl.ds(start, PIECE), :]
        for e in range(3):
            total = total + y_in[q, e].astype(F32)
        z_out[q, 0:7] = total.reshape(7, 16, CH)
        z_out[q, 7] = jnp.zeros((16, CH), F32)
        for e in (4, 3, 5, 2, 6, 1, 7):
            other, where = peer("z", e)
            remote(z_out.at[q, other], z_in.at[q, e - 1], *sem(q, 3), **where).start()

    def start_gather_third(q):
        await_bytes(z_in.at[q], sem_sum_r.at[q, 3])
        total = z_out[q, z]
        for e in range(7):
            total = total + z_in[q, e]
        mine = final.at[q, core, place[dims[q][0]], place[dims[q][1]], z]
        mine[...] = (total * scale).astype(BF16)
        for e in (4, 3, 5, 2, 6, 1, 7):
            _, where = peer("z", e)
            remote(mine, mine, *sem(q, 4), **where).start()

    def start_gather_second(q):
        await_bytes(final.at[q, core, 0, 0, pl.ds(0, 7)], sem_sum_r.at[q, 4])
        mine = final.at[q, core, place[dims[q][0]], place[dims[q][1]], pl.ds(0, 7)]
        for e in (2, 1, 3):
            _, where = peer(dims[q][1], e)
            remote(mine, mine, *sem(q, 5), **where).start()

    def gather_core_copy(q, chunk):
        piece = final.at[q, core, chunk, :, pl.ds(0, 7)]
        return remote(piece, piece, *sem(q, 7), **partner)

    def gather_first_copy(q, e):
        mine = final.at[q, core, place[dims[q][0]], :, pl.ds(0, 7)]
        _, where = peer(dims[q][0], e)
        return remote(mine, mine, sem_sum_s.at[q, 6], sem_first.at[q, e - 1], **where)

    def start_gather_first(q):
        await_bytes(final.at[q, core, 0, pl.ds(0, 3), pl.ds(0, 7)], sem_sum_r.at[q, 5])
        for e in (2, 1, 3):
            gather_first_copy(q, e).start()
        gather_core_copy(q, place[dims[q][0]]).start()

    def start_gather_core(q):
        for e in (1, 3, 2):
            gather_first_copy(q, e).wait_recv()
            gather_core_copy(q, lax.rem(place[dims[q][0]] + 4 - e, 4)).start()

    start_first(1)
    start_first(0)
    finish_halo(halo_h, tab_h)
    expand(tab_h, y_x)
    pre_two = conv(y_x, w2)
    out_output[...] = (
        (own[0].reshape(BLK * VOX, CH).astype(F32) + pre_two).astype(BF16).reshape(BLK, VOX, CH)
    )
    finish_halo(halo_p, tab_p)
    expand(tab_p, y_x)
    back = conv(y_x, wt1) + cot[...].reshape(BLK * VOX, CH).astype(F32)
    own[1] = back.astype(BF16).reshape(BLK, VOX, CH)

    @pl.loop(0, n_dev)
    def _(d):
        for c in range(2):
            repacked[d, c] = own[1, slots[0, 0, 2 * d + c]]

    returned[0] = repacked[0]

    order = [7 * i % n_dev for i in range(1, n_dev)]

    def send_back(offsets):
        for d in offsets:
            where = lax.rem(dev - d + n_dev, n_dev)
            remote(repacked.at[d], returned.at[d], sem_back.at[0], sem_back.at[1], dev=where).start()

    for stage, offsets in (
        (start_second, order[0:6]),
        (start_third, order[6:12]),
        (start_gather_third, order[12:18]),
        (start_gather_second, order[18:24]),
        (start_gather_first, order[24:]),
        (start_gather_core, []),
    ):
        stage(1)
        stage(0)
        send_back(offsets)
    await_bytes(returned.at[pl.ds(1, n_dev - 1)], sem_back.at[1])
    for r in range(BLK):
        linear = idxs[1, r, 0]
        out_grad[r] = returned[linear // 2, lax.rem(linear, 2)]

    await_bytes(labels.at[pl.ds(1, n_dev - 1)], sem_lab.at[0])
    await_bytes(packed.at[pl.ds(1, n_dev - 1)], sem_a2a.at[0])
    await_bytes(repacked.at[pl.ds(1, n_dev - 1)], sem_back.at[0])
    for q in range(2):
        await_bytes(final.at[q, 1 - core, :, :, pl.ds(0, 7)], sem_sum_r.at[q, 7])
        for c in range(2):
            for j in range(4):
                out_sums[q, c, j] = final[q, c, j, :, 0:7].reshape(28, 16, CH)[0:TILES]
    for q in range(2):
        core_copy(q).wait_send()
        await_bytes(x_in.at[q], sem_sum_s.at[q, 1])
        await_bytes(y_in.at[q], sem_sum_s.at[q, 2])
        await_bytes(z_in.at[q], sem_sum_s.at[q, 3])
        await_bytes(final.at[q, core, 0, 0, pl.ds(0, 7)], sem_sum_s.at[q, 4])
        await_bytes(final.at[q, core, 0, pl.ds(0, 3), pl.ds(0, 7)], sem_sum_s.at[q, 5])
        await_bytes(final.at[q, core, pl.ds(0, 3), :, pl.ds(0, 7)], sem_sum_s.at[q, 6])
        await_bytes(final.at[q, core, :, :, pl.ds(0, 7)], sem_sum_s.at[q, 7])


def per_device(
    n_tile, n_dev, features, morton_pos, neighbours, rim, cotangent, weight_one, weight_two
):
    blocks, voxels, channels = features.shape
    scale = 1.0 / math.sqrt(blocks * voxels * n_tile * n_dev)
    n_x = n_tile // 2
    hbm = pl.BlockSpec(memory_space=pltpu.HBM)
    vmem = pl.BlockSpec(memory_space=pltpu.VMEM)
    dma = pltpu.SemaphoreType.DMA
    block_table = pltpu.VMEM((BLK + 4 * RIM + 1, VOX, CH), BF16)
    wide = pltpu.VMEM((BLK, 6, PLANE, 9 * CH), BF16)
    flat = pltpu.VMEM((BLK * VOX, CH), F32)
    slab = pltpu.VMEM((n_dev, 2, VOX, CH), BF16)
    output, input_grad, sums = pl.pallas_call(
        functools.partial(unit_kernel, n_tile, n_dev, scale),
        out_shape=(
            jax.ShapeDtypeStruct(features.shape, BF16),
            jax.ShapeDtypeStruct(features.shape, BF16),
            jax.ShapeDtypeStruct((2, 2, 4, TILES, 16, CH), BF16),
        ),
        in_specs=[hbm] * 8,
        out_specs=(vmem, vmem, vmem),
        scratch_shapes=[
            pltpu.SMEM(morton_pos.shape, I32),
            pltpu.SMEM(neighbours.shape, I32),
            pltpu.SMEM(rim.shape, I32),
            pltpu.VMEM(features.shape, BF16),
            pltpu.VMEM(cotangent.shape, BF16),
            pltpu.VMEM(weight_one.shape, BF16),
            pltpu.VMEM(weight_two.shape, BF16),
            pltpu.VMEM((9 * PLANE, 9 * PLANE), BF16),
            pltpu.VMEM((2, 8, CH), I32),
            pltpu.SMEM((2, 8, CH), I32),
            pltpu.VMEM((2, 8, CH), I32),
            pltpu.SMEM((2, 8, CH), I32),
            pltpu.VMEM((n_dev, 1, CH), I32),
            slab,
            slab,
            slab,
            slab,
            block_table,
            block_table,
            block_table,
            block_table,
            pltpu.VMEM((3, BLK, VOX, CH), BF16),
            pltpu.VMEM((4, RIM, VOX, CH), BF16),
            pltpu.VMEM((27 * CH, CH), BF16),
            pltpu.VMEM((27 * CH, CH), BF16),
            pltpu.VMEM((9 * PLANE, 6 * CH), BF16),
            wide,
            wide,
            wide,
            flat,
            flat,
            pltpu.VMEM((2, 27 * CH, CH), F32),
            pltpu.VMEM((2, HALF, CH), F32),
            pltpu.VMEM((2, 4, QUARTER, CH), BF16),
            pltpu.VMEM((2, 3, QUARTER, CH), BF16),
            pltpu.VMEM((2, 4, PIECE, CH), BF16),
            pltpu.VMEM((2, 3, PIECE, CH), BF16),
            pltpu.VMEM((2, 4 * PIECE, CH), F32),
            pltpu.VMEM((2, 8, 16, CH), F32),
            pltpu.VMEM((2, 7, 16, CH), F32),
            pltpu.VMEM((2, 2, 4, 4, 8, 16, CH), BF16),
            dma((8,)),
            dma((1,)),
            dma((2,)),
            dma((2,)),
            dma((2,)),
            dma((4, 4)),
            dma((4, 4)),
            dma((2, 8)),
            dma((2, 8)),
            dma((2, 3)),
        ],
        compiler_params=pltpu.CompilerParams(
            collective_id=0, has_side_effects=True, vmem_limit_bytes=62 * 1024 * 1024
        ),
    )(
        morton_pos,
        neighbours,
        rim,
        features,
        cotangent,
        weight_one,
        weight_two,
        jnp.asarray(shift_matrix(), BF16),
    )
    kernels = sums.astype(F32).reshape(2, 27 * CH, CH)
    return (output, input_grad, kernels[0], kernels[1])


def solution(mesh):
    placed = (
        P(("tile", "dev"), None, None),
        P(("tile", "dev")),
        P(("tile", "dev"), None),
        P(("tile", "dev")),
        P(("tile", "dev"), None, None),
        P(),
        P(),
    )
    return jax.shard_map(
        functools.partial(per_device, mesh.shape["tile"], mesh.shape["dev"]),
        mesh=mesh,
        in_specs=placed,
        out_specs=(P(("tile", "dev"), None, None), P(("tile", "dev"), None, None), P(), P()),
        check_vma=False,
    )
```

```python
import functools
import math

import jax
import jax.numpy as jnp
import numpy as np
from jax import lax
from jax.experimental import pallas as pl
from jax.experimental.pallas import tpu as pltpu
from jax.sharding import PartitionSpec as P

EDGE = 4
PLANE = EDGE * EDGE
BLK = 8
VOX = 64
CH = 128
RIM = 4
HALF = 27 * CH // 2
QUARTER = HALF // 4
TILES = QUARTER // 16
PIECE = 7 * 16
F32 = jnp.float32
BF16 = jnp.bfloat16
I32 = jnp.int32


def shift_matrix():
    result = np.zeros((9 * PLANE, 9 * PLANE), np.float32)
    for ky in range(3):
        for kz in range(3):
            for j in range(EDGE):
                for k in range(EDGE):
                    y, z = j + ky - 1, k + kz - 1
                    dy, dz = y // EDGE + 1, z // EDGE + 1
                    source = ((dy * 3 + dz) * EDGE + y % EDGE) * EDGE + z % EDGE
                    result[((ky * 3 + kz) * EDGE + j) * EDGE + k, source] = 1.0
    return result


def dot(left, right):
    return jnp.dot(left, right, preferred_element_type=F32)


def unit_kernel(
    n_tile,
    n_dev,
    scale,
    pos_in,
    nbr_in,
    rim_in,
    feat_in,
    cot_in,
    w1_in,
    w2_in,
    smat_in,
    out_output,
    out_grad,
    out_sums,
    pos,
    nbr,
    rim,
    feat,
    cot,
    w1,
    w2,
    smat,
    idxv,
    idxs,
    slotv,
    slots,
    labels,
    packed,
    arrived,
    repacked,
    returned,
    tab_m,
    tab_c,
    tab_h,
    tab_p,
    own,
    leaving,
    rims,
    wt1,
    wt2,
    planes,
    y_m,
    y_c,
    y_x,
    pre_one,
    hidden_grad,
    grads,
    core_in,
    x_out,
    x_in,
    y_out,
    y_in,
    own_sum,
    z_out,
    z_in,
    final,
    sem_in,
    sem_local,
    sem_a2a,
    sem_lab,
    sem_back,
    sem_halo_s,
    sem_halo_r,
    sem_sum_s,
    sem_sum_r,
    sem_first,
    sem_core,
    sem_out,
):
    tile = lax.axis_index("tile")
    dev = lax.axis_index("dev")
    core = lax.rem(tile, 2)
    chip_x = tile // 2
    n_x = n_tile // 2

    def remote(src, dst, send, recv, **where):
        return pltpu.make_async_remote_copy(
            src_ref=src,
            dst_ref=dst,
            send_sem=send,
            recv_sem=recv,
            device_id=where,
            device_id_type=pl.DeviceIdType.MESH,
        )

    def await_bytes(ref, sem):
        pltpu.make_async_copy(ref, ref, sem).wait()

    operands = (pos_in, rim_in, feat_in, cot_in, w2_in, w1_in, smat_in, nbr_in)
    places = (pos, rim, feat, cot, w2, w1, smat, nbr)
    loads = [
        pltpu.make_async_copy(source, place, sem_in.at[i])
        for i, (source, place) in enumerate(zip(operands, places))
    ]
    load_pos, load_rim, load_feat, load_cot, load_w2, load_w1, load_smat, load_nbr = loads
    for load in loads:
        load.start()
    barrier = pltpu.get_barrier_semaphore()

    @pl.loop(1, n_dev)
    def _(d):
        pl.semaphore_signal(barrier, inc=1, device_id={"dev": lax.rem(dev + d, n_dev)})

    @pl.loop(1, n_tile)
    def _(d):
        pl.semaphore_signal(barrier, inc=1, device_id={"tile": lax.rem(tile + d, n_tile)})

    sub = lax.broadcasted_iota(I32, (8, CH), 0)
    lane = lax.broadcasted_iota(I32, (8, CH), 1)
    load_pos.wait()
    posv = jnp.zeros((8, CH), I32)
    for r in range(BLK):
        posv = jnp.where(sub == r, pos[r], posv)
    owner = posv // BLK
    count = jnp.zeros((8, CH), I32)
    for r in range(BLK):
        count = count + jnp.where((owner == pos[r] // BLK) & (sub > r), 1, 0)
    slot_of_row = lax.rem(owner - dev + n_dev, n_dev) * 2 + count
    hit = lane == slot_of_row
    row_of_slot = jnp.min(jnp.where(hit, sub, BLK - 1), axis=0, keepdims=True)
    label_of_slot = jnp.min(jnp.where(hit, lax.rem(posv, BLK), BLK), axis=0, keepdims=True)
    idxv[0] = jnp.broadcast_to(row_of_slot, (8, CH))
    idxv[1] = jnp.minimum(slot_of_row, 2 * n_dev - 1)
    labels[0] = label_of_slot
    to_scalars = pltpu.make_async_copy(idxv, idxs, sem_local.at[0])
    to_scalars.start()

    def pack_rims(rows, which):
        for h in range(RIM):
            rims[which, h] = rows[rim[h]]

    def halo_copies(which, table):
        result = []
        for q, where in enumerate(
            (
                dict(tile=lax.rem(tile + 1, n_tile)),
                dict(tile=lax.rem(tile + n_tile - 1, n_tile)),
                dict(dev=lax.rem(dev + 1, n_dev)),
                dict(dev=lax.rem(dev + n_dev - 1, n_dev)),
            )
        ):
            result.append(
                remote(
                    rims.at[which],
                    table.at[pl.ds(BLK + q * RIM, RIM)],
                    sem_halo_s.at[which, q],
                    sem_halo_r.at[which, q],
                    **where,
                )
            )
        return result

    def finish_halo(copies, table):
        for copy in copies:
            copy.wait()
        edges = (tile == 0, tile == n_tile - 1, dev == 0, dev == n_dev - 1)
        for q, edge in enumerate(edges):

            @pl.when(edge)
            def _(q=q):
                table[BLK + q * RIM : BLK + (q + 1) * RIM] = jnp.zeros((RIM, VOX, CH), BF16)

    for table in (tab_m, tab_c, tab_h, tab_p):
        table[BLK + 4 * RIM] = jnp.zeros((VOX, CH), BF16)
    load_rim.wait()
    load_cot.wait()
    tab_c[0:BLK] = cot[...]
    pack_rims(cot, 0)
    load_feat.wait()
    to_scalars.wait()

    @pl.loop(0, n_dev)
    def _(d):
        for c in range(2):
            packed[d, c] = feat[idxs[0, 0, 2 * d + c]]

    arrived[0] = packed[0]

    pl.semaphore_wait(barrier, n_dev + n_tile - 2)

    @pl.loop(1, n_dev)
    def _(d):
        where = lax.rem(dev + d, n_dev)
        remote(labels.at[0], labels.at[d], sem_lab.at[0], sem_lab.at[1], dev=where).start()

    halo_c = halo_copies(0, tab_c)
    for copy in halo_c:
        copy.start()

    @pl.loop(1, n_dev)
    def _(d):
        where = lax.rem(dev + d, n_dev)
        remote(packed.at[d], arrived.at[d], sem_a2a.at[0], sem_a2a.at[1], dev=where).start()

    def flip_weights(source, target):
        for o in range(27):
            piece = source[o * CH : (o + 1) * CH, :].astype(F32)
            target[(26 - o) * CH : (27 - o) * CH, :] = piece.T.astype(BF16)

    def expand(table, y):
        for b in range(BLK):
            near = planes.at[b % 2]
            for i in range(6):
                dx = 0 if i == 0 else (2 if i == 5 else 1)
                row = (i + EDGE - 1) % EDGE
                for t in range(9):
                    near[t * PLANE : (t + 1) * PLANE, i * CH : (i + 1) * CH] = table[
                        nbr[b, dx * 9 + t], row * PLANE : (row + 1) * PLANE, :
                    ]
            moved = dot(smat[...], near[...]).astype(BF16)
            for i in range(6):
                for t in range(9):
                    y[b, i, :, t * CH : (t + 1) * CH] = moved[
                        t * PLANE : (t + 1) * PLANE, i * CH : (i + 1) * CH
                    ]

    def columns(y, kx):
        return y[:, kx : kx + EDGE].reshape(BLK * VOX, 9 * CH)

    def conv(y, w):
        return (
            dot(columns(y, 0), w[0 : 9 * CH, :])
            + dot(columns(y, 1), w[9 * CH : 18 * CH, :])
            + dot(columns(y, 2), w[18 * CH : 27 * CH, :])
        )

    load_w2.wait()
    flip_weights(w2, wt2)
    load_w1.wait()
    flip_weights(w1, wt1)
    load_smat.wait()
    load_nbr.wait()
    finish_halo(halo_c, tab_c)
    expand(tab_c, y_c)
    hidden_grad[...] = conv(y_c, wt2)

    await_bytes(labels.at[pl.ds(1, n_dev - 1)], sem_lab.at[1])
    label_at = jnp.zeros((8, CH), I32)
    for d in range(n_dev):
        label_at = jnp.where(lane // 2 == d, labels[d], label_at)
    label_at = jnp.where(lane < 2 * n_dev, label_at, BLK)
    slotv[0] = jnp.minimum(label_at, BLK - 1)
    slotv[1] = jnp.broadcast_to(
        jnp.max(jnp.where(label_at == sub, lane, 0), axis=1, keepdims=True), (8, CH)
    )
    to_slots = pltpu.make_async_copy(slotv, slots, sem_local.at[0])
    to_slots.start()
    to_slots.wait()
    await_bytes(arrived.at[pl.ds(1, n_dev - 1)], sem_a2a.at[1])
    for s in range(BLK):
        linear = slots[1, s, 0]
        own[0, s] = arrived[linear // 2, lax.rem(linear, 2)]
    tab_m[0:BLK] = own[0]
    pack_rims(own.at[0], 1)
    halo_m = halo_copies(1, tab_m)
    for copy in halo_m:
        copy.start()
    finish_halo(halo_m, tab_m)
    expand(tab_m, y_m)
    pre = conv(y_m, w1)
    gate = jax.nn.sigmoid(pre)
    hidden = (pre * gate).astype(BF16)
    pre_grad = (hidden_grad[...] * gate * (1.0 + pre * (1.0 - gate))).astype(BF16)
    tab_h[0:BLK] = hidden.reshape(BLK, VOX, CH)
    tab_p[0:BLK] = pre_grad.reshape(BLK, VOX, CH)
    own[1] = hidden.reshape(BLK, VOX, CH)
    own[2] = pre_grad.reshape(BLK, VOX, CH)
    pack_rims(own.at[1], 2)
    pack_rims(own.at[2], 3)
    halo_h = halo_copies(2, tab_h)
    halo_p = halo_copies(3, tab_p)
    for copy in halo_h + halo_p:
        copy.start()

    partner = dict(tile=tile + 1 - 2 * core)

    def core_copy(q, chunk):
        start = pl.multiple_of((1 - core) * HALF + chunk * QUARTER, 16)
        return remote(
            grads.at[q, pl.ds(start, QUARTER)],
            core_in.at[q, chunk],
            sem_sum_s.at[q, 0],
            sem_core.at[q, chunk],
            **partner,
        )

    y = lax.rem(dev, 4)
    z = dev // 4
    n_z = n_dev // 4
    dims = (("x", "y"), ("y", "x"))
    place = dict(x=chip_x, y=y)

    def start_core(q):
        for e in (2, 1, 3, 0):
            core_copy(q, lax.rem(place[dims[q][0]] + e, 4)).start()

    hidden_t = own[1].reshape(BLK * VOX, CH).astype(F32).T.astype(BF16)
    for kx in range(3):
        part = dot(hidden_t, columns(y_c, kx))
        for t in range(9):
            o = 26 - (kx * 9 + t)
            grads[1, o * CH : (o + 1) * CH, :] = part[:, t * CH : (t + 1) * CH]
    start_core(1)
    pre_grad_t = own[2].reshape(BLK * VOX, CH).astype(F32).T.astype(BF16)
    for kx in range(3):
        part = dot(pre_grad_t, columns(y_m, kx))
        for t in range(9):
            o = kx * 9 + t
            grads[0, o * CH : (o + 1) * CH, :] = part[:, t * CH : (t + 1) * CH].T
    start_core(0)

    def peer(dim, e):
        if dim == "x":
            other = lax.rem(chip_x + e, n_x)
            return other, dict(tile=other * 2 + core)
        if dim == "y":
            other = lax.rem(y + e, 4)
            return other, dict(dev=z * 4 + other)
        other = lax.rem(z + e, n_z)
        return other, dict(dev=other * 4 + y)

    def sem(q, stage):
        return sem_sum_s.at[q, stage], sem_sum_r.at[q, stage]

    def both_cores(q, chunk):
        start = pl.multiple_of(core * HALF + chunk * QUARTER, 16)
        return grads[q, pl.ds(start, QUARTER), :] + core_in[q, chunk]

    def start_first(q):
        for e in (2, 1, 3):
            other, where = peer(dims[q][0], e)
            core_copy(q, other).wait_recv()
            x_out[q, other] = both_cores(q, other).astype(BF16)
            remote(x_out.at[q, other], x_in.at[q, e - 1], *sem(q, 1), **where).start()
        core_copy(q, place[dims[q][0]]).wait_recv()

    def start_second(q):
        await_bytes(x_in.at[q], sem_sum_r.at[q, 1])
        total = both_cores(q, place[dims[q][0]])
        for e in range(3):
            total = total + x_in[q, e].astype(F32)
        own_sum[q, 0:QUARTER] = total
        own_sum[q, QUARTER:] = jnp.zeros((4 * PIECE - QUARTER, CH), F32)
        for j in range(4):
            y_out[q, j] = own_sum[q, j * PIECE : (j + 1) * PIECE].astype(BF16)
        for e in (2, 1, 3):
            other, where = peer(dims[q][1], e)
            remote(y_out.at[q, other], y_in.at[q, e - 1], *sem(q, 2), **where).start()

    def start_third(q):
        await_bytes(y_in.at[q], sem_sum_r.at[q, 2])
        start = pl.multiple_of(place[dims[q][1]] * PIECE, 16)
        total = own_sum[q, pl.ds(start, PIECE), :]
        for e in range(3):
            total = total + y_in[q, e].astype(F32)
        z_out[q, 0:7] = total.reshape(7, 16, CH)
        z_out[q, 7] = jnp.zeros((16, CH), F32)
        for e in (4, 3, 5, 2, 6, 1, 7):
            other, where = peer("z", e)
            remote(z_out.at[q, other], z_in.at[q, e - 1], *sem(q, 3), **where).start()

    def start_gather_third(q):
        await_bytes(z_in.at[q], sem_sum_r.at[q, 3])
        total = z_out[q, z]
        for e in range(7):
            total = total + z_in[q, e]
        mine = final.at[q, core, place[dims[q][0]], place[dims[q][1]], z]
        mine[...] = (total * scale).astype(BF16)
        for e in (4, 3, 5, 2, 6, 1, 7):
            _, where = peer("z", e)
            remote(mine, mine, *sem(q, 4), **where).start()

    def start_gather_second(q):
        await_bytes(final.at[q, core, 0, 0, pl.ds(0, 7)], sem_sum_r.at[q, 4])
        mine = final.at[q, core, place[dims[q][0]], place[dims[q][1]], pl.ds(0, 7)]
        for e in (2, 1, 3):
            _, where = peer(dims[q][1], e)
            remote(mine, mine, *sem(q, 5), **where).start()

    def gather_core_copy(q, chunk):
        piece = final.at[q, core, chunk, :, pl.ds(0, 7)]
        return remote(piece, piece, *sem(q, 7), **partner)

    def exit_copy(q, chunk):
        return pltpu.make_async_copy(
            final.at[q, core, chunk], out_sums.at[q, core, chunk], sem_out.at[q, chunk]
        )

    def gather_first_copy(q, e):
        mine = final.at[q, core, place[dims[q][0]], :, pl.ds(0, 7)]
        _, where = peer(dims[q][0], e)
        return remote(mine, mine, sem_sum_s.at[q, 6], sem_first.at[q, e - 1], **where)

    def start_gather_first(q):
        await_bytes(final.at[q, core, 0, pl.ds(0, 3), pl.ds(0, 7)], sem_sum_r.at[q, 5])
        for e in (2, 1, 3):
            gather_first_copy(q, e).start()
        gather_core_copy(q, place[dims[q][0]]).start()
        exit_copy(q, place[dims[q][0]]).start()

    def start_gather_core(q):
        for e in (1, 3, 2):
            chunk = lax.rem(place[dims[q][0]] + 4 - e, 4)
            gather_first_copy(q, e).wait_recv()
            gather_core_copy(q, chunk).start()
            exit_copy(q, chunk).start()

    start_first(1)
    start_first(0)
    finish_halo(halo_h, tab_h)
    expand(tab_h, y_x)
    pre_two = conv(y_x, w2)
    leaving[0] = (
        (own[0].reshape(BLK * VOX, CH).astype(F32) + pre_two).astype(BF16).reshape(BLK, VOX, CH)
    )
    exit_output = pltpu.make_async_copy(leaving.at[0], out_output, sem_out.at[0, 5])
    exit_output.start()
    finish_halo(halo_p, tab_p)
    expand(tab_p, y_x)
    back = conv(y_x, wt1) + cot[...].reshape(BLK * VOX, CH).astype(F32)
    own[1] = back.astype(BF16).reshape(BLK, VOX, CH)

    @pl.loop(0, n_dev)
    def _(d):
        for c in range(2):
            repacked[d, c] = own[1, slots[0, 0, 2 * d + c]]

    returned[0] = repacked[0]

    order = [7 * i % n_dev for i in range(1, n_dev)]

    def send_back(offsets):
        for d in offsets:
            where = lax.rem(dev - d + n_dev, n_dev)
            remote(repacked.at[d], returned.at[d], sem_back.at[0], sem_back.at[1], dev=where).start()

    for stage, offsets in (
        (start_second, order[0:6]),
        (start_third, order[6:12]),
        (start_gather_third, order[12:18]),
        (start_gather_second, order[18:24]),
        (start_gather_first, order[24:]),
        (start_gather_core, []),
    ):
        stage(1)
        stage(0)
        send_back(offsets)
    await_bytes(returned.at[pl.ds(1, n_dev - 1)], sem_back.at[1])
    for r in range(BLK):
        linear = idxs[1, r, 0]
        leaving[1, r] = returned[linear // 2, lax.rem(linear, 2)]
    exit_grad = pltpu.make_async_copy(leaving.at[1], out_grad, sem_out.at[1, 5])
    exit_grad.start()

    await_bytes(labels.at[pl.ds(1, n_dev - 1)], sem_lab.at[0])
    await_bytes(packed.at[pl.ds(1, n_dev - 1)], sem_a2a.at[0])
    await_bytes(repacked.at[pl.ds(1, n_dev - 1)], sem_back.at[0])
    for q in (1, 0):
        await_bytes(final.at[q, 1 - core, :, :, pl.ds(0, 7)], sem_sum_r.at[q, 7])
        pltpu.make_async_copy(
            final.at[q, 1 - core], out_sums.at[q, 1 - core], sem_out.at[q, 4]
        ).start()
    for q in range(2):
        await_bytes(core_in.at[q], sem_sum_s.at[q, 0])
        await_bytes(x_in.at[q], sem_sum_s.at[q, 1])
        await_bytes(y_in.at[q], sem_sum_s.at[q, 2])
        await_bytes(z_in.at[q], sem_sum_s.at[q, 3])
        await_bytes(final.at[q, core, 0, 0, pl.ds(0, 7)], sem_sum_s.at[q, 4])
        await_bytes(final.at[q, core, 0, pl.ds(0, 3), pl.ds(0, 7)], sem_sum_s.at[q, 5])
        await_bytes(final.at[q, core, pl.ds(0, 3), :, pl.ds(0, 7)], sem_sum_s.at[q, 6])
        await_bytes(final.at[q, core, :, :, pl.ds(0, 7)], sem_sum_s.at[q, 7])
        for chunk in range(4):
            exit_copy(q, chunk).wait()
        pltpu.make_async_copy(
            final.at[q, 1 - core], out_sums.at[q, 1 - core], sem_out.at[q, 4]
        ).wait()
    exit_output.wait()
    exit_grad.wait()


def finish_kernel(sums, output_in, grad_in, output, grad, grad_one, grad_two):
    output[...] = output_in[...]
    grad[...] = grad_in[...]
    for q, target in enumerate((grad_one, grad_two)):
        rows = sums[q, 0, 0, :, 0:7].reshape(4 * PIECE, CH)
        target[...] = rows[0:QUARTER].astype(F32)


def per_device(
    n_tile, n_dev, features, morton_pos, neighbours, rim, cotangent, weight_one, weight_two
):
    blocks, voxels, channels = features.shape
    scale = 1.0 / math.sqrt(blocks * voxels * n_tile * n_dev)
    n_x = n_tile // 2
    hbm = pl.BlockSpec(memory_space=pltpu.HBM)
    dma = pltpu.SemaphoreType.DMA
    block_table = pltpu.VMEM((BLK + 4 * RIM + 1, VOX, CH), BF16)
    wide = pltpu.VMEM((BLK, 6, PLANE, 9 * CH), BF16)
    flat = pltpu.VMEM((BLK * VOX, CH), F32)
    slab = pltpu.VMEM((n_dev, 2, VOX, CH), BF16)
    output, input_grad, sums = pl.pallas_call(
        functools.partial(unit_kernel, n_tile, n_dev, scale),
        out_shape=(
            jax.ShapeDtypeStruct(features.shape, BF16),
            jax.ShapeDtypeStruct(features.shape, BF16),
            jax.ShapeDtypeStruct((2, 2, 4, 4, 8, 16, CH), BF16),
        ),
        in_specs=[hbm] * 8,
        out_specs=(hbm, hbm, hbm),
        scratch_shapes=[
            pltpu.SMEM(morton_pos.shape, I32),
            pltpu.SMEM(neighbours.shape, I32),
            pltpu.SMEM(rim.shape, I32),
            pltpu.VMEM(features.shape, BF16),
            pltpu.VMEM(cotangent.shape, BF16),
            pltpu.VMEM(weight_one.shape, BF16),
            pltpu.VMEM(weight_two.shape, BF16),
            pltpu.VMEM((9 * PLANE, 9 * PLANE), BF16),
            pltpu.VMEM((2, 8, CH), I32),
            pltpu.SMEM((2, 8, CH), I32),
            pltpu.VMEM((2, 8, CH), I32),
            pltpu.SMEM((2, 8, CH), I32),
            pltpu.VMEM((n_dev, 1, CH), I32),
            slab,
            slab,
            slab,
            slab,
            block_table,
            block_table,
            block_table,
            block_table,
            pltpu.VMEM((3, BLK, VOX, CH), BF16),
            pltpu.VMEM((2, BLK, VOX, CH), BF16),
            pltpu.VMEM((4, RIM, VOX, CH), BF16),
            pltpu.VMEM((27 * CH, CH), BF16),
            pltpu.VMEM((27 * CH, CH), BF16),
            pltpu.VMEM((2, 9 * PLANE, 6 * CH), BF16),
            wide,
            wide,
            wide,
            flat,
            flat,
            pltpu.VMEM((2, 27 * CH, CH), F32),
            pltpu.VMEM((2, 4, QUARTER, CH), F32),
            pltpu.VMEM((2, 4, QUARTER, CH), BF16),
            pltpu.VMEM((2, 3, QUARTER, CH), BF16),
            pltpu.VMEM((2, 4, PIECE, CH), BF16),
            pltpu.VMEM((2, 3, PIECE, CH), BF16),
            pltpu.VMEM((2, 4 * PIECE, CH), F32),
            pltpu.VMEM((2, 8, 16, CH), F32),
            pltpu.VMEM((2, 7, 16, CH), F32),
            pltpu.VMEM((2, 2, 4, 4, 8, 16, CH), BF16),
            dma((8,)),
            dma((1,)),
            dma((2,)),
            dma((2,)),
            dma((2,)),
            dma((4, 4)),
            dma((4, 4)),
            dma((2, 8)),
            dma((2, 8)),
            dma((2, 3)),
            dma((2, 4)),
            dma((2, 6)),
        ],
        compiler_params=pltpu.CompilerParams(
            collective_id=0, has_side_effects=True, vmem_limit_bytes=62 * 1024 * 1024
        ),
    )(
        morton_pos,
        neighbours,
        rim,
        features,
        cotangent,
        weight_one,
        weight_two,
        jnp.asarray(shift_matrix(), BF16),
    )
    one_block = pl.BlockSpec((1, voxels, channels), lambda i: (i, 0, 0))
    kernel_rows = pl.BlockSpec((QUARTER, channels), lambda i: (i, 0))
    kernel_shape = jax.ShapeDtypeStruct(weight_one.shape, F32)
    return pl.pallas_call(
        finish_kernel,
        grid=(8,),
        out_shape=(
            jax.ShapeDtypeStruct(features.shape, BF16),
            jax.ShapeDtypeStruct(features.shape, BF16),
            kernel_shape,
            kernel_shape,
        ),
        in_specs=[
            pl.BlockSpec((2, 1, 1, 4, 8, 16, CH), lambda i: (0, i // 4, i % 4, 0, 0, 0, 0)),
            one_block,
            one_block,
        ],
        out_specs=(one_block, one_block, kernel_rows, kernel_rows),
    )(sums, output, input_grad)


def solution(mesh):
    placed = (
        P(("tile", "dev"), None, None),
        P(("tile", "dev")),
        P(("tile", "dev"), None),
        P(("tile", "dev")),
        P(("tile", "dev"), None, None),
        P(),
        P(),
    )
    return jax.shard_map(
        functools.partial(per_device, mesh.shape["tile"], mesh.shape["dev"]),
        mesh=mesh,
        in_specs=placed,
        out_specs=(P(("tile", "dev"), None, None), P(("tile", "dev"), None, None), P(), P()),
        check_vma=False,
    )
```

```python
import functools
import math

import jax
import jax.numpy as jnp
import numpy as np
from jax import lax
from jax.experimental import pallas as pl
from jax.experimental.pallas import tpu as pltpu
from jax.sharding import PartitionSpec as P

EDGE = 4
PLANE = EDGE * EDGE
BLK = 8
VOX = 64
CH = 128
RIM = 4
HALF = 27 * CH // 2
QUARTER = HALF // 4
TILES = QUARTER // 16
PIECE = 7 * 16
F32 = jnp.float32
BF16 = jnp.bfloat16
I32 = jnp.int32


def shift_matrix():
    result = np.zeros((9 * PLANE, 9 * PLANE), np.float32)
    for ky in range(3):
        for kz in range(3):
            for j in range(EDGE):
                for k in range(EDGE):
                    y, z = j + ky - 1, k + kz - 1
                    dy, dz = y // EDGE + 1, z // EDGE + 1
                    source = ((dy * 3 + dz) * EDGE + y % EDGE) * EDGE + z % EDGE
                    result[((ky * 3 + kz) * EDGE + j) * EDGE + k, source] = 1.0
    return result


def dot(left, right):
    return jnp.dot(left, right, preferred_element_type=F32)


def unit_kernel(
    n_tile,
    n_dev,
    scale,
    pos_in,
    nbr_in,
    rim_in,
    feat_in,
    cot_in,
    w1_in,
    w2_in,
    smat_in,
    out_output,
    out_grad,
    out_sums,
    pos,
    nbr,
    rim,
    feat,
    cot,
    w1,
    w2,
    smat,
    idxv,
    idxs,
    slotv,
    slots,
    labels,
    packed,
    arrived,
    repacked,
    returned,
    tab_m,
    tab_c,
    tab_h,
    tab_p,
    own,
    leaving,
    rims,
    wt1,
    wt2,
    planes,
    y_m,
    y_c,
    y_x,
    pre_one,
    hidden_grad,
    grads,
    core_in,
    x_out,
    x_in,
    y_out,
    y_in,
    own_sum,
    z_out,
    z_in,
    final,
    sem_in,
    sem_local,
    sem_a2a,
    sem_lab,
    sem_back,
    sem_halo_s,
    sem_halo_r,
    sem_sum_s,
    sem_sum_r,
    sem_first,
    sem_core,
    sem_out,
):
    tile = lax.axis_index("tile")
    dev = lax.axis_index("dev")
    core = lax.rem(tile, 2)
    chip_x = tile // 2
    n_x = n_tile // 2

    def remote(src, dst, send, recv, **where):
        return pltpu.make_async_remote_copy(
            src_ref=src,
            dst_ref=dst,
            send_sem=send,
            recv_sem=recv,
            device_id=where,
            device_id_type=pl.DeviceIdType.MESH,
        )

    def await_bytes(ref, sem):
        pltpu.make_async_copy(ref, ref, sem).wait()

    operands = (pos_in, rim_in, feat_in, cot_in, w2_in, w1_in, smat_in, nbr_in)
    places = (pos, rim, feat, cot, w2, w1, smat, nbr)
    loads = [
        pltpu.make_async_copy(source, place, sem_in.at[i])
        for i, (source, place) in enumerate(zip(operands, places))
    ]
    load_pos, load_rim, load_feat, load_cot, load_w2, load_w1, load_smat, load_nbr = loads
    for load in loads:
        load.start()
    barrier = pltpu.get_barrier_semaphore()

    @pl.loop(1, n_dev)
    def _(d):
        pl.semaphore_signal(barrier, inc=1, device_id={"dev": lax.rem(dev + d, n_dev)})

    @pl.loop(1, n_tile)
    def _(d):
        pl.semaphore_signal(barrier, inc=1, device_id={"tile": lax.rem(tile + d, n_tile)})

    sub = lax.broadcasted_iota(I32, (8, CH), 0)
    lane = lax.broadcasted_iota(I32, (8, CH), 1)
    load_pos.wait()
    posv = jnp.zeros((8, CH), I32)
    for r in range(BLK):
        posv = jnp.where(sub == r, pos[r], posv)
    owner = posv // BLK
    count = jnp.zeros((8, CH), I32)
    for r in range(BLK):
        count = count + jnp.where((owner == pos[r] // BLK) & (sub > r), 1, 0)
    slot_of_row = lax.rem(owner - dev + n_dev, n_dev) * 2 + count
    hit = lane == slot_of_row
    row_of_slot = jnp.min(jnp.where(hit, sub, BLK - 1), axis=0, keepdims=True)
    label_of_slot = jnp.min(jnp.where(hit, lax.rem(posv, BLK), BLK), axis=0, keepdims=True)
    idxv[0] = jnp.broadcast_to(row_of_slot, (8, CH))
    idxv[1] = jnp.minimum(slot_of_row, 2 * n_dev - 1)
    labels[0] = label_of_slot
    to_scalars = pltpu.make_async_copy(idxv, idxs, sem_local.at[0])
    to_scalars.start()

    def pack_rims(rows, which):
        for h in range(RIM):
            rims[which, h] = rows[rim[h]]

    def halo_copies(which, table):
        result = []
        for q, where in enumerate(
            (
                dict(tile=lax.rem(tile + 1, n_tile)),
                dict(tile=lax.rem(tile + n_tile - 1, n_tile)),
                dict(dev=lax.rem(dev + 1, n_dev)),
                dict(dev=lax.rem(dev + n_dev - 1, n_dev)),
            )
        ):
            result.append(
                remote(
                    rims.at[which],
                    table.at[pl.ds(BLK + q * RIM, RIM)],
                    sem_halo_s.at[which, q],
                    sem_halo_r.at[which, q],
                    **where,
                )
            )
        return result

    def finish_halo(copies, table):
        for copy in copies:
            copy.wait()
        edges = (tile == 0, tile == n_tile - 1, dev == 0, dev == n_dev - 1)
        for q, edge in enumerate(edges):

            @pl.when(edge)
            def _(q=q):
                table[BLK + q * RIM : BLK + (q + 1) * RIM] = jnp.zeros((RIM, VOX, CH), BF16)

    for table in (tab_m, tab_c, tab_h, tab_p):
        table[BLK + 4 * RIM] = jnp.zeros((VOX, CH), BF16)
    load_rim.wait()
    load_cot.wait()
    tab_c[0:BLK] = cot[...]
    pack_rims(cot, 0)
    load_feat.wait()
    to_scalars.wait()

    @pl.loop(0, n_dev)
    def _(d):
        for c in range(2):
            packed[d, c] = feat[idxs[0, 0, 2 * d + c]]

    arrived[0] = packed[0]

    pl.semaphore_wait(barrier, n_dev + n_tile - 2)

    @pl.loop(1, n_dev)
    def _(d):
        where = lax.rem(dev + d, n_dev)
        remote(labels.at[0], labels.at[d], sem_lab.at[0], sem_lab.at[1], dev=where).start()

    halo_c = halo_copies(0, tab_c)
    for copy in halo_c:
        copy.start()

    @pl.loop(1, n_dev)
    def _(d):
        where = lax.rem(dev + d, n_dev)
        remote(packed.at[d], arrived.at[d], sem_a2a.at[0], sem_a2a.at[1], dev=where).start()

    def flip_weights(source, target):
        for o in range(27):
            piece = source[o * CH : (o + 1) * CH, :].astype(F32)
            target[(26 - o) * CH : (27 - o) * CH, :] = piece.T.astype(BF16)

    def expand(table, y):
        for b in range(BLK):
            near = planes.at[b % 2]
            for i in range(6):
                dx = 0 if i == 0 else (2 if i == 5 else 1)
                row = (i + EDGE - 1) % EDGE
                for t in range(9):
                    near[t * PLANE : (t + 1) * PLANE, i * CH : (i + 1) * CH] = table[
                        nbr[b, dx * 9 + t], row * PLANE : (row + 1) * PLANE, :
                    ]
            moved = dot(smat[...], near[...]).astype(BF16)
            for i in range(6):
                for t in range(9):
                    y[b, i, :, t * CH : (t + 1) * CH] = moved[
                        t * PLANE : (t + 1) * PLANE, i * CH : (i + 1) * CH
                    ]

    def columns(y, kx):
        return y[:, kx : kx + EDGE].reshape(BLK * VOX, 9 * CH)

    def conv(y, w):
        return (
            dot(columns(y, 0), w[0 : 9 * CH, :])
            + dot(columns(y, 1), w[9 * CH : 18 * CH, :])
            + dot(columns(y, 2), w[18 * CH : 27 * CH, :])
        )

    load_w2.wait()
    flip_weights(w2, wt2)
    load_w1.wait()
    flip_weights(w1, wt1)
    load_smat.wait()
    load_nbr.wait()
    finish_halo(halo_c, tab_c)
    expand(tab_c, y_c)
    hidden_grad[...] = conv(y_c, wt2)

    await_bytes(labels.at[pl.ds(1, n_dev - 1)], sem_lab.at[1])
    label_at = jnp.zeros((8, CH), I32)
    for d in range(n_dev):
        label_at = jnp.where(lane // 2 == d, labels[d], label_at)
    label_at = jnp.where(lane < 2 * n_dev, label_at, BLK)
    slotv[0] = jnp.minimum(label_at, BLK - 1)
    slotv[1] = jnp.broadcast_to(
        jnp.max(jnp.where(label_at == sub, lane, 0), axis=1, keepdims=True), (8, CH)
    )
    to_slots = pltpu.make_async_copy(slotv, slots, sem_local.at[0])
    to_slots.start()
    to_slots.wait()
    await_bytes(arrived.at[pl.ds(1, n_dev - 1)], sem_a2a.at[1])
    for s in range(BLK):
        linear = slots[1, s, 0]
        own[0, s] = arrived[linear // 2, lax.rem(linear, 2)]
    tab_m[0:BLK] = own[0]
    pack_rims(own.at[0], 1)
    halo_m = halo_copies(1, tab_m)
    for copy in halo_m:
        copy.start()
    finish_halo(halo_m, tab_m)
    expand(tab_m, y_m)
    pre = conv(y_m, w1)
    gate = jax.nn.sigmoid(pre)
    hidden = (pre * gate).astype(BF16)
    pre_grad = (hidden_grad[...] * gate * (1.0 + pre * (1.0 - gate))).astype(BF16)
    tab_h[0:BLK] = hidden.reshape(BLK, VOX, CH)
    tab_p[0:BLK] = pre_grad.reshape(BLK, VOX, CH)
    own[1] = hidden.reshape(BLK, VOX, CH)
    own[2] = pre_grad.reshape(BLK, VOX, CH)
    pack_rims(own.at[1], 2)
    pack_rims(own.at[2], 3)
    halo_h = halo_copies(2, tab_h)
    halo_p = halo_copies(3, tab_p)
    for copy in halo_h + halo_p:
        copy.start()

    partner = dict(tile=tile + 1 - 2 * core)

    def core_copy(q, chunk):
        start = pl.multiple_of((1 - core) * HALF + chunk * QUARTER, 16)
        return remote(
            grads.at[q, pl.ds(start, QUARTER)],
            core_in.at[q, chunk],
            sem_sum_s.at[q, 0],
            sem_core.at[q, chunk],
            **partner,
        )

    y = lax.rem(dev, 4)
    z = dev // 4
    n_z = n_dev // 4
    dims = (("x", "y"), ("y", "x"))
    place = dict(x=chip_x, y=y)

    def start_core(q):
        for e in (2, 1, 3, 0):
            core_copy(q, lax.rem(place[dims[q][0]] + e, 4)).start()

    hidden_t = own[1].reshape(BLK * VOX, CH).astype(F32).T.astype(BF16)
    for kx in range(3):
        part = dot(hidden_t, columns(y_c, kx))
        for t in range(9):
            o = 26 - (kx * 9 + t)
            grads[1, o * CH : (o + 1) * CH, :] = part[:, t * CH : (t + 1) * CH]
    start_core(1)
    pre_grad_t = own[2].reshape(BLK * VOX, CH).astype(F32).T.astype(BF16)
    for kx in range(3):
        part = dot(pre_grad_t, columns(y_m, kx))
        for t in range(9):
            o = kx * 9 + t
            grads[0, o * CH : (o + 1) * CH, :] = part[:, t * CH : (t + 1) * CH].T
    start_core(0)

    def peer(dim, e):
        if dim == "x":
            other = lax.rem(chip_x + e, n_x)
            return other, dict(tile=other * 2 + core)
        if dim == "y":
            other = lax.rem(y + e, 4)
            return other, dict(dev=z * 4 + other)
        other = lax.rem(z + e, n_z)
        return other, dict(dev=other * 4 + y)

    def sem(q, stage):
        return sem_sum_s.at[q, stage], sem_sum_r.at[q, stage]

    def both_cores(q, chunk):
        start = pl.multiple_of(core * HALF + chunk * QUARTER, 16)
        return grads[q, pl.ds(start, QUARTER), :] + core_in[q, chunk]

    def start_first(q):
        for e in (2, 1, 3):
            other, where = peer(dims[q][0], e)
            core_copy(q, other).wait_recv()
            x_out[q, other] = both_cores(q, other).astype(BF16)
            remote(x_out.at[q, other], x_in.at[q, e - 1], *sem(q, 1), **where).start()
        core_copy(q, place[dims[q][0]]).wait_recv()

    def start_second(q):
        await_bytes(x_in.at[q], sem_sum_r.at[q, 1])
        total = both_cores(q, place[dims[q][0]])
        for e in range(3):
            total = total + x_in[q, e].astype(F32)
        own_sum[q, 0:QUARTER] = total
        own_sum[q, QUARTER:] = jnp.zeros((4 * PIECE - QUARTER, CH), F32)
        for j in range(4):
            y_out[q, j] = own_sum[q, j * PIECE : (j + 1) * PIECE].astype(BF16)
        for e in (2, 1, 3):
            other, where = peer(dims[q][1], e)
            remote(y_out.at[q, other], y_in.at[q, e - 1], *sem(q, 2), **where).start()

    def start_third(q):
        await_bytes(y_in.at[q], sem_sum_r.at[q, 2])
        start = pl.multiple_of(place[dims[q][1]] * PIECE, 16)
        total = own_sum[q, pl.ds(start, PIECE), :]
        for e in range(3):
            total = total + y_in[q, e].astype(F32)
        z_out[q, 0:7] = total.reshape(7, 16, CH)
        z_out[q, 7] = jnp.zeros((16, CH), F32)
        for e in (4, 3, 5, 2, 6, 1, 7):
            other, where = peer("z", e)
            remote(z_out.at[q, other], z_in.at[q, e - 1], *sem(q, 3), **where).start()

    def start_gather_third(q):
        await_bytes(z_in.at[q], sem_sum_r.at[q, 3])
        total = z_out[q, z]
        for e in range(7):
            total = total + z_in[q, e]
        mine = final.at[q, core, place[dims[q][0]], place[dims[q][1]], z]
        mine[...] = (total * scale).astype(BF16)
        for e in (4, 3, 5, 2, 6, 1, 7):
            _, where = peer("z", e)
            remote(mine, mine, *sem(q, 4), **where).start()

    def start_gather_second(q):
        await_bytes(final.at[q, core, 0, 0, pl.ds(0, 7)], sem_sum_r.at[q, 4])
        mine = final.at[q, core, place[dims[q][0]], place[dims[q][1]], pl.ds(0, 7)]
        for e in (2, 1, 3):
            _, where = peer(dims[q][1], e)
            remote(mine, mine, *sem(q, 5), **where).start()

    def gather_core_copy(q, chunk):
        piece = final.at[q, core, chunk, :, pl.ds(0, 7)]
        return remote(piece, piece, *sem(q, 7), **partner)

    def exit_copy(q, chunk):
        return pltpu.make_async_copy(
            final.at[q, core, chunk], out_sums.at[q, core, chunk], sem_out.at[q, chunk]
        )

    def gather_first_copy(q, e):
        mine = final.at[q, core, place[dims[q][0]], :, pl.ds(0, 7)]
        _, where = peer(dims[q][0], e)
        return remote(mine, mine, sem_sum_s.at[q, 6], sem_first.at[q, e - 1], **where)

    def start_gather_first(q):
        await_bytes(final.at[q, core, 0, pl.ds(0, 3), pl.ds(0, 7)], sem_sum_r.at[q, 5])
        for e in (2, 1, 3):
            gather_first_copy(q, e).start()
        gather_core_copy(q, place[dims[q][0]]).start()
        exit_copy(q, place[dims[q][0]]).start()

    def start_gather_core(q):
        for e in (1, 3, 2):
            chunk = lax.rem(place[dims[q][0]] + 4 - e, 4)
            gather_first_copy(q, e).wait_recv()
            gather_core_copy(q, chunk).start()
            exit_copy(q, chunk).start()

    start_first(1)
    start_first(0)
    finish_halo(halo_h, tab_h)
    expand(tab_h, y_x)
    pre_two = conv(y_x, w2)
    leaving[0] = (
        (own[0].reshape(BLK * VOX, CH).astype(F32) + pre_two).astype(BF16).reshape(BLK, VOX, CH)
    )
    exit_output = pltpu.make_async_copy(leaving.at[0], out_output, sem_out.at[0, 5])
    exit_output.start()
    finish_halo(halo_p, tab_p)
    expand(tab_p, y_x)
    back = conv(y_x, wt1) + cot[...].reshape(BLK * VOX, CH).astype(F32)
    own[1] = back.astype(BF16).reshape(BLK, VOX, CH)

    @pl.loop(0, n_dev)
    def _(d):
        for c in range(2):
            repacked[d, c] = own[1, slots[0, 0, 2 * d + c]]

    returned[0] = repacked[0]

    order = [7 * i % n_dev for i in range(1, n_dev)]

    def send_back(offsets):
        for d in offsets:
            where = lax.rem(dev - d + n_dev, n_dev)
            remote(repacked.at[d], returned.at[d], sem_back.at[0], sem_back.at[1], dev=where).start()

    for stage, offsets in (
        (start_second, order[0:6]),
        (start_third, order[6:12]),
        (start_gather_third, order[12:18]),
        (start_gather_second, order[18:24]),
        (start_gather_first, order[24:]),
        (start_gather_core, []),
    ):
        stage(1)
        stage(0)
        send_back(offsets)
    await_bytes(returned.at[pl.ds(1, n_dev - 1)], sem_back.at[1])
    for r in range(BLK):
        linear = idxs[1, r, 0]
        leaving[1, r] = returned[linear // 2, lax.rem(linear, 2)]
    exit_grad = pltpu.make_async_copy(leaving.at[1], out_grad, sem_out.at[1, 5])
    exit_grad.start()

    await_bytes(labels.at[pl.ds(1, n_dev - 1)], sem_lab.at[0])
    await_bytes(packed.at[pl.ds(1, n_dev - 1)], sem_a2a.at[0])
    await_bytes(repacked.at[pl.ds(1, n_dev - 1)], sem_back.at[0])
    for q in (1, 0):
        await_bytes(final.at[q, 1 - core, :, :, pl.ds(0, 7)], sem_sum_r.at[q, 7])
        pltpu.make_async_copy(
            final.at[q, 1 - core], out_sums.at[q, 1 - core], sem_out.at[q, 4]
        ).start()
    for q in range(2):
        await_bytes(core_in.at[q], sem_sum_s.at[q, 0])
        await_bytes(x_in.at[q], sem_sum_s.at[q, 1])
        await_bytes(y_in.at[q], sem_sum_s.at[q, 2])
        await_bytes(z_in.at[q], sem_sum_s.at[q, 3])
        await_bytes(final.at[q, core, 0, 0, pl.ds(0, 7)], sem_sum_s.at[q, 4])
        await_bytes(final.at[q, core, 0, pl.ds(0, 3), pl.ds(0, 7)], sem_sum_s.at[q, 5])
        await_bytes(final.at[q, core, pl.ds(0, 3), :, pl.ds(0, 7)], sem_sum_s.at[q, 6])
        await_bytes(final.at[q, core, :, :, pl.ds(0, 7)], sem_sum_s.at[q, 7])
        for chunk in range(4):
            exit_copy(q, chunk).wait()
        pltpu.make_async_copy(
            final.at[q, 1 - core], out_sums.at[q, 1 - core], sem_out.at[q, 4]
        ).wait()
    exit_output.wait()
    exit_grad.wait()


def finish_kernel(
    sums, output_in, grad_in, output, grad, grad_one, grad_two, held, wide, sem_load, sem_store, sem_pass
):
    passes = [
        pltpu.make_async_copy(output_in, output, sem_pass.at[0]),
        pltpu.make_async_copy(grad_in, grad, sem_pass.at[1]),
    ]
    parts = [(q, c, j) for c in range(2) for j in range(4) for q in range(2)]
    loads = [pltpu.make_async_copy(sums.at[part], held.at[part], sem_load.at[part]) for part in parts]
    for copy in loads + passes:
        copy.start()
    stores = []
    for part, load in zip(parts, loads):
        q, c, j = part
        load.wait()
        rows = held[q, c, j, :, 0:7].reshape(4 * PIECE, CH)
        wide[q, c, j] = rows[0:QUARTER].astype(F32)
        target = (grad_one, grad_two)[q].at[pl.ds(c * HALF + j * QUARTER, QUARTER)]
        stores.append(pltpu.make_async_copy(wide.at[part], target, sem_store.at[part]))
        stores[-1].start()
    for copy in stores + passes:
        copy.wait()


def per_device(
    n_tile, n_dev, features, morton_pos, neighbours, rim, cotangent, weight_one, weight_two
):
    blocks, voxels, channels = features.shape
    scale = 1.0 / math.sqrt(blocks * voxels * n_tile * n_dev)
    n_x = n_tile // 2
    hbm = pl.BlockSpec(memory_space=pltpu.HBM)
    dma = pltpu.SemaphoreType.DMA
    block_table = pltpu.VMEM((BLK + 4 * RIM + 1, VOX, CH), BF16)
    wide = pltpu.VMEM((BLK, 6, PLANE, 9 * CH), BF16)
    flat = pltpu.VMEM((BLK * VOX, CH), F32)
    slab = pltpu.VMEM((n_dev, 2, VOX, CH), BF16)
    output, input_grad, sums = pl.pallas_call(
        functools.partial(unit_kernel, n_tile, n_dev, scale),
        out_shape=(
            jax.ShapeDtypeStruct(features.shape, BF16),
            jax.ShapeDtypeStruct(features.shape, BF16),
            jax.ShapeDtypeStruct((2, 2, 4, 4, 8, 16, CH), BF16),
        ),
        in_specs=[hbm] * 8,
        out_specs=(hbm, hbm, hbm),
        scratch_shapes=[
            pltpu.SMEM(morton_pos.shape, I32),
            pltpu.SMEM(neighbours.shape, I32),
            pltpu.SMEM(rim.shape, I32),
            pltpu.VMEM(features.shape, BF16),
            pltpu.VMEM(cotangent.shape, BF16),
            pltpu.VMEM(weight_one.shape, BF16),
            pltpu.VMEM(weight_two.shape, BF16),
            pltpu.VMEM((9 * PLANE, 9 * PLANE), BF16),
            pltpu.VMEM((2, 8, CH), I32),
            pltpu.SMEM((2, 8, CH), I32),
            pltpu.VMEM((2, 8, CH), I32),
            pltpu.SMEM((2, 8, CH), I32),
            pltpu.VMEM((n_dev, 1, CH), I32),
            slab,
            slab,
            slab,
            slab,
            block_table,
            block_table,
            block_table,
            block_table,
            pltpu.VMEM((3, BLK, VOX, CH), BF16),
            pltpu.VMEM((2, BLK, VOX, CH), BF16),
            pltpu.VMEM((4, RIM, VOX, CH), BF16),
            pltpu.VMEM((27 * CH, CH), BF16),
            pltpu.VMEM((27 * CH, CH), BF16),
            pltpu.VMEM((2, 9 * PLANE, 6 * CH), BF16),
            wide,
            wide,
            wide,
            flat,
            flat,
            pltpu.VMEM((2, 27 * CH, CH), F32),
            pltpu.VMEM((2, 4, QUARTER, CH), F32),
            pltpu.VMEM((2, 4, QUARTER, CH), BF16),
            pltpu.VMEM((2, 3, QUARTER, CH), BF16),
            pltpu.VMEM((2, 4, PIECE, CH), BF16),
            pltpu.VMEM((2, 3, PIECE, CH), BF16),
            pltpu.VMEM((2, 4 * PIECE, CH), F32),
            pltpu.VMEM((2, 8, 16, CH), F32),
            pltpu.VMEM((2, 7, 16, CH), F32),
            pltpu.VMEM((2, 2, 4, 4, 8, 16, CH), BF16),
            dma((8,)),
            dma((1,)),
            dma((2,)),
            dma((2,)),
            dma((2,)),
            dma((4, 4)),
            dma((4, 4)),
            dma((2, 8)),
            dma((2, 8)),
            dma((2, 3)),
            dma((2, 4)),
            dma((2, 6)),
        ],
        compiler_params=pltpu.CompilerParams(
            collective_id=0, has_side_effects=True, vmem_limit_bytes=62 * 1024 * 1024
        ),
    )(
        morton_pos,
        neighbours,
        rim,
        features,
        cotangent,
        weight_one,
        weight_two,
        jnp.asarray(shift_matrix(), BF16),
    )
    kernel_shape = jax.ShapeDtypeStruct(weight_one.shape, F32)
    return pl.pallas_call(
        finish_kernel,
        out_shape=(
            jax.ShapeDtypeStruct(features.shape, BF16),
            jax.ShapeDtypeStruct(features.shape, BF16),
            kernel_shape,
            kernel_shape,
        ),
        in_specs=[hbm] * 3,
        out_specs=(hbm,) * 4,
        scratch_shapes=[
            pltpu.VMEM((2, 2, 4, 4, 8, 16, CH), BF16),
            pltpu.VMEM((2, 2, 4, QUARTER, CH), F32),
            dma((2, 2, 4)),
            dma((2, 2, 4)),
            dma((2,)),
        ],
        compiler_params=pltpu.CompilerParams(vmem_limit_bytes=62 * 1024 * 1024),
    )(sums, output, input_grad)


def solution(mesh):
    placed = (
        P(("tile", "dev"), None, None),
        P(("tile", "dev")),
        P(("tile", "dev"), None),
        P(("tile", "dev")),
        P(("tile", "dev"), None, None),
        P(),
        P(),
    )
    return jax.shard_map(
        functools.partial(per_device, mesh.shape["tile"], mesh.shape["dev"]),
        mesh=mesh,
        in_specs=placed,
        out_specs=(P(("tile", "dev"), None, None), P(("tile", "dev"), None, None), P(), P()),
        check_vma=False,
    )
```

```python
import functools
import math

import jax
import jax.numpy as jnp
import numpy as np
from jax import lax
from jax.experimental import pallas as pl
from jax.experimental.pallas import tpu as pltpu
from jax.sharding import PartitionSpec as P

EDGE = 4
PLANE = EDGE * EDGE
BLK = 8
VOX = 64
CH = 128
RIM = 4
HALF = 27 * CH // 2
QUARTER = HALF // 4
TILES = QUARTER // 16
PIECE = 7 * 16
F32 = jnp.float32
BF16 = jnp.bfloat16
I32 = jnp.int32


def shift_matrix():
    result = np.zeros((9 * PLANE, 9 * PLANE), np.float32)
    for ky in range(3):
        for kz in range(3):
            for j in range(EDGE):
                for k in range(EDGE):
                    y, z = j + ky - 1, k + kz - 1
                    dy, dz = y // EDGE + 1, z // EDGE + 1
                    source = ((dy * 3 + dz) * EDGE + y % EDGE) * EDGE + z % EDGE
                    result[((ky * 3 + kz) * EDGE + j) * EDGE + k, source] = 1.0
    return result


def dot(left, right):
    return jnp.dot(left, right, preferred_element_type=F32)


def unit_kernel(
    n_tile,
    n_dev,
    scale,
    pos_in,
    nbr_in,
    rim_in,
    feat_in,
    cot_in,
    w1_in,
    w2_in,
    smat_in,
    out_output,
    out_grad,
    out_sums,
    pos,
    nbr,
    rim,
    feat,
    cot,
    w1,
    w2,
    smat,
    idxv,
    idxs,
    slotv,
    slots,
    labels,
    z_labels,
    z_slotv,
    z_slots,
    ring_0,
    ring_1,
    ring_2,
    ring_3,
    y_send,
    y_got,
    repacked,
    returned,
    tab_m,
    tab_c,
    tab_h,
    tab_p,
    own,
    leaving,
    rims,
    wt1,
    wt2,
    planes,
    y_m,
    y_c,
    y_x,
    pre_one,
    hidden_grad,
    grads,
    core_in,
    x_out,
    x_in,
    y_out,
    y_in,
    own_sum,
    z_out,
    z_in,
    final,
    sem_in,
    sem_local,
    sem_ring_s,
    sem_ring_r,
    sem_y,
    sem_z_lab,
    sem_lab,
    sem_back,
    sem_halo_s,
    sem_halo_r,
    sem_sum_s,
    sem_sum_r,
    sem_first,
    sem_core,
    sem_out,
):
    tile = lax.axis_index("tile")
    dev = lax.axis_index("dev")
    core = lax.rem(tile, 2)
    chip_x = tile // 2
    n_x = n_tile // 2

    def remote(src, dst, send, recv, **where):
        return pltpu.make_async_remote_copy(
            src_ref=src,
            dst_ref=dst,
            send_sem=send,
            recv_sem=recv,
            device_id=where,
            device_id_type=pl.DeviceIdType.MESH,
        )

    def await_bytes(ref, sem):
        pltpu.make_async_copy(ref, ref, sem).wait()

    operands = (pos_in, rim_in, feat_in, cot_in, w2_in, w1_in, smat_in, nbr_in)
    places = (pos, rim, feat, cot, w2, w1, smat, nbr)
    loads = [
        pltpu.make_async_copy(source, place, sem_in.at[i])
        for i, (source, place) in enumerate(zip(operands, places))
    ]
    load_pos, load_rim, load_feat, load_cot, load_w2, load_w1, load_smat, load_nbr = loads
    for load in loads:
        load.start()
    barrier = pltpu.get_barrier_semaphore()

    @pl.loop(1, n_dev)
    def _(d):
        pl.semaphore_signal(barrier, inc=1, device_id={"dev": lax.rem(dev + d, n_dev)})

    @pl.loop(1, n_tile)
    def _(d):
        pl.semaphore_signal(barrier, inc=1, device_id={"tile": lax.rem(tile + d, n_tile)})

    sub = lax.broadcasted_iota(I32, (8, CH), 0)
    lane = lax.broadcasted_iota(I32, (8, CH), 1)
    load_pos.wait()
    posv = jnp.zeros((8, CH), I32)
    for r in range(BLK):
        posv = jnp.where(sub == r, pos[r], posv)
    owner = posv // BLK
    count = jnp.zeros((8, CH), I32)
    for r in range(BLK):
        count = count + jnp.where((owner == pos[r] // BLK) & (sub > r), 1, 0)
    slot_of_row = lax.rem(owner - dev + n_dev, n_dev) * 2 + count
    hit = lane == slot_of_row
    row_of_slot = jnp.min(jnp.where(hit, sub, BLK - 1), axis=0, keepdims=True)
    label_of_slot = jnp.min(jnp.where(hit, lax.rem(posv, BLK), BLK), axis=0, keepdims=True)
    idxv[0] = jnp.broadcast_to(row_of_slot, (8, CH))
    idxv[1] = jnp.minimum(slot_of_row, 2 * n_dev - 1)
    labels[0] = label_of_slot
    to_scalars = pltpu.make_async_copy(idxv, idxs, sem_local.at[0])
    to_scalars.start()

    def pack_rims(rows, which):
        for h in range(RIM):
            rims[which, h] = rows[rim[h]]

    def halo_copies(which, table):
        result = []
        for q, where in enumerate(
            (
                dict(tile=lax.rem(tile + 1, n_tile)),
                dict(tile=lax.rem(tile + n_tile - 1, n_tile)),
                dict(dev=lax.rem(dev + 1, n_dev)),
                dict(dev=lax.rem(dev + n_dev - 1, n_dev)),
            )
        ):
            result.append(
                remote(
                    rims.at[which],
                    table.at[pl.ds(BLK + q * RIM, RIM)],
                    sem_halo_s.at[which, q],
                    sem_halo_r.at[which, q],
                    **where,
                )
            )
        return result

    def finish_halo(copies, table):
        for copy in copies:
            copy.wait()
        edges = (tile == 0, tile == n_tile - 1, dev == 0, dev == n_dev - 1)
        for q, edge in enumerate(edges):

            @pl.when(edge)
            def _(q=q):
                table[BLK + q * RIM : BLK + (q + 1) * RIM] = jnp.zeros((RIM, VOX, CH), BF16)

    for table in (tab_m, tab_c, tab_h, tab_p):
        table[BLK + 4 * RIM] = jnp.zeros((VOX, CH), BF16)
    load_rim.wait()
    load_cot.wait()
    tab_c[0:BLK] = cot[...]
    pack_rims(cot, 0)
    load_feat.wait()
    to_scalars.wait()

    rings = (ring_0, ring_1, ring_2, ring_3)
    for p, ring in enumerate(rings):
        ring[0:BLK] = feat[:, p * PLANE : (p + 1) * PLANE, :]
        ring[8 * BLK] = jnp.zeros((PLANE, CH), BF16)
    pos_lanes = jnp.zeros((1, CH), I32)
    for r in range(BLK):
        pos_lanes = jnp.where(lax.rem(lane[0:1], BLK) == r, pos[r], pos_lanes)
    z_labels[0] = pos_lanes

    y = lax.rem(dev, 4)
    z = dev // 4
    n_z = n_dev // 4

    def ring_copy(step, p, ahead):
        source = step - 1 if ahead else (9 - step) % 8
        target = step if ahead else 8 - step
        where = lax.rem(dev + (4 if ahead else n_dev - 4), n_dev)
        return remote(
            rings[p].at[pl.ds(source * BLK, BLK)],
            rings[p].at[pl.ds(target * BLK, BLK)],
            sem_ring_s.at[p],
            sem_ring_r.at[target, p],
            dev=where,
        )

    def ring_starts(step, p):
        if step < 4:
            return [ring_copy(step, p, True), ring_copy(step, p, False)]
        return [ring_copy(4, p, p < 2)]

    def ring_step(step):
        for p in range(4):
            arriving = ring_starts(step, p)
            leaving_now = ring_starts(step + 1, p)
            for copy in arriving:
                copy.wait_recv()
            for copy in leaving_now:
                copy.start()

    pl.semaphore_wait(barrier, n_dev + n_tile - 2)

    for k in range(1, n_z):
        where = lax.rem(dev + 4 * k, n_dev)
        remote(z_labels.at[0], z_labels.at[k], sem_z_lab.at[0], sem_z_lab.at[1], dev=where).start()
    for p in range(4):
        for copy in ring_starts(1, p):
            copy.start()
    halo_c = halo_copies(0, tab_c)
    for copy in halo_c:
        copy.start()

    @pl.loop(1, n_dev)
    def _(d):
        where = lax.rem(dev + d, n_dev)
        remote(labels.at[0], labels.at[d], sem_lab.at[0], sem_lab.at[1], dev=where).start()

    def flip_weights(source, target):
        for o in range(27):
            piece = source[o * CH : (o + 1) * CH, :].astype(F32)
            target[(26 - o) * CH : (27 - o) * CH, :] = piece.T.astype(BF16)

    def expand(table, y):
        for b in range(BLK):
            near = planes.at[b % 2]
            for i in range(6):
                dx = 0 if i == 0 else (2 if i == 5 else 1)
                row = (i + EDGE - 1) % EDGE
                for t in range(9):
                    near[t * PLANE : (t + 1) * PLANE, i * CH : (i + 1) * CH] = table[
                        nbr[b, dx * 9 + t], row * PLANE : (row + 1) * PLANE, :
                    ]
            moved = dot(smat[...], near[...]).astype(BF16)
            for i in range(6):
                for t in range(9):
                    y[b, i, :, t * CH : (t + 1) * CH] = moved[
                        t * PLANE : (t + 1) * PLANE, i * CH : (i + 1) * CH
                    ]

    def columns(y, kx):
        return y[:, kx : kx + EDGE].reshape(BLK * VOX, 9 * CH)

    def conv(y, w):
        return (
            dot(columns(y, 0), w[0 : 9 * CH, :])
            + dot(columns(y, 1), w[9 * CH : 18 * CH, :])
            + dot(columns(y, 2), w[18 * CH : 27 * CH, :])
        )

    load_w2.wait()
    flip_weights(w2, wt2)
    load_w1.wait()
    flip_weights(w1, wt1)
    load_smat.wait()
    load_nbr.wait()
    ring_step(1)
    finish_halo(halo_c, tab_c)
    expand(tab_c, y_c)
    ring_step(2)
    hidden_grad[...] = conv(y_c, wt2)
    await_bytes(z_labels.at[pl.ds(1, n_z - 1)], sem_z_lab.at[1])
    z_pos = jnp.full((8, CH), -1, I32)
    for k in range(n_z):
        z_pos = jnp.where(lane // BLK == k, z_labels[k], z_pos)
    for dy in range(4):
        wanted = (z * 4 + lax.rem(y + dy, 4)) * BLK + sub
        found = jnp.min(jnp.where(z_pos == wanted, lane, 8 * BLK), axis=1, keepdims=True)
        z_slotv[dy] = jnp.broadcast_to(found, (8, CH))
    to_z_slots = pltpu.make_async_copy(z_slotv, z_slots, sem_local.at[0])
    to_z_slots.start()
    to_z_slots.wait()
    ring_step(3)

    def y_copy(p, dy):
        where = dict(dev=z * 4 + lax.rem(y + dy, 4))
        return remote(y_send.at[p, dy], y_got.at[p, dy - 1], sem_y.at[0, p], sem_y.at[1, p], **where)

    for p in (0, 2, 1, 3):
        for copy in ring_starts(4, p):
            copy.wait_recv()
        for dy in (2, 1, 3, 0):
            for s in range(BLK):
                y_send[p, dy, s] = rings[p][z_slots[dy, s, 0]]
            if dy:
                y_copy(p, dy).start()
    for p in (0, 2, 1, 3):
        await_bytes(y_got.at[p], sem_y.at[1, p])
        rows = y_send[p, 0].astype(F32)
        for dy in range(3):
            rows = rows + y_got[p, dy].astype(F32)
        own[0, :, p * PLANE : (p + 1) * PLANE, :] = rows.astype(BF16)
    tab_m[0:BLK] = own[0]
    pack_rims(own.at[0], 1)
    halo_m = halo_copies(1, tab_m)
    for copy in halo_m:
        copy.start()
    await_bytes(labels.at[pl.ds(1, n_dev - 1)], sem_lab.at[1])
    label_at = jnp.zeros((8, CH), I32)
    for d in range(n_dev):
        label_at = jnp.where(lane // 2 == d, labels[d], label_at)
    slotv[0] = jnp.minimum(label_at, BLK - 1)
    to_slots = pltpu.make_async_copy(slotv, slots, sem_local.at[0])
    to_slots.start()
    to_slots.wait()
    finish_halo(halo_m, tab_m)
    expand(tab_m, y_m)
    pre = conv(y_m, w1)
    gate = jax.nn.sigmoid(pre)
    hidden = (pre * gate).astype(BF16)
    pre_grad = (hidden_grad[...] * gate * (1.0 + pre * (1.0 - gate))).astype(BF16)
    tab_h[0:BLK] = hidden.reshape(BLK, VOX, CH)
    tab_p[0:BLK] = pre_grad.reshape(BLK, VOX, CH)
    own[1] = hidden.reshape(BLK, VOX, CH)
    own[2] = pre_grad.reshape(BLK, VOX, CH)
    pack_rims(own.at[1], 2)
    pack_rims(own.at[2], 3)
    halo_h = halo_copies(2, tab_h)
    halo_p = halo_copies(3, tab_p)
    for copy in halo_h + halo_p:
        copy.start()

    partner = dict(tile=tile + 1 - 2 * core)

    def core_copy(q, chunk):
        start = pl.multiple_of((1 - core) * HALF + chunk * QUARTER, 16)
        return remote(
            grads.at[q, pl.ds(start, QUARTER)],
            core_in.at[q, chunk],
            sem_sum_s.at[q, 0],
            sem_core.at[q, chunk],
            **partner,
        )

    dims = (("x", "y"), ("y", "x"))
    place = dict(x=chip_x, y=y)

    def start_core(q):
        for e in (2, 1, 3, 0):
            core_copy(q, lax.rem(place[dims[q][0]] + e, 4)).start()

    hidden_t = own[1].reshape(BLK * VOX, CH).astype(F32).T.astype(BF16)
    for kx in range(3):
        part = dot(hidden_t, columns(y_c, kx))
        for t in range(9):
            o = 26 - (kx * 9 + t)
            grads[1, o * CH : (o + 1) * CH, :] = part[:, t * CH : (t + 1) * CH]
    start_core(1)
    pre_grad_t = own[2].reshape(BLK * VOX, CH).astype(F32).T.astype(BF16)
    for kx in range(3):
        part = dot(pre_grad_t, columns(y_m, kx))
        for t in range(9):
            o = kx * 9 + t
            grads[0, o * CH : (o + 1) * CH, :] = part[:, t * CH : (t + 1) * CH].T
    start_core(0)

    def peer(dim, e):
        if dim == "x":
            other = lax.rem(chip_x + e, n_x)
            return other, dict(tile=other * 2 + core)
        if dim == "y":
            other = lax.rem(y + e, 4)
            return other, dict(dev=z * 4 + other)
        other = lax.rem(z + e, n_z)
        return other, dict(dev=other * 4 + y)

    def sem(q, stage):
        return sem_sum_s.at[q, stage], sem_sum_r.at[q, stage]

    def both_cores(q, chunk):
        start = pl.multiple_of(core * HALF + chunk * QUARTER, 16)
        return grads[q, pl.ds(start, QUARTER), :] + core_in[q, chunk]

    def start_first(q):
        for e in (2, 1, 3):
            other, where = peer(dims[q][0], e)
            core_copy(q, other).wait_recv()
            x_out[q, other] = both_cores(q, other).astype(BF16)
            remote(x_out.at[q, other], x_in.at[q, e - 1], *sem(q, 1), **where).start()
        core_copy(q, place[dims[q][0]]).wait_recv()

    def start_second(q):
        await_bytes(x_in.at[q], sem_sum_r.at[q, 1])
        total = both_cores(q, place[dims[q][0]])
        for e in range(3):
            total = total + x_in[q, e].astype(F32)
        own_sum[q, 0:QUARTER] = total
        own_sum[q, QUARTER:] = jnp.zeros((4 * PIECE - QUARTER, CH), F32)
        for j in range(4):
            y_out[q, j] = own_sum[q, j * PIECE : (j + 1) * PIECE].astype(BF16)
        for e in (2, 1, 3):
            other, where = peer(dims[q][1], e)
            remote(y_out.at[q, other], y_in.at[q, e - 1], *sem(q, 2), **where).start()

    def start_third(q):
        await_bytes(y_in.at[q], sem_sum_r.at[q, 2])
        start = pl.multiple_of(place[dims[q][1]] * PIECE, 16)
        total = own_sum[q, pl.ds(start, PIECE), :]
        for e in range(3):
            total = total + y_in[q, e].astype(F32)
        z_out[q, 0:7] = total.reshape(7, 16, CH)
        z_out[q, 7] = jnp.zeros((16, CH), F32)
        for e in (4, 3, 5, 2, 6, 1, 7):
            other, where = peer("z", e)
            remote(z_out.at[q, other], z_in.at[q, e - 1], *sem(q, 3), **where).start()

    def start_gather_third(q):
        await_bytes(z_in.at[q], sem_sum_r.at[q, 3])
        total = z_out[q, z]
        for e in range(7):
            total = total + z_in[q, e]
        mine = final.at[q, core, place[dims[q][0]], place[dims[q][1]], z]
        mine[...] = (total * scale).astype(BF16)
        for e in (4, 3, 5, 2, 6, 1, 7):
            _, where = peer("z", e)
            remote(mine, mine, *sem(q, 4), **where).start()

    def start_gather_second(q):
        await_bytes(final.at[q, core, 0, 0, pl.ds(0, 7)], sem_sum_r.at[q, 4])
        mine = final.at[q, core, place[dims[q][0]], place[dims[q][1]], pl.ds(0, 7)]
        for e in (2, 1, 3):
            _, where = peer(dims[q][1], e)
            remote(mine, mine, *sem(q, 5), **where).start()

    def gather_core_copy(q, chunk):
        piece = final.at[q, core, chunk, :, pl.ds(0, 7)]
        return remote(piece, piece, *sem(q, 7), **partner)

    def exit_copy(q, chunk):
        return pltpu.make_async_copy(
            final.at[q, core, chunk], out_sums.at[q, core, chunk], sem_out.at[q, chunk]
        )

    def gather_first_copy(q, e):
        mine = final.at[q, core, place[dims[q][0]], :, pl.ds(0, 7)]
        _, where = peer(dims[q][0], e)
        return remote(mine, mine, sem_sum_s.at[q, 6], sem_first.at[q, e - 1], **where)

    def start_gather_first(q):
        await_bytes(final.at[q, core, 0, pl.ds(0, 3), pl.ds(0, 7)], sem_sum_r.at[q, 5])
        for e in (2, 1, 3):
            gather_first_copy(q, e).start()
        gather_core_copy(q, place[dims[q][0]]).start()
        exit_copy(q, place[dims[q][0]]).start()

    def start_gather_core(q):
        for e in (1, 3, 2):
            chunk = lax.rem(place[dims[q][0]] + 4 - e, 4)
            gather_first_copy(q, e).wait_recv()
            gather_core_copy(q, chunk).start()
            exit_copy(q, chunk).start()

    start_first(1)
    start_first(0)
    finish_halo(halo_h, tab_h)
    expand(tab_h, y_x)
    pre_two = conv(y_x, w2)
    leaving[0] = (
        (own[0].reshape(BLK * VOX, CH).astype(F32) + pre_two).astype(BF16).reshape(BLK, VOX, CH)
    )
    exit_output = pltpu.make_async_copy(leaving.at[0], out_output, sem_out.at[0, 5])
    exit_output.start()
    finish_halo(halo_p, tab_p)
    expand(tab_p, y_x)
    back = conv(y_x, wt1) + cot[...].reshape(BLK * VOX, CH).astype(F32)
    own[1] = back.astype(BF16).reshape(BLK, VOX, CH)

    @pl.loop(0, n_dev)
    def _(d):
        for c in range(2):
            repacked[d, c] = own[1, slots[0, 0, 2 * d + c]]

    returned[0] = repacked[0]

    order = [7 * i % n_dev for i in range(1, n_dev)]

    def send_back(offsets):
        for d in offsets:
            where = lax.rem(dev - d + n_dev, n_dev)
            remote(repacked.at[d], returned.at[d], sem_back.at[0], sem_back.at[1], dev=where).start()

    for stage, offsets in (
        (start_second, order[0:6]),
        (start_third, order[6:12]),
        (start_gather_third, order[12:18]),
        (start_gather_second, order[18:24]),
        (start_gather_first, order[24:]),
        (start_gather_core, []),
    ):
        stage(1)
        stage(0)
        send_back(offsets)
    await_bytes(returned.at[pl.ds(1, n_dev - 1)], sem_back.at[1])
    for r in range(BLK):
        linear = idxs[1, r, 0]
        leaving[1, r] = returned[linear // 2, lax.rem(linear, 2)]
    exit_grad = pltpu.make_async_copy(leaving.at[1], out_grad, sem_out.at[1, 5])
    exit_grad.start()

    await_bytes(labels.at[pl.ds(1, n_dev - 1)], sem_lab.at[0])
    await_bytes(z_labels.at[pl.ds(1, n_z - 1)], sem_z_lab.at[0])
    for p in range(4):
        await_bytes(rings[p].at[pl.ds(0, 7 * BLK)], sem_ring_s.at[p])
        await_bytes(y_got.at[p], sem_y.at[0, p])
    await_bytes(repacked.at[pl.ds(1, n_dev - 1)], sem_back.at[0])
    for q in (1, 0):
        await_bytes(final.at[q, 1 - core, :, :, pl.ds(0, 7)], sem_sum_r.at[q, 7])
        pltpu.make_async_copy(
            final.at[q, 1 - core], out_sums.at[q, 1 - core], sem_out.at[q, 4]
        ).start()
    for q in range(2):
        await_bytes(core_in.at[q], sem_sum_s.at[q, 0])
        await_bytes(x_in.at[q], sem_sum_s.at[q, 1])
        await_bytes(y_in.at[q], sem_sum_s.at[q, 2])
        await_bytes(z_in.at[q], sem_sum_s.at[q, 3])
        await_bytes(final.at[q, core, 0, 0, pl.ds(0, 7)], sem_sum_s.at[q, 4])
        await_bytes(final.at[q, core, 0, pl.ds(0, 3), pl.ds(0, 7)], sem_sum_s.at[q, 5])
        await_bytes(final.at[q, core, pl.ds(0, 3), :, pl.ds(0, 7)], sem_sum_s.at[q, 6])
        await_bytes(final.at[q, core, :, :, pl.ds(0, 7)], sem_sum_s.at[q, 7])
        for chunk in range(4):
            exit_copy(q, chunk).wait()
        pltpu.make_async_copy(
            final.at[q, 1 - core], out_sums.at[q, 1 - core], sem_out.at[q, 4]
        ).wait()
    exit_output.wait()
    exit_grad.wait()


def finish_kernel(
    sums, output_in, grad_in, output, grad, grad_one, grad_two, rows_held, held, wide, sem_load, sem_store, sem_pass
):
    passes = [
        pltpu.make_async_copy(output_in, rows_held.at[0], sem_pass.at[0]),
        pltpu.make_async_copy(grad_in, rows_held.at[1], sem_pass.at[1]),
    ]
    parts = [(q, c, j) for c in range(2) for j in range(4) for q in range(2)]
    loads = [pltpu.make_async_copy(sums.at[part], held.at[part], sem_load.at[part]) for part in parts]
    for copy in passes + loads:
        copy.start()
    stores = [
        pltpu.make_async_copy(rows_held.at[0], output, sem_pass.at[2]),
        pltpu.make_async_copy(rows_held.at[1], grad, sem_pass.at[3]),
    ]
    for copy, store in zip(passes, stores):
        copy.wait()
        store.start()
    for part, load in zip(parts, loads):
        q, c, j = part
        load.wait()
        rows = held[q, c, j, :, 0:7].reshape(4 * PIECE, CH)
        wide[q, c, j] = rows[0:QUARTER].astype(F32)
        target = (grad_one, grad_two)[q].at[pl.ds(c * HALF + j * QUARTER, QUARTER)]
        stores.append(pltpu.make_async_copy(wide.at[part], target, sem_store.at[part]))
        stores[-1].start()
    for copy in stores:
        copy.wait()


def per_device(
    n_tile, n_dev, features, morton_pos, neighbours, rim, cotangent, weight_one, weight_two
):
    blocks, voxels, channels = features.shape
    scale = 1.0 / math.sqrt(blocks * voxels * n_tile * n_dev)
    n_x = n_tile // 2
    hbm = pl.BlockSpec(memory_space=pltpu.HBM)
    dma = pltpu.SemaphoreType.DMA
    block_table = pltpu.VMEM((BLK + 4 * RIM + 1, VOX, CH), BF16)
    wide = pltpu.VMEM((BLK, 6, PLANE, 9 * CH), BF16)
    flat = pltpu.VMEM((BLK * VOX, CH), F32)
    ring = pltpu.VMEM((9 * BLK, PLANE, CH), BF16)
    slab = pltpu.VMEM((n_dev, 2, VOX, CH), BF16)
    output, input_grad, sums = pl.pallas_call(
        functools.partial(unit_kernel, n_tile, n_dev, scale),
        out_shape=(
            jax.ShapeDtypeStruct(features.shape, BF16),
            jax.ShapeDtypeStruct(features.shape, BF16),
            jax.ShapeDtypeStruct((2, 2, 4, 4, 8, 16, CH), BF16),
        ),
        in_specs=[hbm] * 8,
        out_specs=(hbm, hbm, hbm),
        scratch_shapes=[
            pltpu.SMEM(morton_pos.shape, I32),
            pltpu.SMEM(neighbours.shape, I32),
            pltpu.SMEM(rim.shape, I32),
            pltpu.VMEM(features.shape, BF16),
            pltpu.VMEM(cotangent.shape, BF16),
            pltpu.VMEM(weight_one.shape, BF16),
            pltpu.VMEM(weight_two.shape, BF16),
            pltpu.VMEM((9 * PLANE, 9 * PLANE), BF16),
            pltpu.VMEM((2, 8, CH), I32),
            pltpu.SMEM((2, 8, CH), I32),
            pltpu.VMEM((2, 8, CH), I32),
            pltpu.SMEM((2, 8, CH), I32),
            pltpu.VMEM((n_dev, 1, CH), I32),
            pltpu.VMEM((8, 1, CH), I32),
            pltpu.VMEM((4, 8, CH), I32),
            pltpu.SMEM((4, 8, CH), I32),
            ring,
            ring,
            ring,
            ring,
            pltpu.VMEM((4, 4, BLK, PLANE, CH), BF16),
            pltpu.VMEM((4, 3, BLK, PLANE, CH), BF16),
            slab,
            slab,
            block_table,
            block_table,
            block_table,
            block_table,
            pltpu.VMEM((3, BLK, VOX, CH), BF16),
            pltpu.VMEM((2, BLK, VOX, CH), BF16),
            pltpu.VMEM((4, RIM, VOX, CH), BF16),
            pltpu.VMEM((27 * CH, CH), BF16),
            pltpu.VMEM((27 * CH, CH), BF16),
            pltpu.VMEM((2, 9 * PLANE, 6 * CH), BF16),
            wide,
            wide,
            wide,
            flat,
            flat,
            pltpu.VMEM((2, 27 * CH, CH), F32),
            pltpu.VMEM((2, 4, QUARTER, CH), F32),
            pltpu.VMEM((2, 4, QUARTER, CH), BF16),
            pltpu.VMEM((2, 3, QUARTER, CH), BF16),
            pltpu.VMEM((2, 4, PIECE, CH), BF16),
            pltpu.VMEM((2, 3, PIECE, CH), BF16),
            pltpu.VMEM((2, 4 * PIECE, CH), F32),
            pltpu.VMEM((2, 8, 16, CH), F32),
            pltpu.VMEM((2, 7, 16, CH), F32),
            pltpu.VMEM((2, 2, 4, 4, 8, 16, CH), BF16),
            dma((8,)),
            dma((1,)),
            dma((4,)),
            dma((8, 4)),
            dma((2, 4)),
            dma((2,)),
            dma((2,)),
            dma((2,)),
            dma((4, 4)),
            dma((4, 4)),
            dma((2, 8)),
            dma((2, 8)),
            dma((2, 3)),
            dma((2, 4)),
            dma((2, 6)),
        ],
        compiler_params=pltpu.CompilerParams(
            collective_id=0, has_side_effects=True, vmem_limit_bytes=62 * 1024 * 1024
        ),
    )(
        morton_pos,
        neighbours,
        rim,
        features,
        cotangent,
        weight_one,
        weight_two,
        jnp.asarray(shift_matrix(), BF16),
    )
    kernel_shape = jax.ShapeDtypeStruct(weight_one.shape, F32)
    return pl.pallas_call(
        finish_kernel,
        out_shape=(
            jax.ShapeDtypeStruct(features.shape, BF16),
            jax.ShapeDtypeStruct(features.shape, BF16),
            kernel_shape,
            kernel_shape,
        ),
        in_specs=[hbm] * 3,
        out_specs=(hbm,) * 4,
        scratch_shapes=[
            pltpu.VMEM((2,) + features.shape, BF16),
            pltpu.VMEM((2, 2, 4, 4, 8, 16, CH), BF16),
            pltpu.VMEM((2, 2, 4, QUARTER, CH), F32),
            dma((2, 2, 4)),
            dma((2, 2, 4)),
            dma((4,)),
        ],
        compiler_params=pltpu.CompilerParams(vmem_limit_bytes=62 * 1024 * 1024),
    )(sums, output, input_grad)


def solution(mesh):
    placed = (
        P(("tile", "dev"), None, None),
        P(("tile", "dev")),
        P(("tile", "dev"), None),
        P(("tile", "dev")),
        P(("tile", "dev"), None, None),
        P(),
        P(),
    )
    return jax.shard_map(
        functools.partial(per_device, mesh.shape["tile"], mesh.shape["dev"]),
        mesh=mesh,
        in_specs=placed,
        out_specs=(P(("tile", "dev"), None, None), P(("tile", "dev"), None, None), P(), P()),
        check_vma=False,
    )
```

```python
import functools
import math

import jax
import jax.numpy as jnp
import numpy as np
from jax import lax
from jax.experimental import pallas as pl
from jax.experimental.pallas import tpu as pltpu
from jax.sharding import PartitionSpec as P

EDGE = 4
PLANE = EDGE * EDGE
BLK = 8
VOX = 64
CH = 128
RIM = 4
HALF = 27 * CH // 2
QUARTER = HALF // 4
TILES = QUARTER // 16
PIECE = 7 * 16
F32 = jnp.float32
BF16 = jnp.bfloat16
I32 = jnp.int32


def shift_matrix():
    result = np.zeros((9 * PLANE, 9 * PLANE), np.float32)
    for ky in range(3):
        for kz in range(3):
            for j in range(EDGE):
                for k in range(EDGE):
                    y, z = j + ky - 1, k + kz - 1
                    dy, dz = y // EDGE + 1, z // EDGE + 1
                    source = ((dy * 3 + dz) * EDGE + y % EDGE) * EDGE + z % EDGE
                    result[((ky * 3 + kz) * EDGE + j) * EDGE + k, source] = 1.0
    return result


def dot(left, right):
    return jnp.dot(left, right, preferred_element_type=F32)


def unit_kernel(
    n_tile,
    n_dev,
    scale,
    pos_in,
    nbr_in,
    rim_in,
    feat_in,
    cot_in,
    w1_in,
    w2_in,
    smat_in,
    out_output,
    out_grad,
    out_sums,
    pos,
    nbr,
    rim,
    feat,
    cot,
    w1,
    w2,
    smat,
    idxv,
    idxs,
    slotv,
    slots,
    labels,
    z_labels,
    z_slotv,
    z_slots,
    ring_0,
    ring_1,
    ring_2,
    ring_3,
    y_send,
    y_got,
    repacked,
    returned,
    tab_m,
    tab_c,
    tab_h,
    tab_p,
    own,
    leaving,
    rims,
    wt1,
    wt2,
    planes,
    y_m,
    y_c,
    y_x,
    pre_one,
    hidden_grad,
    grads,
    core_in,
    x_out,
    x_in,
    y_out,
    y_in,
    own_sum,
    z_out,
    z_in,
    final,
    sem_in,
    sem_local,
    sem_ring_s,
    sem_ring_r,
    sem_y,
    sem_z_lab,
    sem_lab,
    sem_back,
    sem_halo_s,
    sem_halo_r,
    sem_sum_s,
    sem_sum_r,
    sem_first,
    sem_core,
    sem_out,
):
    tile = lax.axis_index("tile")
    dev = lax.axis_index("dev")
    core = lax.rem(tile, 2)
    chip_x = tile // 2
    n_x = n_tile // 2

    def remote(src, dst, send, recv, **where):
        return pltpu.make_async_remote_copy(
            src_ref=src,
            dst_ref=dst,
            send_sem=send,
            recv_sem=recv,
            device_id=where,
            device_id_type=pl.DeviceIdType.MESH,
        )

    def await_bytes(ref, sem):
        pltpu.make_async_copy(ref, ref, sem).wait()

    operands = (pos_in, rim_in, feat_in, cot_in, w2_in, w1_in, smat_in, nbr_in)
    places = (pos, rim, feat, cot, w2, w1, smat, nbr)
    loads = [
        pltpu.make_async_copy(source, place, sem_in.at[i])
        for i, (source, place) in enumerate(zip(operands, places))
    ]
    load_pos, load_rim, load_feat, load_cot, load_w2, load_w1, load_smat, load_nbr = loads
    for load in loads:
        load.start()
    for table in (tab_m, tab_c, tab_h, tab_p):
        table[BLK + 2 * RIM :] = jnp.zeros((2 * RIM + 1, EDGE, PLANE, CH), BF16)
    barrier = pltpu.get_barrier_semaphore()

    @pl.loop(1, n_dev)
    def _(d):
        pl.semaphore_signal(barrier, inc=1, device_id={"dev": lax.rem(dev + d, n_dev)})

    @pl.loop(1, n_tile)
    def _(d):
        pl.semaphore_signal(barrier, inc=1, device_id={"tile": lax.rem(tile + d, n_tile)})

    sub = lax.broadcasted_iota(I32, (8, CH), 0)
    lane = lax.broadcasted_iota(I32, (8, CH), 1)
    load_pos.wait()
    posv = jnp.zeros((8, CH), I32)
    for r in range(BLK):
        posv = jnp.where(sub == r, pos[r], posv)
    owner = posv // BLK
    count = jnp.zeros((8, CH), I32)
    for r in range(BLK):
        count = count + jnp.where((owner == pos[r] // BLK) & (sub > r), 1, 0)
    slot_of_row = lax.rem(owner - dev + n_dev, n_dev) * 2 + count
    hit = lane == slot_of_row
    row_of_slot = jnp.min(jnp.where(hit, sub, BLK - 1), axis=0, keepdims=True)
    label_of_slot = jnp.min(jnp.where(hit, lax.rem(posv, BLK), BLK), axis=0, keepdims=True)
    idxv[0] = jnp.broadcast_to(row_of_slot, (8, CH))
    idxv[1] = jnp.minimum(slot_of_row, 2 * n_dev - 1)
    labels[0] = label_of_slot
    to_scalars = pltpu.make_async_copy(idxv, idxs, sem_local.at[0])
    to_scalars.start()

    def pack_rims(rows, which):
        for h in range(RIM):
            rims[which, h] = rows[rim[h]].reshape(EDGE, PLANE, CH)

    def halo_copies(which, table):
        result = []
        every, low, high = slice(None), pl.ds(0, PLANE // 2), pl.ds(PLANE // 2, PLANE // 2)
        for q, (where, part) in enumerate(
            (
                (dict(tile=lax.rem(tile + 1, n_tile)), (pl.ds(EDGE - 1, 1), every)),
                (dict(tile=lax.rem(tile + n_tile - 1, n_tile)), (pl.ds(0, 1), every)),
                (dict(dev=lax.rem(dev + 1, n_dev)), (every, high)),
                (dict(dev=lax.rem(dev + n_dev - 1, n_dev)), (every, low)),
            )
        ):
            result.append(
                remote(
                    rims.at[(which, every) + part],
                    table.at[(pl.ds(BLK + q * RIM, RIM),) + part],
                    sem_halo_s.at[which, q],
                    sem_halo_r.at[which, q],
                    **where,
                )
            )
        return result

    def finish_halo(copies, table):
        for copy in copies:
            copy.wait()
        edges = (tile == 0, tile == n_tile - 1, dev == 0, dev == n_dev - 1)
        for q, edge in enumerate(edges):

            @pl.when(edge)
            def _(q=q):
                table[BLK + q * RIM : BLK + (q + 1) * RIM] = jnp.zeros((RIM, EDGE, PLANE, CH), BF16)

    load_rim.wait()
    load_cot.wait()
    tab_c[0:BLK] = cot[...].reshape(BLK, EDGE, PLANE, CH)
    pack_rims(cot, 0)
    load_feat.wait()
    to_scalars.wait()

    rings = (ring_0, ring_1, ring_2, ring_3)
    for p, ring in enumerate(rings):
        ring[0:BLK] = feat[:, p * PLANE : (p + 1) * PLANE, :]
        ring[8 * BLK] = jnp.zeros((PLANE, CH), BF16)
    pos_lanes = jnp.zeros((1, CH), I32)
    for r in range(BLK):
        pos_lanes = jnp.where(lax.rem(lane[0:1], BLK) == r, pos[r], pos_lanes)
    z_labels[0] = pos_lanes

    y = lax.rem(dev, 4)
    z = dev // 4
    n_z = n_dev // 4

    def ring_copy(step, p, ahead):
        source = step - 1 if ahead else (9 - step) % 8
        target = step if ahead else 8 - step
        where = lax.rem(dev + (4 if ahead else n_dev - 4), n_dev)
        return remote(
            rings[p].at[pl.ds(source * BLK, BLK)],
            rings[p].at[pl.ds(target * BLK, BLK)],
            sem_ring_s.at[p],
            sem_ring_r.at[target, p],
            dev=where,
        )

    def ring_starts(step, p):
        if step < 4:
            return [ring_copy(step, p, True), ring_copy(step, p, False)]
        return [ring_copy(4, p, p < 2)]

    def ring_step(step):
        for p in range(4):
            arriving = ring_starts(step, p)
            leaving_now = ring_starts(step + 1, p)
            for copy in arriving:
                copy.wait_recv()
            for copy in leaving_now:
                copy.start()

    pl.semaphore_wait(barrier, n_dev + n_tile - 2)

    for k in range(1, n_z):
        where = lax.rem(dev + 4 * k, n_dev)
        remote(z_labels.at[0], z_labels.at[k], sem_z_lab.at[0], sem_z_lab.at[1], dev=where).start()
    for p in range(4):
        for copy in ring_starts(1, p):
            copy.start()
    halo_c = halo_copies(0, tab_c)
    for copy in halo_c:
        copy.start()

    @pl.loop(1, n_dev)
    def _(d):
        where = lax.rem(dev + d, n_dev)
        remote(labels.at[0], labels.at[d], sem_lab.at[0], sem_lab.at[1], dev=where).start()

    def flip_weights(source, target):
        for o in range(27):
            piece = source[o * CH : (o + 1) * CH, :].astype(F32)
            target[(26 - o) * CH : (27 - o) * CH, :] = piece.T.astype(BF16)

    def expand(table, y):
        for b in range(BLK):
            near = planes.at[b % 2]
            for i in range(6):
                dx = 0 if i == 0 else (2 if i == 5 else 1)
                row = (i + EDGE - 1) % EDGE
                for t in range(9):
                    near[t * PLANE : (t + 1) * PLANE, i * CH : (i + 1) * CH] = table[
                        nbr[b, dx * 9 + t], row
                    ]
            moved = dot(smat[...], near[...]).astype(BF16)
            for i in range(6):
                for t in range(9):
                    y[b, i, :, t * CH : (t + 1) * CH] = moved[
                        t * PLANE : (t + 1) * PLANE, i * CH : (i + 1) * CH
                    ]

    def columns(y, kx):
        return y[:, kx : kx + EDGE].reshape(BLK * VOX, 9 * CH)

    def conv(y, w):
        return (
            dot(columns(y, 0), w[0 : 9 * CH, :])
            + dot(columns(y, 1), w[9 * CH : 18 * CH, :])
            + dot(columns(y, 2), w[18 * CH : 27 * CH, :])
        )

    load_w2.wait()
    flip_weights(w2, wt2)
    load_w1.wait()
    flip_weights(w1, wt1)
    load_smat.wait()
    load_nbr.wait()
    ring_step(1)
    finish_halo(halo_c, tab_c)
    expand(tab_c, y_c)
    ring_step(2)
    hidden_grad[...] = conv(y_c, wt2)
    await_bytes(z_labels.at[pl.ds(1, n_z - 1)], sem_z_lab.at[1])
    z_pos = jnp.full((8, CH), -1, I32)
    for k in range(n_z):
        z_pos = jnp.where(lane // BLK == k, z_labels[k], z_pos)
    for dy in range(4):
        wanted = (z * 4 + lax.rem(y + dy, 4)) * BLK + sub
        found = jnp.min(jnp.where(z_pos == wanted, lane, 8 * BLK), axis=1, keepdims=True)
        z_slotv[dy] = jnp.broadcast_to(found, (8, CH))
    to_z_slots = pltpu.make_async_copy(z_slotv, z_slots, sem_local.at[0])
    to_z_slots.start()
    to_z_slots.wait()
    ring_step(3)

    def y_copy(p, dy):
        where = dict(dev=z * 4 + lax.rem(y + dy, 4))
        return remote(y_send.at[p, dy], y_got.at[p, dy - 1], sem_y.at[0, p], sem_y.at[1, p], **where)

    for p in (0, 2, 1, 3):
        for copy in ring_starts(4, p):
            copy.wait_recv()
        for dy in (2, 1, 3, 0):
            for s in range(BLK):
                y_send[p, dy, s] = rings[p][z_slots[dy, s, 0]]
            if dy:
                y_copy(p, dy).start()
    for p in (0, 2, 1, 3):
        await_bytes(y_got.at[p], sem_y.at[1, p])
        rows = y_send[p, 0].astype(F32)
        for dy in range(3):
            rows = rows + y_got[p, dy].astype(F32)
        own[0, :, p * PLANE : (p + 1) * PLANE, :] = rows.astype(BF16)
    tab_m[0:BLK] = own[0].reshape(BLK, EDGE, PLANE, CH)
    pack_rims(own.at[0], 1)
    halo_m = halo_copies(1, tab_m)
    for copy in halo_m:
        copy.start()
    await_bytes(labels.at[pl.ds(1, n_dev - 1)], sem_lab.at[1])
    label_at = jnp.zeros((8, CH), I32)
    for d in range(n_dev):
        label_at = jnp.where(lane // 2 == d, labels[d], label_at)
    slotv[0] = jnp.minimum(label_at, BLK - 1)
    to_slots = pltpu.make_async_copy(slotv, slots, sem_local.at[0])
    to_slots.start()
    to_slots.wait()
    finish_halo(halo_m, tab_m)
    expand(tab_m, y_m)
    pre = conv(y_m, w1)
    gate = jax.nn.sigmoid(pre)
    hidden = (pre * gate).astype(BF16)
    pre_grad = (hidden_grad[...] * gate * (1.0 + pre * (1.0 - gate))).astype(BF16)
    tab_h[0:BLK] = hidden.reshape(BLK, EDGE, PLANE, CH)
    tab_p[0:BLK] = pre_grad.reshape(BLK, EDGE, PLANE, CH)
    own[1] = hidden.reshape(BLK, VOX, CH)
    own[2] = pre_grad.reshape(BLK, VOX, CH)
    pack_rims(own.at[1], 2)
    pack_rims(own.at[2], 3)
    halo_h = halo_copies(2, tab_h)
    halo_p = halo_copies(3, tab_p)
    for copy in halo_h + halo_p:
        copy.start()

    partner = dict(tile=tile + 1 - 2 * core)

    def core_copy(q, chunk):
        start = pl.multiple_of((1 - core) * HALF + chunk * QUARTER, 16)
        return remote(
            grads.at[q, pl.ds(start, QUARTER)],
            core_in.at[q, chunk],
            sem_sum_s.at[q, 0],
            sem_core.at[q, chunk],
            **partner,
        )

    dims = (("x", "y"), ("y", "x"))
    place = dict(x=chip_x, y=y)

    def start_core(q):
        for e in (2, 1, 3, 0):
            core_copy(q, lax.rem(place[dims[q][0]] + e, 4)).start()

    hidden_t = own[1].reshape(BLK * VOX, CH).astype(F32).T.astype(BF16)
    for kx in range(3):
        part = dot(hidden_t, columns(y_c, kx))
        for t in range(9):
            o = 26 - (kx * 9 + t)
            grads[1, o * CH : (o + 1) * CH, :] = part[:, t * CH : (t + 1) * CH]
    start_core(1)
    pre_grad_t = own[2].reshape(BLK * VOX, CH).astype(F32).T.astype(BF16)
    for kx in range(3):
        part = dot(pre_grad_t, columns(y_m, kx))
        for t in range(9):
            o = kx * 9 + t
            grads[0, o * CH : (o + 1) * CH, :] = part[:, t * CH : (t + 1) * CH].T
    start_core(0)

    def peer(dim, e):
        if dim == "x":
            other = lax.rem(chip_x + e, n_x)
            return other, dict(tile=other * 2 + core)
        if dim == "y":
            other = lax.rem(y + e, 4)
            return other, dict(dev=z * 4 + other)
        other = lax.rem(z + e, n_z)
        return other, dict(dev=other * 4 + y)

    def sem(q, stage):
        return sem_sum_s.at[q, stage], sem_sum_r.at[q, stage]

    def both_cores(q, chunk):
        start = pl.multiple_of(core * HALF + chunk * QUARTER, 16)
        return grads[q, pl.ds(start, QUARTER), :] + core_in[q, chunk]

    def start_first(q):
        for e in (2, 1, 3):
            other, where = peer(dims[q][0], e)
            core_copy(q, other).wait_recv()
            x_out[q, other] = both_cores(q, other).astype(BF16)
            remote(x_out.at[q, other], x_in.at[q, e - 1], *sem(q, 1), **where).start()
        core_copy(q, place[dims[q][0]]).wait_recv()

    def start_second(q):
        await_bytes(x_in.at[q], sem_sum_r.at[q, 1])
        total = both_cores(q, place[dims[q][0]])
        for e in range(3):
            total = total + x_in[q, e].astype(F32)
        own_sum[q, 0:QUARTER] = total
        own_sum[q, QUARTER:] = jnp.zeros((4 * PIECE - QUARTER, CH), F32)
        for j in range(4):
            y_out[q, j] = own_sum[q, j * PIECE : (j + 1) * PIECE].astype(BF16)
        for e in (2, 1, 3):
            other, where = peer(dims[q][1], e)
            remote(y_out.at[q, other], y_in.at[q, e - 1], *sem(q, 2), **where).start()

    def start_third(q):
        await_bytes(y_in.at[q], sem_sum_r.at[q, 2])
        start = pl.multiple_of(place[dims[q][1]] * PIECE, 16)
        total = own_sum[q, pl.ds(start, PIECE), :]
        for e in range(3):
            total = total + y_in[q, e].astype(F32)
        z_out[q, 0:7] = total.reshape(7, 16, CH)
        z_out[q, 7] = jnp.zeros((16, CH), F32)
        for e in (4, 3, 5, 2, 6, 1, 7):
            other, where = peer("z", e)
            remote(z_out.at[q, other], z_in.at[q, e - 1], *sem(q, 3), **where).start()

    def start_gather_third(q):
        await_bytes(z_in.at[q], sem_sum_r.at[q, 3])
        total = z_out[q, z]
        for e in range(7):
            total = total + z_in[q, e]
        mine = final.at[q, core, place[dims[q][0]], place[dims[q][1]], z]
        mine[...] = (total * scale).astype(BF16)
        for e in (4, 3, 5, 2, 6, 1, 7):
            _, where = peer("z", e)
            remote(mine, mine, *sem(q, 4), **where).start()

    def start_gather_second(q):
        await_bytes(final.at[q, core, 0, 0, pl.ds(0, 7)], sem_sum_r.at[q, 4])
        mine = final.at[q, core, place[dims[q][0]], place[dims[q][1]], pl.ds(0, 7)]
        for e in (2, 1, 3):
            _, where = peer(dims[q][1], e)
            remote(mine, mine, *sem(q, 5), **where).start()

    def gather_core_copy(q, chunk):
        piece = final.at[q, core, chunk, :, pl.ds(0, 7)]
        return remote(piece, piece, *sem(q, 7), **partner)

    def exit_copy(q, chunk):
        return pltpu.make_async_copy(
            final.at[q, core, chunk], out_sums.at[q, core, chunk], sem_out.at[q, chunk]
        )

    def gather_first_copy(q, e):
        mine = final.at[q, core, place[dims[q][0]], :, pl.ds(0, 7)]
        _, where = peer(dims[q][0], e)
        return remote(mine, mine, sem_sum_s.at[q, 6], sem_first.at[q, e - 1], **where)

    def start_gather_first(q):
        await_bytes(final.at[q, core, 0, pl.ds(0, 3), pl.ds(0, 7)], sem_sum_r.at[q, 5])
        for e in (2, 1, 3):
            gather_first_copy(q, e).start()
        gather_core_copy(q, place[dims[q][0]]).start()
        exit_copy(q, place[dims[q][0]]).start()

    def start_gather_core(q):
        for e in (1, 3, 2):
            chunk = lax.rem(place[dims[q][0]] + 4 - e, 4)
            gather_first_copy(q, e).wait_recv()
            gather_core_copy(q, chunk).start()
            exit_copy(q, chunk).start()

    start_first(1)
    start_first(0)
    finish_halo(halo_h, tab_h)
    expand(tab_h, y_x)
    pre_two = conv(y_x, w2)
    leaving[0] = (
        (own[0].reshape(BLK * VOX, CH).astype(F32) + pre_two).astype(BF16).reshape(BLK, VOX, CH)
    )
    exit_output = pltpu.make_async_copy(leaving.at[0], out_output, sem_out.at[0, 5])
    exit_output.start()
    finish_halo(halo_p, tab_p)
    expand(tab_p, y_x)
    back = conv(y_x, wt1) + cot[...].reshape(BLK * VOX, CH).astype(F32)
    own[1] = back.astype(BF16).reshape(BLK, VOX, CH)

    @pl.loop(0, n_dev)
    def _(d):
        for c in range(2):
            repacked[d, c] = own[1, slots[0, 0, 2 * d + c]]

    returned[0] = repacked[0]

    order = [7 * i % n_dev for i in range(1, n_dev)]

    def send_back(offsets):
        for d in offsets:
            where = lax.rem(dev - d + n_dev, n_dev)
            remote(repacked.at[d], returned.at[d], sem_back.at[0], sem_back.at[1], dev=where).start()

    for stage, offsets in (
        (start_second, order[0:6]),
        (start_third, order[6:12]),
        (start_gather_third, order[12:18]),
        (start_gather_second, order[18:24]),
        (start_gather_first, order[24:]),
        (start_gather_core, []),
    ):
        stage(1)
        stage(0)
        send_back(offsets)
    await_bytes(returned.at[pl.ds(1, n_dev - 1)], sem_back.at[1])
    for r in range(BLK):
        linear = idxs[1, r, 0]
        leaving[1, r] = returned[linear // 2, lax.rem(linear, 2)]
    exit_grad = pltpu.make_async_copy(leaving.at[1], out_grad, sem_out.at[1, 5])
    exit_grad.start()

    await_bytes(labels.at[pl.ds(1, n_dev - 1)], sem_lab.at[0])
    await_bytes(z_labels.at[pl.ds(1, n_z - 1)], sem_z_lab.at[0])
    for p in range(4):
        await_bytes(rings[p].at[pl.ds(0, 7 * BLK)], sem_ring_s.at[p])
        await_bytes(y_got.at[p], sem_y.at[0, p])
    await_bytes(repacked.at[pl.ds(1, n_dev - 1)], sem_back.at[0])
    for q in (1, 0):
        await_bytes(final.at[q, 1 - core, :, :, pl.ds(0, 7)], sem_sum_r.at[q, 7])
        pltpu.make_async_copy(
            final.at[q, 1 - core], out_sums.at[q, 1 - core], sem_out.at[q, 4]
        ).start()
    for q in range(2):
        await_bytes(core_in.at[q], sem_sum_s.at[q, 0])
        await_bytes(x_in.at[q], sem_sum_s.at[q, 1])
        await_bytes(y_in.at[q], sem_sum_s.at[q, 2])
        await_bytes(z_in.at[q], sem_sum_s.at[q, 3])
        await_bytes(final.at[q, core, 0, 0, pl.ds(0, 7)], sem_sum_s.at[q, 4])
        await_bytes(final.at[q, core, 0, pl.ds(0, 3), pl.ds(0, 7)], sem_sum_s.at[q, 5])
        await_bytes(final.at[q, core, pl.ds(0, 3), :, pl.ds(0, 7)], sem_sum_s.at[q, 6])
        await_bytes(final.at[q, core, :, :, pl.ds(0, 7)], sem_sum_s.at[q, 7])
        for chunk in range(4):
            exit_copy(q, chunk).wait()
        pltpu.make_async_copy(
            final.at[q, 1 - core], out_sums.at[q, 1 - core], sem_out.at[q, 4]
        ).wait()
    exit_output.wait()
    exit_grad.wait()


def finish_kernel(
    sums, output_in, grad_in, output, grad, grad_one, grad_two, rows_held, held, wide, sem_load, sem_store, sem_pass
):
    passes = [
        pltpu.make_async_copy(output_in, rows_held.at[0], sem_pass.at[0]),
        pltpu.make_async_copy(grad_in, rows_held.at[1], sem_pass.at[1]),
    ]
    parts = [(q, c, j) for c in range(2) for j in range(4) for q in range(2)]
    loads = [pltpu.make_async_copy(sums.at[part], held.at[part], sem_load.at[part]) for part in parts]
    for copy in passes + loads:
        copy.start()
    stores = [
        pltpu.make_async_copy(rows_held.at[0], output, sem_pass.at[2]),
        pltpu.make_async_copy(rows_held.at[1], grad, sem_pass.at[3]),
    ]
    for copy, store in zip(passes, stores):
        copy.wait()
        store.start()
    for part, load in zip(parts, loads):
        q, c, j = part
        load.wait()
        rows = held[q, c, j, :, 0:7].reshape(4 * PIECE, CH)
        wide[q, c, j] = rows[0:QUARTER].astype(F32)
        target = (grad_one, grad_two)[q].at[pl.ds(c * HALF + j * QUARTER, QUARTER)]
        stores.append(pltpu.make_async_copy(wide.at[part], target, sem_store.at[part]))
        stores[-1].start()
    for copy in stores:
        copy.wait()


def per_device(
    n_tile, n_dev, features, morton_pos, neighbours, rim, cotangent, weight_one, weight_two
):
    blocks, voxels, channels = features.shape
    scale = 1.0 / math.sqrt(blocks * voxels * n_tile * n_dev)
    n_x = n_tile // 2
    hbm = pl.BlockSpec(memory_space=pltpu.HBM)
    dma = pltpu.SemaphoreType.DMA
    block_table = pltpu.VMEM((BLK + 4 * RIM + 1, EDGE, PLANE, CH), BF16)
    wide = pltpu.VMEM((BLK, 6, PLANE, 9 * CH), BF16)
    flat = pltpu.VMEM((BLK * VOX, CH), F32)
    ring = pltpu.VMEM((9 * BLK, PLANE, CH), BF16)
    slab = pltpu.VMEM((n_dev, 2, VOX, CH), BF16)
    output, input_grad, sums = pl.pallas_call(
        functools.partial(unit_kernel, n_tile, n_dev, scale),
        out_shape=(
            jax.ShapeDtypeStruct(features.shape, BF16),
            jax.ShapeDtypeStruct(features.shape, BF16),
            jax.ShapeDtypeStruct((2, 2, 4, 4, 8, 16, CH), BF16),
        ),
        in_specs=[hbm] * 8,
        out_specs=(hbm, hbm, hbm),
        scratch_shapes=[
            pltpu.SMEM(morton_pos.shape, I32),
            pltpu.SMEM(neighbours.shape, I32),
            pltpu.SMEM(rim.shape, I32),
            pltpu.VMEM(features.shape, BF16),
            pltpu.VMEM(cotangent.shape, BF16),
            pltpu.VMEM(weight_one.shape, BF16),
            pltpu.VMEM(weight_two.shape, BF16),
            pltpu.VMEM((9 * PLANE, 9 * PLANE), BF16),
            pltpu.VMEM((2, 8, CH), I32),
            pltpu.SMEM((2, 8, CH), I32),
            pltpu.VMEM((2, 8, CH), I32),
            pltpu.SMEM((2, 8, CH), I32),
            pltpu.VMEM((n_dev, 1, CH), I32),
            pltpu.VMEM((8, 1, CH), I32),
            pltpu.VMEM((4, 8, CH), I32),
            pltpu.SMEM((4, 8, CH), I32),
            ring,
            ring,
            ring,
            ring,
            pltpu.VMEM((4, 4, BLK, PLANE, CH), BF16),
            pltpu.VMEM((4, 3, BLK, PLANE, CH), BF16),
            slab,
            slab,
            block_table,
            block_table,
            block_table,
            block_table,
            pltpu.VMEM((3, BLK, VOX, CH), BF16),
            pltpu.VMEM((2, BLK, VOX, CH), BF16),
            pltpu.VMEM((4, RIM, EDGE, PLANE, CH), BF16),
            pltpu.VMEM((27 * CH, CH), BF16),
            pltpu.VMEM((27 * CH, CH), BF16),
            pltpu.VMEM((2, 9 * PLANE, 6 * CH), BF16),
            wide,
            wide,
            wide,
            flat,
            flat,
            pltpu.VMEM((2, 27 * CH, CH), F32),
            pltpu.VMEM((2, 4, QUARTER, CH), F32),
            pltpu.VMEM((2, 4, QUARTER, CH), BF16),
            pltpu.VMEM((2, 3, QUARTER, CH), BF16),
            pltpu.VMEM((2, 4, PIECE, CH), BF16),
            pltpu.VMEM((2, 3, PIECE, CH), BF16),
            pltpu.VMEM((2, 4 * PIECE, CH), F32),
            pltpu.VMEM((2, 8, 16, CH), F32),
            pltpu.VMEM((2, 7, 16, CH), F32),
            pltpu.VMEM((2, 2, 4, 4, 8, 16, CH), BF16),
            dma((8,)),
            dma((1,)),
            dma((4,)),
            dma((8, 4)),
            dma((2, 4)),
            dma((2,)),
            dma((2,)),
            dma((2,)),
            dma((4, 4)),
            dma((4, 4)),
            dma((2, 8)),
            dma((2, 8)),
            dma((2, 3)),
            dma((2, 4)),
            dma((2, 6)),
        ],
        compiler_params=pltpu.CompilerParams(
            collective_id=0, has_side_effects=True, vmem_limit_bytes=62 * 1024 * 1024
        ),
    )(
        morton_pos,
        neighbours,
        rim,
        features,
        cotangent,
        weight_one,
        weight_two,
        jnp.asarray(shift_matrix(), BF16),
    )
    kernel_shape = jax.ShapeDtypeStruct(weight_one.shape, F32)
    return pl.pallas_call(
        finish_kernel,
        out_shape=(
            jax.ShapeDtypeStruct(features.shape, BF16),
            jax.ShapeDtypeStruct(features.shape, BF16),
            kernel_shape,
            kernel_shape,
        ),
        in_specs=[hbm] * 3,
        out_specs=(hbm,) * 4,
        scratch_shapes=[
            pltpu.VMEM((2,) + features.shape, BF16),
            pltpu.VMEM((2, 2, 4, 4, 8, 16, CH), BF16),
            pltpu.VMEM((2, 2, 4, QUARTER, CH), F32),
            dma((2, 2, 4)),
            dma((2, 2, 4)),
            dma((4,)),
        ],
        compiler_params=pltpu.CompilerParams(vmem_limit_bytes=62 * 1024 * 1024),
    )(sums, output, input_grad)


def solution(mesh):
    placed = (
        P(("tile", "dev"), None, None),
        P(("tile", "dev")),
        P(("tile", "dev"), None),
        P(("tile", "dev")),
        P(("tile", "dev"), None, None),
        P(),
        P(),
    )
    return jax.shard_map(
        functools.partial(per_device, mesh.shape["tile"], mesh.shape["dev"]),
        mesh=mesh,
        in_specs=placed,
        out_specs=(P(("tile", "dev"), None, None), P(("tile", "dev"), None, None), P(), P()),
        check_vma=False,
    )
```

```python
import functools
import math

import jax
import jax.numpy as jnp
import numpy as np
from jax import lax
from jax.experimental import pallas as pl
from jax.experimental.pallas import tpu as pltpu
from jax.sharding import PartitionSpec as P

EDGE = 4
PLANE = EDGE * EDGE
BLK = 8
VOX = 64
CH = 128
RIM = 4
HALF = 27 * CH // 2
QUARTER = HALF // 4
TILES = QUARTER // 16
PIECE = 7 * 16
F32 = jnp.float32
BF16 = jnp.bfloat16
I32 = jnp.int32


def shift_matrix():
    result = np.zeros((9 * PLANE, 9 * PLANE), np.float32)
    for ky in range(3):
        for kz in range(3):
            for j in range(EDGE):
                for k in range(EDGE):
                    y, z = j + ky - 1, k + kz - 1
                    dy, dz = y // EDGE + 1, z // EDGE + 1
                    source = ((dy * 3 + dz) * EDGE + y % EDGE) * EDGE + z % EDGE
                    result[((ky * 3 + kz) * EDGE + j) * EDGE + k, source] = 1.0
    return result


def dot(left, right):
    return jnp.dot(left, right, preferred_element_type=F32)


def unit_kernel(
    n_tile,
    n_dev,
    scale,
    pos_in,
    nbr_in,
    rim_in,
    feat_in,
    cot_in,
    w1_in,
    w2_in,
    smat_in,
    out_output,
    out_grad,
    out_sums,
    pos,
    nbr,
    rim,
    feat,
    cot,
    w1,
    w2,
    smat,
    idxv,
    idxs,
    slotv,
    slots,
    labels,
    z_labels,
    z_slotv,
    z_slots,
    ring_0,
    ring_1,
    ring_2,
    ring_3,
    y_send,
    y_got,
    repacked,
    returned,
    tab_m,
    tab_c,
    tab_h,
    tab_p,
    own,
    leaving,
    rims,
    wt1,
    wt2,
    planes,
    y_m,
    y_c,
    y_x,
    pre_one,
    hidden_grad,
    grads,
    core_in,
    x_out,
    x_in,
    y_out,
    y_in,
    own_sum,
    z_out,
    z_in,
    final,
    sem_in,
    sem_local,
    sem_ring_s,
    sem_ring_r,
    sem_y,
    sem_z_lab,
    sem_lab,
    sem_back,
    sem_halo_s,
    sem_halo_r,
    sem_sum_s,
    sem_sum_r,
    sem_first,
    sem_core,
    sem_out,
):
    tile = lax.axis_index("tile")
    dev = lax.axis_index("dev")
    core = lax.rem(tile, 2)
    chip_x = tile // 2
    n_x = n_tile // 2

    def remote(src, dst, send, recv, **where):
        return pltpu.make_async_remote_copy(
            src_ref=src,
            dst_ref=dst,
            send_sem=send,
            recv_sem=recv,
            device_id=where,
            device_id_type=pl.DeviceIdType.MESH,
        )

    def await_bytes(ref, sem):
        pltpu.make_async_copy(ref, ref, sem).wait()

    operands = (pos_in, rim_in, feat_in, cot_in, w2_in, w1_in, smat_in, nbr_in)
    places = (pos, rim, feat, cot, w2, w1, smat, nbr)
    loads = [
        pltpu.make_async_copy(source, place, sem_in.at[i])
        for i, (source, place) in enumerate(zip(operands, places))
    ]
    load_pos, load_rim, load_feat, load_cot, load_w2, load_w1, load_smat, load_nbr = loads
    for load in loads:
        load.start()
    for table in (tab_m, tab_c, tab_h, tab_p):
        table[BLK + 2 * RIM :] = jnp.zeros((2 * RIM + 1, EDGE, PLANE, CH), BF16)
    barrier = pltpu.get_barrier_semaphore()

    @pl.loop(1, n_dev)
    def _(d):
        pl.semaphore_signal(barrier, inc=1, device_id={"dev": lax.rem(dev + d, n_dev)})

    @pl.loop(1, n_tile)
    def _(d):
        pl.semaphore_signal(barrier, inc=1, device_id={"tile": lax.rem(tile + d, n_tile)})

    sub = lax.broadcasted_iota(I32, (8, CH), 0)
    lane = lax.broadcasted_iota(I32, (8, CH), 1)
    load_pos.wait()
    posv = jnp.zeros((8, CH), I32)
    for r in range(BLK):
        posv = jnp.where(sub == r, pos[r], posv)
    owner = posv // BLK
    count = jnp.zeros((8, CH), I32)
    for r in range(BLK):
        count = count + jnp.where((owner == pos[r] // BLK) & (sub > r), 1, 0)
    slot_of_row = lax.rem(owner - dev + n_dev, n_dev) * 2 + count
    hit = lane == slot_of_row
    row_of_slot = jnp.min(jnp.where(hit, sub, BLK - 1), axis=0, keepdims=True)
    label_of_slot = jnp.min(jnp.where(hit, lax.rem(posv, BLK), BLK), axis=0, keepdims=True)
    idxv[0] = jnp.broadcast_to(row_of_slot, (8, CH))
    idxv[1] = jnp.minimum(slot_of_row, 2 * n_dev - 1)
    labels[0] = label_of_slot
    to_scalars = pltpu.make_async_copy(idxv, idxs, sem_local.at[0])
    to_scalars.start()

    def pack_rims(rows, which):
        for h in range(RIM):
            rims[which, h] = rows[rim[h]].reshape(EDGE, PLANE, CH)

    def halo_copies(which, table):
        result = []
        every, low, high = slice(None), pl.ds(0, PLANE // 2), pl.ds(PLANE // 2, PLANE // 2)
        for q, (where, part) in enumerate(
            (
                (dict(tile=lax.rem(tile + 1, n_tile)), (pl.ds(EDGE - 1, 1), every)),
                (dict(tile=lax.rem(tile + n_tile - 1, n_tile)), (pl.ds(0, 1), every)),
                (dict(dev=lax.rem(dev + 1, n_dev)), (every, high)),
                (dict(dev=lax.rem(dev + n_dev - 1, n_dev)), (every, low)),
            )
        ):
            result.append(
                remote(
                    rims.at[(which, every) + part],
                    table.at[(pl.ds(BLK + q * RIM, RIM),) + part],
                    sem_halo_s.at[which, q],
                    sem_halo_r.at[which, q],
                    **where,
                )
            )
        return result

    def finish_halo(copies, table):
        for copy in copies:
            copy.wait()
        edges = (tile == 0, tile == n_tile - 1, dev == 0, dev == n_dev - 1)
        for q, edge in enumerate(edges):

            @pl.when(edge)
            def _(q=q):
                table[BLK + q * RIM : BLK + (q + 1) * RIM] = jnp.zeros((RIM, EDGE, PLANE, CH), BF16)

    load_rim.wait()
    load_cot.wait()
    tab_c[0:BLK] = cot[...].reshape(BLK, EDGE, PLANE, CH)
    pack_rims(cot, 0)
    load_feat.wait()
    to_scalars.wait()

    rings = (ring_0, ring_1, ring_2, ring_3)
    for p, ring in enumerate(rings):
        ring[0:BLK] = feat[:, p * PLANE : (p + 1) * PLANE, :]
        ring[8 * BLK] = jnp.zeros((PLANE, CH), BF16)
    pos_lanes = jnp.zeros((1, CH), I32)
    for r in range(BLK):
        pos_lanes = jnp.where(lax.rem(lane[0:1], BLK) == r, pos[r], pos_lanes)
    z_labels[0] = pos_lanes

    y = lax.rem(dev, 4)
    z = dev // 4
    n_z = n_dev // 4

    def ring_copy(step, p, ahead):
        source = step - 1 if ahead else (9 - step) % 8
        target = step if ahead else 8 - step
        where = lax.rem(dev + (4 if ahead else n_dev - 4), n_dev)
        return remote(
            rings[p].at[pl.ds(source * BLK, BLK)],
            rings[p].at[pl.ds(target * BLK, BLK)],
            sem_ring_s.at[p],
            sem_ring_r.at[target, p],
            dev=where,
        )

    def ring_starts(step, p):
        if step < 4:
            return [ring_copy(step, p, True), ring_copy(step, p, False)]
        return [ring_copy(4, p, p < 2)]

    def ring_step(step):
        for p in range(4):
            arriving = ring_starts(step, p)
            leaving_now = ring_starts(step + 1, p)
            for copy in arriving:
                copy.wait_recv()
            for copy in leaving_now:
                copy.start()

    pl.semaphore_wait(barrier, n_dev + n_tile - 2)

    for k in range(1, n_z):
        where = lax.rem(dev + 4 * k, n_dev)
        remote(z_labels.at[0], z_labels.at[k], sem_z_lab.at[0], sem_z_lab.at[1], dev=where).start()
    for p in range(4):
        for copy in ring_starts(1, p):
            copy.start()
    halo_c = halo_copies(0, tab_c)
    for copy in halo_c:
        copy.start()

    @pl.loop(1, n_dev)
    def _(d):
        where = lax.rem(dev + d, n_dev)
        remote(labels.at[0], labels.at[d], sem_lab.at[0], sem_lab.at[1], dev=where).start()

    def flip_weights(source, target):
        for o in range(27):
            piece = source[o * CH : (o + 1) * CH, :].astype(F32)
            target[(26 - o) * CH : (27 - o) * CH, :] = piece.T.astype(BF16)

    def expand(table, y):
        for b in range(BLK):
            near = planes.at[b % 2]
            for i in range(6):
                dx = 0 if i == 0 else (2 if i == 5 else 1)
                row = (i + EDGE - 1) % EDGE
                for t in range(9):
                    near[t * PLANE : (t + 1) * PLANE, i * CH : (i + 1) * CH] = table[
                        nbr[b, dx * 9 + t], row
                    ]
            moved = dot(smat[...], near[...]).astype(BF16)
            for i in range(6):
                for t in range(9):
                    y[b, i, :, t * CH : (t + 1) * CH] = moved[
                        t * PLANE : (t + 1) * PLANE, i * CH : (i + 1) * CH
                    ]

    def columns(y, kx):
        return y[:, kx : kx + EDGE].reshape(BLK * VOX, 9 * CH)

    def conv(y, w):
        return (
            dot(columns(y, 0), w[0 : 9 * CH, :])
            + dot(columns(y, 1), w[9 * CH : 18 * CH, :])
            + dot(columns(y, 2), w[18 * CH : 27 * CH, :])
        )

    load_w2.wait()
    flip_weights(w2, wt2)
    load_w1.wait()
    flip_weights(w1, wt1)
    load_smat.wait()
    load_nbr.wait()
    ring_step(1)
    finish_halo(halo_c, tab_c)
    expand(tab_c, y_c)
    ring_step(2)
    hidden_grad[...] = conv(y_c, wt2)
    await_bytes(z_labels.at[pl.ds(1, n_z - 1)], sem_z_lab.at[1])
    z_pos = jnp.full((8, CH), -1, I32)
    for k in range(n_z):
        z_pos = jnp.where(lane // BLK == k, z_labels[k], z_pos)
    for dy in range(4):
        wanted = (z * 4 + lax.rem(y + dy, 4)) * BLK + sub
        found = jnp.min(jnp.where(z_pos == wanted, lane, 8 * BLK), axis=1, keepdims=True)
        z_slotv[dy] = jnp.broadcast_to(found, (8, CH))
    to_z_slots = pltpu.make_async_copy(z_slotv, z_slots, sem_local.at[0])
    to_z_slots.start()
    to_z_slots.wait()
    ring_step(3)

    def y_copy(p, dy):
        where = dict(dev=z * 4 + lax.rem(y + dy, 4))
        return remote(y_send.at[p, dy], y_got.at[p, dy - 1], sem_y.at[0, p], sem_y.at[1, p], **where)

    for p in (0, 2, 1, 3):
        for copy in ring_starts(4, p):
            copy.wait_recv()
        for dy in (2, 1, 3, 0):
            for s in range(BLK):
                y_send[p, dy, s] = rings[p][z_slots[dy, s, 0]]
            if dy:
                y_copy(p, dy).start()
    for p in (0, 2, 1, 3):
        await_bytes(y_got.at[p], sem_y.at[1, p])
        rows = y_send[p, 0].astype(F32)
        for dy in range(3):
            rows = rows + y_got[p, dy].astype(F32)
        own[0, :, p * PLANE : (p + 1) * PLANE, :] = rows.astype(BF16)
    tab_m[0:BLK] = own[0].reshape(BLK, EDGE, PLANE, CH)
    pack_rims(own.at[0], 1)
    halo_m = halo_copies(1, tab_m)
    for copy in halo_m:
        copy.start()
    await_bytes(labels.at[pl.ds(1, n_dev - 1)], sem_lab.at[1])
    label_at = jnp.zeros((8, CH), I32)
    for d in range(n_dev):
        label_at = jnp.where(lane // 2 == d, labels[d], label_at)
    slotv[0] = jnp.minimum(label_at, BLK - 1)
    to_slots = pltpu.make_async_copy(slotv, slots, sem_local.at[0])
    to_slots.start()
    to_slots.wait()
    finish_halo(halo_m, tab_m)
    expand(tab_m, y_m)
    pre = conv(y_m, w1)
    gate = jax.nn.sigmoid(pre)
    hidden = (pre * gate).astype(BF16)
    pre_grad = (hidden_grad[...] * gate * (1.0 + pre * (1.0 - gate))).astype(BF16)
    tab_h[0:BLK] = hidden.reshape(BLK, EDGE, PLANE, CH)
    tab_p[0:BLK] = pre_grad.reshape(BLK, EDGE, PLANE, CH)
    own[1] = hidden.reshape(BLK, VOX, CH)
    own[2] = pre_grad.reshape(BLK, VOX, CH)
    pack_rims(own.at[1], 2)
    pack_rims(own.at[2], 3)
    halo_h = halo_copies(2, tab_h)
    halo_p = halo_copies(3, tab_p)
    for copy in halo_h + halo_p:
        copy.start()

    partner = dict(tile=tile + 1 - 2 * core)

    def core_copy(q, chunk):
        start = pl.multiple_of((1 - core) * HALF + chunk * QUARTER, 16)
        return remote(
            grads.at[q, pl.ds(start, QUARTER)],
            core_in.at[q, chunk],
            sem_sum_s.at[q, 0],
            sem_core.at[q, chunk],
            **partner,
        )

    dims = (("x", "y"), ("y", "x"))
    place = dict(x=chip_x, y=y)

    def start_core(q):
        for e in (2, 1, 3, 0):
            core_copy(q, lax.rem(place[dims[q][0]] + e, 4)).start()

    hidden_t = own[1].reshape(BLK * VOX, CH).astype(F32).T.astype(BF16)
    for kx in range(3):
        part = dot(hidden_t, columns(y_c, kx))
        for t in range(9):
            o = 26 - (kx * 9 + t)
            grads[1, o * CH : (o + 1) * CH, :] = part[:, t * CH : (t + 1) * CH]
    start_core(1)
    pre_grad_t = own[2].reshape(BLK * VOX, CH).astype(F32).T.astype(BF16)
    for kx in range(3):
        part = dot(pre_grad_t, columns(y_m, kx))
        for t in range(9):
            o = kx * 9 + t
            grads[0, o * CH : (o + 1) * CH, :] = part[:, t * CH : (t + 1) * CH].T
    start_core(0)

    def peer(dim, e):
        if dim == "x":
            other = lax.rem(chip_x + e, n_x)
            return other, dict(tile=other * 2 + core)
        if dim == "y":
            other = lax.rem(y + e, 4)
            return other, dict(dev=z * 4 + other)
        other = lax.rem(z + e, n_z)
        return other, dict(dev=other * 4 + y)

    def sem(q, stage):
        return sem_sum_s.at[q, stage], sem_sum_r.at[q, stage]

    def both_cores(q, chunk):
        start = pl.multiple_of(core * HALF + chunk * QUARTER, 16)
        return grads[q, pl.ds(start, QUARTER), :] + core_in[q, chunk]

    def start_first(q):
        for e in (2, 1, 3):
            other, where = peer(dims[q][0], e)
            core_copy(q, other).wait_recv()
            x_out[q, other] = both_cores(q, other).astype(BF16)
            remote(x_out.at[q, other], x_in.at[q, e - 1], *sem(q, 1), **where).start()
        core_copy(q, place[dims[q][0]]).wait_recv()

    def start_second(q):
        await_bytes(x_in.at[q], sem_sum_r.at[q, 1])
        total = both_cores(q, place[dims[q][0]])
        for e in range(3):
            total = total + x_in[q, e].astype(F32)
        own_sum[q, 0:QUARTER] = total
        own_sum[q, QUARTER:] = jnp.zeros((4 * PIECE - QUARTER, CH), F32)
        for j in range(4):
            y_out[q, j] = own_sum[q, j * PIECE : (j + 1) * PIECE].astype(BF16)
        for e in (2, 1, 3):
            other, where = peer(dims[q][1], e)
            remote(y_out.at[q, other], y_in.at[q, e - 1], *sem(q, 2), **where).start()

    def start_third(q):
        await_bytes(y_in.at[q], sem_sum_r.at[q, 2])
        start = pl.multiple_of(place[dims[q][1]] * PIECE, 16)
        total = own_sum[q, pl.ds(start, PIECE), :]
        for e in range(3):
            total = total + y_in[q, e].astype(F32)
        z_out[q, 0:7] = total.reshape(7, 16, CH)
        z_out[q, 7] = jnp.zeros((16, CH), F32)
        for e in (4, 3, 5, 2, 6, 1, 7):
            other, where = peer("z", e)
            remote(z_out.at[q, other], z_in.at[q, e - 1], *sem(q, 3), **where).start()

    def start_gather_third(q):
        await_bytes(z_in.at[q], sem_sum_r.at[q, 3])
        total = z_out[q, z]
        for e in range(7):
            total = total + z_in[q, e]
        mine = final.at[q, core, place[dims[q][0]], place[dims[q][1]], z]
        mine[...] = (total * scale).astype(BF16)
        for e in (4, 3, 5, 2, 6, 1, 7):
            _, where = peer("z", e)
            remote(mine, mine, *sem(q, 4), **where).start()

    def start_gather_second(q):
        await_bytes(final.at[q, core, 0, 0, pl.ds(0, 7)], sem_sum_r.at[q, 4])
        mine = final.at[q, core, place[dims[q][0]], place[dims[q][1]], pl.ds(0, 7)]
        for e in (2, 1, 3):
            _, where = peer(dims[q][1], e)
            remote(mine, mine, *sem(q, 5), **where).start()

    def gather_core_copy(q, chunk):
        piece = final.at[q, core, chunk, :, pl.ds(0, 7)]
        return remote(piece, piece, *sem(q, 7), **partner)

    def exit_copy(q, chunk):
        return pltpu.make_async_copy(
            final.at[q, core, chunk], out_sums.at[q, core, chunk], sem_out.at[q, chunk]
        )

    def gather_first_copy(q, e):
        mine = final.at[q, core, place[dims[q][0]], :, pl.ds(0, 7)]
        _, where = peer(dims[q][0], e)
        return remote(mine, mine, sem_sum_s.at[q, 6], sem_first.at[q, e - 1], **where)

    def start_gather_first(q):
        await_bytes(final.at[q, core, 0, pl.ds(0, 3), pl.ds(0, 7)], sem_sum_r.at[q, 5])
        for e in (2, 1, 3):
            gather_first_copy(q, e).start()
        gather_core_copy(q, place[dims[q][0]]).start()
        exit_copy(q, place[dims[q][0]]).start()

    def start_gather_core(q):
        for e in (1, 3, 2):
            chunk = lax.rem(place[dims[q][0]] + 4 - e, 4)
            gather_first_copy(q, e).wait_recv()
            gather_core_copy(q, chunk).start()
            exit_copy(q, chunk).start()

    start_first(1)
    start_first(0)
    finish_halo(halo_h, tab_h)
    expand(tab_h, y_x)
    pre_two = conv(y_x, w2)
    leaving[0] = (
        (own[0].reshape(BLK * VOX, CH).astype(F32) + pre_two).astype(BF16).reshape(BLK, VOX, CH)
    )
    exit_output = pltpu.make_async_copy(leaving.at[0], out_output, sem_out.at[0, 5])
    exit_output.start()
    finish_halo(halo_p, tab_p)
    expand(tab_p, y_x)
    back = conv(y_x, wt1) + cot[...].reshape(BLK * VOX, CH).astype(F32)
    own[1] = back.astype(BF16).reshape(BLK, VOX, CH)

    @pl.loop(0, n_dev)
    def _(d):
        for c in range(2):
            repacked[d, c] = own[1, slots[0, 0, 2 * d + c]]

    returned[0] = repacked[0]

    order = [7 * i % n_dev for i in range(1, n_dev)]

    def send_back(offsets):
        for d in offsets:
            where = lax.rem(dev - d + n_dev, n_dev)
            remote(repacked.at[d], returned.at[d], sem_back.at[0], sem_back.at[1], dev=where).start()

    send_back(order[0:4])
    for stage, offsets in (
        (start_second, order[4:9]),
        (start_third, order[9:14]),
        (start_gather_third, order[14:19]),
        (start_gather_second, order[19:24]),
        (start_gather_first, order[24:]),
        (start_gather_core, []),
    ):
        stage(1)
        stage(0)
        send_back(offsets)
    await_bytes(returned.at[pl.ds(1, n_dev - 1)], sem_back.at[1])
    for r in range(BLK):
        linear = idxs[1, r, 0]
        leaving[1, r] = returned[linear // 2, lax.rem(linear, 2)]
    exit_grad = pltpu.make_async_copy(leaving.at[1], out_grad, sem_out.at[1, 5])
    exit_grad.start()

    await_bytes(labels.at[pl.ds(1, n_dev - 1)], sem_lab.at[0])
    await_bytes(z_labels.at[pl.ds(1, n_z - 1)], sem_z_lab.at[0])
    for p in range(4):
        await_bytes(rings[p].at[pl.ds(0, 7 * BLK)], sem_ring_s.at[p])
        await_bytes(y_got.at[p], sem_y.at[0, p])
    await_bytes(repacked.at[pl.ds(1, n_dev - 1)], sem_back.at[0])
    for q in (1, 0):
        await_bytes(final.at[q, 1 - core, :, :, pl.ds(0, 7)], sem_sum_r.at[q, 7])
        pltpu.make_async_copy(
            final.at[q, 1 - core], out_sums.at[q, 1 - core], sem_out.at[q, 4]
        ).start()
    for q in range(2):
        await_bytes(core_in.at[q], sem_sum_s.at[q, 0])
        await_bytes(x_in.at[q], sem_sum_s.at[q, 1])
        await_bytes(y_in.at[q], sem_sum_s.at[q, 2])
        await_bytes(z_in.at[q], sem_sum_s.at[q, 3])
        await_bytes(final.at[q, core, 0, 0, pl.ds(0, 7)], sem_sum_s.at[q, 4])
        await_bytes(final.at[q, core, 0, pl.ds(0, 3), pl.ds(0, 7)], sem_sum_s.at[q, 5])
        await_bytes(final.at[q, core, pl.ds(0, 3), :, pl.ds(0, 7)], sem_sum_s.at[q, 6])
        await_bytes(final.at[q, core, :, :, pl.ds(0, 7)], sem_sum_s.at[q, 7])
        for chunk in range(4):
            exit_copy(q, chunk).wait()
        pltpu.make_async_copy(
            final.at[q, 1 - core], out_sums.at[q, 1 - core], sem_out.at[q, 4]
        ).wait()
    exit_output.wait()
    exit_grad.wait()


def finish_kernel(
    sums, output_in, grad_in, output, grad, grad_one, grad_two, rows_held, held, wide, sem_load, sem_store, sem_pass
):
    passes = [
        pltpu.make_async_copy(output_in, rows_held.at[0], sem_pass.at[0]),
        pltpu.make_async_copy(grad_in, rows_held.at[1], sem_pass.at[1]),
    ]
    parts = [(q, c, j) for c in range(2) for j in range(4) for q in range(2)]
    loads = [pltpu.make_async_copy(sums.at[part], held.at[part], sem_load.at[part]) for part in parts]
    for copy in passes + loads:
        copy.start()
    stores = [
        pltpu.make_async_copy(rows_held.at[0], output, sem_pass.at[2]),
        pltpu.make_async_copy(rows_held.at[1], grad, sem_pass.at[3]),
    ]
    for copy, store in zip(passes, stores):
        copy.wait()
        store.start()
    for part, load in zip(parts, loads):
        q, c, j = part
        load.wait()
        rows = held[q, c, j, :, 0:7].reshape(4 * PIECE, CH)
        wide[q, c, j] = rows[0:QUARTER].astype(F32)
        target = (grad_one, grad_two)[q].at[pl.ds(c * HALF + j * QUARTER, QUARTER)]
        stores.append(pltpu.make_async_copy(wide.at[part], target, sem_store.at[part]))
        stores[-1].start()
    for copy in stores:
        copy.wait()


def per_device(
    n_tile, n_dev, features, morton_pos, neighbours, rim, cotangent, weight_one, weight_two
):
    blocks, voxels, channels = features.shape
    scale = 1.0 / math.sqrt(blocks * voxels * n_tile * n_dev)
    n_x = n_tile // 2
    hbm = pl.BlockSpec(memory_space=pltpu.HBM)
    dma = pltpu.SemaphoreType.DMA
    block_table = pltpu.VMEM((BLK + 4 * RIM + 1, EDGE, PLANE, CH), BF16)
    wide = pltpu.VMEM((BLK, 6, PLANE, 9 * CH), BF16)
    flat = pltpu.VMEM((BLK * VOX, CH), F32)
    ring = pltpu.VMEM((9 * BLK, PLANE, CH), BF16)
    slab = pltpu.VMEM((n_dev, 2, VOX, CH), BF16)
    output, input_grad, sums = pl.pallas_call(
        functools.partial(unit_kernel, n_tile, n_dev, scale),
        out_shape=(
            jax.ShapeDtypeStruct(features.shape, BF16),
            jax.ShapeDtypeStruct(features.shape, BF16),
            jax.ShapeDtypeStruct((2, 2, 4, 4, 8, 16, CH), BF16),
        ),
        in_specs=[hbm] * 8,
        out_specs=(hbm, hbm, hbm),
        scratch_shapes=[
            pltpu.SMEM(morton_pos.shape, I32),
            pltpu.SMEM(neighbours.shape, I32),
            pltpu.SMEM(rim.shape, I32),
            pltpu.VMEM(features.shape, BF16),
            pltpu.VMEM(cotangent.shape, BF16),
            pltpu.VMEM(weight_one.shape, BF16),
            pltpu.VMEM(weight_two.shape, BF16),
            pltpu.VMEM((9 * PLANE, 9 * PLANE), BF16),
            pltpu.VMEM((2, 8, CH), I32),
            pltpu.SMEM((2, 8, CH), I32),
            pltpu.VMEM((2, 8, CH), I32),
            pltpu.SMEM((2, 8, CH), I32),
            pltpu.VMEM((n_dev, 1, CH), I32),
            pltpu.VMEM((8, 1, CH), I32),
            pltpu.VMEM((4, 8, CH), I32),
            pltpu.SMEM((4, 8, CH), I32),
            ring,
            ring,
            ring,
            ring,
            pltpu.VMEM((4, 4, BLK, PLANE, CH), BF16),
            pltpu.VMEM((4, 3, BLK, PLANE, CH), BF16),
            slab,
            slab,
            block_table,
            block_table,
            block_table,
            block_table,
            pltpu.VMEM((3, BLK, VOX, CH), BF16),
            pltpu.VMEM((2, BLK, VOX, CH), BF16),
            pltpu.VMEM((4, RIM, EDGE, PLANE, CH), BF16),
            pltpu.VMEM((27 * CH, CH), BF16),
            pltpu.VMEM((27 * CH, CH), BF16),
            pltpu.VMEM((2, 9 * PLANE, 6 * CH), BF16),
            wide,
            wide,
            wide,
            flat,
            flat,
            pltpu.VMEM((2, 27 * CH, CH), F32),
            pltpu.VMEM((2, 4, QUARTER, CH), F32),
            pltpu.VMEM((2, 4, QUARTER, CH), BF16),
            pltpu.VMEM((2, 3, QUARTER, CH), BF16),
            pltpu.VMEM((2, 4, PIECE, CH), BF16),
            pltpu.VMEM((2, 3, PIECE, CH), BF16),
            pltpu.VMEM((2, 4 * PIECE, CH), F32),
            pltpu.VMEM((2, 8, 16, CH), F32),
            pltpu.VMEM((2, 7, 16, CH), F32),
            pltpu.VMEM((2, 2, 4, 4, 8, 16, CH), BF16),
            dma((8,)),
            dma((1,)),
            dma((4,)),
            dma((8, 4)),
            dma((2, 4)),
            dma((2,)),
            dma((2,)),
            dma((2,)),
            dma((4, 4)),
            dma((4, 4)),
            dma((2, 8)),
            dma((2, 8)),
            dma((2, 3)),
            dma((2, 4)),
            dma((2, 6)),
        ],
        compiler_params=pltpu.CompilerParams(
            collective_id=0, has_side_effects=True, vmem_limit_bytes=62 * 1024 * 1024
        ),
    )(
        morton_pos,
        neighbours,
        rim,
        features,
        cotangent,
        weight_one,
        weight_two,
        jnp.asarray(shift_matrix(), BF16),
    )
    kernel_shape = jax.ShapeDtypeStruct(weight_one.shape, F32)
    return pl.pallas_call(
        finish_kernel,
        out_shape=(
            jax.ShapeDtypeStruct(features.shape, BF16),
            jax.ShapeDtypeStruct(features.shape, BF16),
            kernel_shape,
            kernel_shape,
        ),
        in_specs=[hbm] * 3,
        out_specs=(hbm,) * 4,
        scratch_shapes=[
            pltpu.VMEM((2,) + features.shape, BF16),
            pltpu.VMEM((2, 2, 4, 4, 8, 16, CH), BF16),
            pltpu.VMEM((2, 2, 4, QUARTER, CH), F32),
            dma((2, 2, 4)),
            dma((2, 2, 4)),
            dma((4,)),
        ],
        compiler_params=pltpu.CompilerParams(vmem_limit_bytes=62 * 1024 * 1024),
    )(sums, output, input_grad)


def solution(mesh):
    placed = (
        P(("tile", "dev"), None, None),
        P(("tile", "dev")),
        P(("tile", "dev"), None),
        P(("tile", "dev")),
        P(("tile", "dev"), None, None),
        P(),
        P(),
    )
    return jax.shard_map(
        functools.partial(per_device, mesh.shape["tile"], mesh.shape["dev"]),
        mesh=mesh,
        in_specs=placed,
        out_specs=(P(("tile", "dev"), None, None), P(("tile", "dev"), None, None), P(), P()),
        check_vma=False,
    )
```

```python
import functools
import math

import jax
import jax.numpy as jnp
import numpy as np
from jax import lax
from jax.experimental import pallas as pl
from jax.experimental.pallas import tpu as pltpu
from jax.sharding import PartitionSpec as P

EDGE = 4
PLANE = EDGE * EDGE
BLK = 8
VOX = 64
CH = 128
RIM = 4
HALF = 27 * CH // 2
QUARTER = HALF // 4
TILES = QUARTER // 16
PIECE = 7 * 16
F32 = jnp.float32
BF16 = jnp.bfloat16
I32 = jnp.int32


def shift_matrix():
    result = np.zeros((9 * PLANE, 9 * PLANE), np.float32)
    for ky in range(3):
        for kz in range(3):
            for j in range(EDGE):
                for k in range(EDGE):
                    y, z = j + ky - 1, k + kz - 1
                    dy, dz = y // EDGE + 1, z // EDGE + 1
                    source = ((dy * 3 + dz) * EDGE + y % EDGE) * EDGE + z % EDGE
                    result[((ky * 3 + kz) * EDGE + j) * EDGE + k, source] = 1.0
    return result


def dot(left, right):
    return jnp.dot(left, right, preferred_element_type=F32)


def unit_kernel(
    n_tile,
    n_dev,
    scale,
    pos_in,
    nbr_in,
    rim_in,
    feat_in,
    cot_in,
    w1_in,
    w2_in,
    smat_in,
    out_output,
    out_grad,
    out_sums,
    pos,
    nbr,
    rim,
    feat,
    cot,
    w1,
    w2,
    smat,
    idxv,
    idxs,
    slotv,
    slots,
    labels,
    z_labels,
    z_slotv,
    z_slots,
    ring_0,
    ring_1,
    ring_2,
    ring_3,
    y_send,
    y_got,
    repacked,
    returned,
    tab_m,
    tab_c,
    tab_h,
    tab_p,
    own,
    leaving,
    rims,
    wt1,
    wt2,
    planes,
    y_m,
    y_c,
    y_x,
    pre_one,
    hidden_grad,
    grads,
    core_in,
    x_out,
    x_in,
    y_out,
    y_in,
    own_sum,
    z_out,
    z_in,
    final,
    sem_in,
    sem_local,
    sem_ring_s,
    sem_ring_r,
    sem_y,
    sem_z_lab,
    sem_lab,
    sem_back,
    sem_halo_s,
    sem_halo_r,
    sem_sum_s,
    sem_sum_r,
    sem_first,
    sem_core,
    sem_out,
):
    tile = lax.axis_index("tile")
    dev = lax.axis_index("dev")
    core = lax.rem(tile, 2)
    chip_x = tile // 2
    n_x = n_tile // 2

    def remote(src, dst, send, recv, **where):
        return pltpu.make_async_remote_copy(
            src_ref=src,
            dst_ref=dst,
            send_sem=send,
            recv_sem=recv,
            device_id=where,
            device_id_type=pl.DeviceIdType.MESH,
        )

    def await_bytes(ref, sem):
        pltpu.make_async_copy(ref, ref, sem).wait()

    operands = (pos_in, rim_in, feat_in, cot_in, w2_in, w1_in, smat_in, nbr_in)
    places = (pos, rim, feat, cot, w2, w1, smat, nbr)
    loads = [
        pltpu.make_async_copy(source, place, sem_in.at[i])
        for i, (source, place) in enumerate(zip(operands, places))
    ]
    load_pos, load_rim, load_feat, load_cot, load_w2, load_w1, load_smat, load_nbr = loads
    for load in loads:
        load.start()
    for table in (tab_m, tab_c, tab_h, tab_p):
        table[BLK + 2 * RIM :] = jnp.zeros((2 * RIM + 1, EDGE, PLANE, CH), BF16)
    barrier = pltpu.get_barrier_semaphore()

    @pl.loop(1, n_dev)
    def _(d):
        pl.semaphore_signal(barrier, inc=1, device_id={"dev": lax.rem(dev + d, n_dev)})

    @pl.loop(1, n_tile)
    def _(d):
        pl.semaphore_signal(barrier, inc=1, device_id={"tile": lax.rem(tile + d, n_tile)})

    sub = lax.broadcasted_iota(I32, (8, CH), 0)
    lane = lax.broadcasted_iota(I32, (8, CH), 1)
    load_pos.wait()
    posv = jnp.zeros((8, CH), I32)
    for r in range(BLK):
        posv = jnp.where(sub == r, pos[r], posv)
    owner = posv // BLK
    count = jnp.zeros((8, CH), I32)
    for r in range(BLK):
        count = count + jnp.where((owner == pos[r] // BLK) & (sub > r), 1, 0)
    slot_of_row = lax.rem(owner - dev + n_dev, n_dev) * 2 + count
    hit = lane == slot_of_row
    row_of_slot = jnp.min(jnp.where(hit, sub, BLK - 1), axis=0, keepdims=True)
    label_of_slot = jnp.min(jnp.where(hit, lax.rem(posv, BLK), BLK), axis=0, keepdims=True)
    idxv[0] = jnp.broadcast_to(row_of_slot, (8, CH))
    idxv[1] = jnp.minimum(slot_of_row, 2 * n_dev - 1)
    labels[0] = label_of_slot
    to_scalars = pltpu.make_async_copy(idxv, idxs, sem_local.at[0])
    to_scalars.start()

    def pack_rims(rows, which):
        for h in range(RIM):
            rims[which, h] = rows[rim[h]].reshape(EDGE, PLANE, CH)

    def halo_copies(which, table):
        result = []
        every, low, high = slice(None), pl.ds(0, PLANE // 2), pl.ds(PLANE // 2, PLANE // 2)
        for q, (where, part) in enumerate(
            (
                (dict(tile=lax.rem(tile + 1, n_tile)), (pl.ds(EDGE - 1, 1), every)),
                (dict(tile=lax.rem(tile + n_tile - 1, n_tile)), (pl.ds(0, 1), every)),
                (dict(dev=lax.rem(dev + 1, n_dev)), (every, high)),
                (dict(dev=lax.rem(dev + n_dev - 1, n_dev)), (every, low)),
            )
        ):
            result.append(
                remote(
                    rims.at[(which, every) + part],
                    table.at[(pl.ds(BLK + q * RIM, RIM),) + part],
                    sem_halo_s.at[which, q],
                    sem_halo_r.at[which, q],
                    **where,
                )
            )
        return result

    def finish_halo(copies, table):
        for copy in copies:
            copy.wait()
        edges = (tile == 0, tile == n_tile - 1, dev == 0, dev == n_dev - 1)
        for q, edge in enumerate(edges):

            @pl.when(edge)
            def _(q=q):
                table[BLK + q * RIM : BLK + (q + 1) * RIM] = jnp.zeros((RIM, EDGE, PLANE, CH), BF16)

    load_rim.wait()
    load_cot.wait()
    tab_c[0:BLK] = cot[...].reshape(BLK, EDGE, PLANE, CH)
    pack_rims(cot, 0)
    load_feat.wait()
    to_scalars.wait()

    rings = (ring_0, ring_1, ring_2, ring_3)
    for p, ring in enumerate(rings):
        ring[0:BLK] = feat[:, p * PLANE : (p + 1) * PLANE, :]
        ring[8 * BLK] = jnp.zeros((PLANE, CH), BF16)
    pos_lanes = jnp.zeros((1, CH), I32)
    for r in range(BLK):
        pos_lanes = jnp.where(lax.rem(lane[0:1], BLK) == r, pos[r], pos_lanes)
    z_labels[0] = pos_lanes

    y = lax.rem(dev, 4)
    z = dev // 4
    n_z = n_dev // 4

    def ring_copy(step, p, ahead):
        source = step - 1 if ahead else (9 - step) % 8
        target = step if ahead else 8 - step
        where = lax.rem(dev + (4 if ahead else n_dev - 4), n_dev)
        return remote(
            rings[p].at[pl.ds(source * BLK, BLK)],
            rings[p].at[pl.ds(target * BLK, BLK)],
            sem_ring_s.at[p],
            sem_ring_r.at[target, p],
            dev=where,
        )

    def ring_starts(step, p):
        if step < 4:
            return [ring_copy(step, p, True), ring_copy(step, p, False)]
        return [ring_copy(4, p, p < 2)]

    def ring_step(step):
        for p in range(4):
            arriving = ring_starts(step, p)
            leaving_now = ring_starts(step + 1, p)
            for copy in arriving:
                copy.wait_recv()
            for copy in leaving_now:
                copy.start()

    pl.semaphore_wait(barrier, n_dev + n_tile - 2)

    for k in range(1, n_z):
        where = lax.rem(dev + 4 * k, n_dev)
        remote(z_labels.at[0], z_labels.at[k], sem_z_lab.at[0], sem_z_lab.at[1], dev=where).start()
    for p in range(4):
        for copy in ring_starts(1, p):
            copy.start()
    halo_c = halo_copies(0, tab_c)
    for copy in halo_c:
        copy.start()

    @pl.loop(1, n_dev)
    def _(d):
        where = lax.rem(dev + d, n_dev)
        remote(labels.at[0], labels.at[d], sem_lab.at[0], sem_lab.at[1], dev=where).start()

    def flip_weights(source, target):
        for o in range(27):
            piece = source[o * CH : (o + 1) * CH, :].astype(F32)
            target[(26 - o) * CH : (27 - o) * CH, :] = piece.T.astype(BF16)

    def expand(table, y):
        for b in range(BLK):
            near = planes.at[b % 2]
            for i in range(6):
                dx = 0 if i == 0 else (2 if i == 5 else 1)
                row = (i + EDGE - 1) % EDGE
                for t in range(9):
                    near[t * PLANE : (t + 1) * PLANE, i * CH : (i + 1) * CH] = table[
                        nbr[b, dx * 9 + t], row
                    ]
            moved = dot(smat[...], near[...]).astype(BF16)
            for i in range(6):
                for t in range(9):
                    y[b, i, :, t * CH : (t + 1) * CH] = moved[
                        t * PLANE : (t + 1) * PLANE, i * CH : (i + 1) * CH
                    ]

    def columns(y, kx):
        return y[:, kx : kx + EDGE].reshape(BLK * VOX, 9 * CH)

    def conv(y, w):
        return (
            dot(columns(y, 0), w[0 : 9 * CH, :])
            + dot(columns(y, 1), w[9 * CH : 18 * CH, :])
            + dot(columns(y, 2), w[18 * CH : 27 * CH, :])
        )

    load_w2.wait()
    flip_weights(w2, wt2)
    load_w1.wait()
    flip_weights(w1, wt1)
    load_smat.wait()
    load_nbr.wait()
    ring_step(1)
    finish_halo(halo_c, tab_c)
    expand(tab_c, y_c)
    ring_step(2)
    hidden_grad[...] = conv(y_c, wt2)
    await_bytes(z_labels.at[pl.ds(1, n_z - 1)], sem_z_lab.at[1])
    z_pos = jnp.full((8, CH), -1, I32)
    for k in range(n_z):
        z_pos = jnp.where(lane // BLK == k, z_labels[k], z_pos)
    for dy in range(4):
        wanted = (z * 4 + lax.rem(y + dy, 4)) * BLK + sub
        found = jnp.min(jnp.where(z_pos == wanted, lane, 8 * BLK), axis=1, keepdims=True)
        z_slotv[dy] = jnp.broadcast_to(found, (8, CH))
    to_z_slots = pltpu.make_async_copy(z_slotv, z_slots, sem_local.at[0])
    to_z_slots.start()
    to_z_slots.wait()
    ring_step(3)

    def y_copy(p, dy):
        where = dict(dev=z * 4 + lax.rem(y + dy, 4))
        return remote(y_send.at[p, dy], y_got.at[p, dy - 1], sem_y.at[0, p], sem_y.at[1, p], **where)

    for p in (0, 2, 1, 3):
        for copy in ring_starts(4, p):
            copy.wait_recv()
        for dy in (2, 1, 3, 0):
            for s in range(BLK):
                y_send[p, dy, s] = rings[p][z_slots[dy, s, 0]]
            if dy:
                y_copy(p, dy).start()
    for p in (0, 2, 1, 3):
        await_bytes(y_got.at[p], sem_y.at[1, p])
        rows = y_send[p, 0].astype(F32)
        for dy in range(3):
            rows = rows + y_got[p, dy].astype(F32)
        own[0, :, p * PLANE : (p + 1) * PLANE, :] = rows.astype(BF16)
    tab_m[0:BLK] = own[0].reshape(BLK, EDGE, PLANE, CH)
    pack_rims(own.at[0], 1)
    halo_m = halo_copies(1, tab_m)
    for copy in halo_m:
        copy.start()
    await_bytes(labels.at[pl.ds(1, n_dev - 1)], sem_lab.at[1])
    label_at = jnp.zeros((8, CH), I32)
    for d in range(n_dev):
        label_at = jnp.where(lane // 2 == d, labels[d], label_at)
    slotv[0] = jnp.minimum(label_at, BLK - 1)
    to_slots = pltpu.make_async_copy(slotv, slots, sem_local.at[0])
    to_slots.start()
    to_slots.wait()
    finish_halo(halo_m, tab_m)
    expand(tab_m, y_m)
    pre = conv(y_m, w1)
    gate = jax.nn.sigmoid(pre)
    hidden = (pre * gate).astype(BF16)
    pre_grad = (hidden_grad[...] * gate * (1.0 + pre * (1.0 - gate))).astype(BF16)
    tab_h[0:BLK] = hidden.reshape(BLK, EDGE, PLANE, CH)
    tab_p[0:BLK] = pre_grad.reshape(BLK, EDGE, PLANE, CH)
    own[1] = hidden.reshape(BLK, VOX, CH)
    own[2] = pre_grad.reshape(BLK, VOX, CH)
    pack_rims(own.at[1], 2)
    pack_rims(own.at[2], 3)
    halo_h = halo_copies(2, tab_h)
    halo_p = halo_copies(3, tab_p)
    for copy in halo_h + halo_p:
        copy.start()

    partner = dict(tile=tile + 1 - 2 * core)

    def core_copy(q, chunk):
        start = pl.multiple_of((1 - core) * HALF + chunk * QUARTER, 16)
        return remote(
            grads.at[q, pl.ds(start, QUARTER)],
            core_in.at[q, chunk],
            sem_sum_s.at[q, 0],
            sem_core.at[q, chunk],
            **partner,
        )

    dims = (("x", "y"), ("y", "x"))
    place = dict(x=chip_x, y=y)

    def start_core(q):
        for e in (2, 1, 3, 0):
            core_copy(q, lax.rem(place[dims[q][0]] + e, 4)).start()

    hidden_t = own[1].reshape(BLK * VOX, CH).astype(F32).T.astype(BF16)
    for kx in range(3):
        part = dot(hidden_t, columns(y_c, kx))
        for t in range(9):
            o = 26 - (kx * 9 + t)
            grads[1, o * CH : (o + 1) * CH, :] = part[:, t * CH : (t + 1) * CH]
    start_core(1)
    pre_grad_t = own[2].reshape(BLK * VOX, CH).astype(F32).T.astype(BF16)
    for kx in range(3):
        part = dot(pre_grad_t, columns(y_m, kx))
        for t in range(9):
            o = kx * 9 + t
            grads[0, o * CH : (o + 1) * CH, :] = part[:, t * CH : (t + 1) * CH].T
    start_core(0)

    def peer(dim, e):
        if dim == "x":
            other = lax.rem(chip_x + e, n_x)
            return other, dict(tile=other * 2 + core)
        if dim == "y":
            other = lax.rem(y + e, 4)
            return other, dict(dev=z * 4 + other)
        other = lax.rem(z + e, n_z)
        return other, dict(dev=other * 4 + y)

    def sem(q, stage):
        return sem_sum_s.at[q, stage], sem_sum_r.at[q, stage]

    def both_cores(q, chunk):
        start = pl.multiple_of(core * HALF + chunk * QUARTER, 16)
        return grads[q, pl.ds(start, QUARTER), :] + core_in[q, chunk]

    def start_first(q):
        for e in (2, 1, 3):
            other, where = peer(dims[q][0], e)
            core_copy(q, other).wait_recv()
            x_out[q, other] = both_cores(q, other).astype(BF16)
            remote(x_out.at[q, other], x_in.at[q, e - 1], *sem(q, 1), **where).start()
        core_copy(q, place[dims[q][0]]).wait_recv()

    def start_second(q):
        await_bytes(x_in.at[q], sem_sum_r.at[q, 1])
        total = both_cores(q, place[dims[q][0]])
        for e in range(3):
            total = total + x_in[q, e].astype(F32)
        own_sum[q, 0:QUARTER] = total
        own_sum[q, QUARTER:] = jnp.zeros((4 * PIECE - QUARTER, CH), F32)
        for j in range(4):
            y_out[q, j] = own_sum[q, j * PIECE : (j + 1) * PIECE].astype(BF16)
        for e in (2, 1, 3):
            other, where = peer(dims[q][1], e)
            remote(y_out.at[q, other], y_in.at[q, e - 1], *sem(q, 2), **where).start()

    def start_third(q):
        await_bytes(y_in.at[q], sem_sum_r.at[q, 2])
        start = pl.multiple_of(place[dims[q][1]] * PIECE, 16)
        total = own_sum[q, pl.ds(start, PIECE), :]
        for e in range(3):
            total = total + y_in[q, e].astype(F32)
        z_out[q, 0:7] = total.reshape(7, 16, CH)
        z_out[q, 7] = jnp.zeros((16, CH), F32)
        for e in (4, 3, 5, 2, 6, 1, 7):
            other, where = peer("z", e)
            remote(z_out.at[q, other], z_in.at[q, e - 1], *sem(q, 3), **where).start()

    def start_gather_third(q):
        await_bytes(z_in.at[q], sem_sum_r.at[q, 3])
        total = z_out[q, z]
        for e in range(7):
            total = total + z_in[q, e]
        mine = final.at[q, core, place[dims[q][0]], place[dims[q][1]], z]
        mine[...] = (total * scale).astype(BF16)
        for e in (4, 3, 5, 2, 6, 1, 7):
            _, where = peer("z", e)
            remote(mine, mine, *sem(q, 4), **where).start()

    def start_gather_second(q):
        await_bytes(final.at[q, core, 0, 0, pl.ds(0, 7)], sem_sum_r.at[q, 4])
        mine = final.at[q, core, place[dims[q][0]], place[dims[q][1]], pl.ds(0, 7)]
        for e in (2, 1, 3):
            _, where = peer(dims[q][1], e)
            remote(mine, mine, *sem(q, 5), **where).start()

    def gather_core_copy(q, chunk):
        piece = final.at[q, core, chunk, :, pl.ds(0, 7)]
        return remote(piece, piece, *sem(q, 7), **partner)

    def exit_copy(q, chunk):
        return pltpu.make_async_copy(
            final.at[q, core, chunk], out_sums.at[q, core, chunk], sem_out.at[q, chunk]
        )

    def gather_first_copy(q, e):
        mine = final.at[q, core, place[dims[q][0]], :, pl.ds(0, 7)]
        _, where = peer(dims[q][0], e)
        return remote(mine, mine, sem_sum_s.at[q, 6], sem_first.at[q, e - 1], **where)

    def start_gather_first(q):
        await_bytes(final.at[q, core, 0, pl.ds(0, 3), pl.ds(0, 7)], sem_sum_r.at[q, 5])
        for e in (2, 1, 3):
            gather_first_copy(q, e).start()
        gather_core_copy(q, place[dims[q][0]]).start()
        exit_copy(q, place[dims[q][0]]).start()

    def start_gather_core(q):
        for e in (1, 3, 2):
            chunk = lax.rem(place[dims[q][0]] + 4 - e, 4)
            gather_first_copy(q, e).wait_recv()
            gather_core_copy(q, chunk).start()
            exit_copy(q, chunk).start()

    start_first(1)
    start_first(0)
    finish_halo(halo_h, tab_h)
    expand(tab_h, y_x)
    pre_two = conv(y_x, w2)
    leaving[0] = (
        (own[0].reshape(BLK * VOX, CH).astype(F32) + pre_two).astype(BF16).reshape(BLK, VOX, CH)
    )
    exit_output = pltpu.make_async_copy(leaving.at[0], out_output, sem_out.at[0, 5])
    exit_output.start()
    finish_halo(halo_p, tab_p)
    expand(tab_p, y_x)
    back = conv(y_x, wt1) + cot[...].reshape(BLK * VOX, CH).astype(F32)
    own[1] = back.astype(BF16).reshape(BLK, VOX, CH)

    @pl.loop(0, n_dev)
    def _(d):
        for c in range(2):
            repacked[d, c] = own[1, slots[0, 0, 2 * d + c]]

    returned[0] = repacked[0]

    order = [7 * i % n_dev for i in range(1, n_dev)]

    def send_back(offsets):
        for d in offsets:
            where = lax.rem(dev - d + n_dev, n_dev)
            remote(repacked.at[d], returned.at[d], sem_back.at[0], sem_back.at[1], dev=where).start()

    for stage, offsets in (
        (start_second, order[0:5]),
        (start_third, order[5:8]),
        (start_gather_third, order[8:12]),
        (start_gather_second, order[12:20]),
        (start_gather_first, order[20:]),
        (start_gather_core, []),
    ):
        stage(1)
        stage(0)
        send_back(offsets)
    await_bytes(returned.at[pl.ds(1, n_dev - 1)], sem_back.at[1])
    for r in range(BLK):
        linear = idxs[1, r, 0]
        leaving[1, r] = returned[linear // 2, lax.rem(linear, 2)]
    exit_grad = pltpu.make_async_copy(leaving.at[1], out_grad, sem_out.at[1, 5])
    exit_grad.start()

    await_bytes(labels.at[pl.ds(1, n_dev - 1)], sem_lab.at[0])
    await_bytes(z_labels.at[pl.ds(1, n_z - 1)], sem_z_lab.at[0])
    for p in range(4):
        await_bytes(rings[p].at[pl.ds(0, 7 * BLK)], sem_ring_s.at[p])
        await_bytes(y_got.at[p], sem_y.at[0, p])
    await_bytes(repacked.at[pl.ds(1, n_dev - 1)], sem_back.at[0])
    for q in (1, 0):
        await_bytes(final.at[q, 1 - core, :, :, pl.ds(0, 7)], sem_sum_r.at[q, 7])
        pltpu.make_async_copy(
            final.at[q, 1 - core], out_sums.at[q, 1 - core], sem_out.at[q, 4]
        ).start()
    for q in range(2):
        await_bytes(core_in.at[q], sem_sum_s.at[q, 0])
        await_bytes(x_in.at[q], sem_sum_s.at[q, 1])
        await_bytes(y_in.at[q], sem_sum_s.at[q, 2])
        await_bytes(z_in.at[q], sem_sum_s.at[q, 3])
        await_bytes(final.at[q, core, 0, 0, pl.ds(0, 7)], sem_sum_s.at[q, 4])
        await_bytes(final.at[q, core, 0, pl.ds(0, 3), pl.ds(0, 7)], sem_sum_s.at[q, 5])
        await_bytes(final.at[q, core, pl.ds(0, 3), :, pl.ds(0, 7)], sem_sum_s.at[q, 6])
        await_bytes(final.at[q, core, :, :, pl.ds(0, 7)], sem_sum_s.at[q, 7])
        for chunk in range(4):
            exit_copy(q, chunk).wait()
        pltpu.make_async_copy(
            final.at[q, 1 - core], out_sums.at[q, 1 - core], sem_out.at[q, 4]
        ).wait()
    exit_output.wait()
    exit_grad.wait()


def finish_kernel(
    sums, output_in, grad_in, output, grad, grad_one, grad_two, rows_held, held, wide, sem_load, sem_store, sem_pass
):
    passes = [
        pltpu.make_async_copy(output_in, rows_held.at[0], sem_pass.at[0]),
        pltpu.make_async_copy(grad_in, rows_held.at[1], sem_pass.at[1]),
    ]
    parts = [(q, c, j) for c in range(2) for j in range(4) for q in range(2)]
    loads = [pltpu.make_async_copy(sums.at[part], held.at[part], sem_load.at[part]) for part in parts]
    for copy in passes + loads:
        copy.start()
    stores = [
        pltpu.make_async_copy(rows_held.at[0], output, sem_pass.at[2]),
        pltpu.make_async_copy(rows_held.at[1], grad, sem_pass.at[3]),
    ]
    for copy, store in zip(passes, stores):
        copy.wait()
        store.start()
    for part, load in zip(parts, loads):
        q, c, j = part
        load.wait()
        rows = held[q, c, j, :, 0:7].reshape(4 * PIECE, CH)
        wide[q, c, j] = rows[0:QUARTER].astype(F32)
        target = (grad_one, grad_two)[q].at[pl.ds(c * HALF + j * QUARTER, QUARTER)]
        stores.append(pltpu.make_async_copy(wide.at[part], target, sem_store.at[part]))
        stores[-1].start()
    for copy in stores:
        copy.wait()


def per_device(
    n_tile, n_dev, features, morton_pos, neighbours, rim, cotangent, weight_one, weight_two
):
    blocks, voxels, channels = features.shape
    scale = 1.0 / math.sqrt(blocks * voxels * n_tile * n_dev)
    n_x = n_tile // 2
    hbm = pl.BlockSpec(memory_space=pltpu.HBM)
    dma = pltpu.SemaphoreType.DMA
    block_table = pltpu.VMEM((BLK + 4 * RIM + 1, EDGE, PLANE, CH), BF16)
    wide = pltpu.VMEM((BLK, 6, PLANE, 9 * CH), BF16)
    flat = pltpu.VMEM((BLK * VOX, CH), F32)
    ring = pltpu.VMEM((9 * BLK, PLANE, CH), BF16)
    slab = pltpu.VMEM((n_dev, 2, VOX, CH), BF16)
    output, input_grad, sums = pl.pallas_call(
        functools.partial(unit_kernel, n_tile, n_dev, scale),
        out_shape=(
            jax.ShapeDtypeStruct(features.shape, BF16),
            jax.ShapeDtypeStruct(features.shape, BF16),
            jax.ShapeDtypeStruct((2, 2, 4, 4, 8, 16, CH), BF16),
        ),
        in_specs=[hbm] * 8,
        out_specs=(hbm, hbm, hbm),
        scratch_shapes=[
            pltpu.SMEM(morton_pos.shape, I32),
            pltpu.SMEM(neighbours.shape, I32),
            pltpu.SMEM(rim.shape, I32),
            pltpu.VMEM(features.shape, BF16),
            pltpu.VMEM(cotangent.shape, BF16),
            pltpu.VMEM(weight_one.shape, BF16),
            pltpu.VMEM(weight_two.shape, BF16),
            pltpu.VMEM((9 * PLANE, 9 * PLANE), BF16),
            pltpu.VMEM((2, 8, CH), I32),
            pltpu.SMEM((2, 8, CH), I32),
            pltpu.VMEM((2, 8, CH), I32),
            pltpu.SMEM((2, 8, CH), I32),
            pltpu.VMEM((n_dev, 1, CH), I32),
            pltpu.VMEM((8, 1, CH), I32),
            pltpu.VMEM((4, 8, CH), I32),
            pltpu.SMEM((4, 8, CH), I32),
            ring,
            ring,
            ring,
            ring,
            pltpu.VMEM((4, 4, BLK, PLANE, CH), BF16),
            pltpu.VMEM((4, 3, BLK, PLANE, CH), BF16),
            slab,
            slab,
            block_table,
            block_table,
            block_table,
            block_table,
            pltpu.VMEM((3, BLK, VOX, CH), BF16),
            pltpu.VMEM((2, BLK, VOX, CH), BF16),
            pltpu.VMEM((4, RIM, EDGE, PLANE, CH), BF16),
            pltpu.VMEM((27 * CH, CH), BF16),
            pltpu.VMEM((27 * CH, CH), BF16),
            pltpu.VMEM((2, 9 * PLANE, 6 * CH), BF16),
            wide,
            wide,
            wide,
            flat,
            flat,
            pltpu.VMEM((2, 27 * CH, CH), F32),
            pltpu.VMEM((2, 4, QUARTER, CH), F32),
            pltpu.VMEM((2, 4, QUARTER, CH), BF16),
            pltpu.VMEM((2, 3, QUARTER, CH), BF16),
            pltpu.VMEM((2, 4, PIECE, CH), BF16),
            pltpu.VMEM((2, 3, PIECE, CH), BF16),
            pltpu.VMEM((2, 4 * PIECE, CH), F32),
            pltpu.VMEM((2, 8, 16, CH), F32),
            pltpu.VMEM((2, 7, 16, CH), F32),
            pltpu.VMEM((2, 2, 4, 4, 8, 16, CH), BF16),
            dma((8,)),
            dma((1,)),
            dma((4,)),
            dma((8, 4)),
            dma((2, 4)),
            dma((2,)),
            dma((2,)),
            dma((2,)),
            dma((4, 4)),
            dma((4, 4)),
            dma((2, 8)),
            dma((2, 8)),
            dma((2, 3)),
            dma((2, 4)),
            dma((2, 6)),
        ],
        compiler_params=pltpu.CompilerParams(
            collective_id=0, has_side_effects=True, vmem_limit_bytes=62 * 1024 * 1024
        ),
    )(
        morton_pos,
        neighbours,
        rim,
        features,
        cotangent,
        weight_one,
        weight_two,
        jnp.asarray(shift_matrix(), BF16),
    )
    kernel_shape = jax.ShapeDtypeStruct(weight_one.shape, F32)
    return pl.pallas_call(
        finish_kernel,
        out_shape=(
            jax.ShapeDtypeStruct(features.shape, BF16),
            jax.ShapeDtypeStruct(features.shape, BF16),
            kernel_shape,
            kernel_shape,
        ),
        in_specs=[hbm] * 3,
        out_specs=(hbm,) * 4,
        scratch_shapes=[
            pltpu.VMEM((2,) + features.shape, BF16),
            pltpu.VMEM((2, 2, 4, 4, 8, 16, CH), BF16),
            pltpu.VMEM((2, 2, 4, QUARTER, CH), F32),
            dma((2, 2, 4)),
            dma((2, 2, 4)),
            dma((4,)),
        ],
        compiler_params=pltpu.CompilerParams(vmem_limit_bytes=62 * 1024 * 1024),
    )(sums, output, input_grad)


def solution(mesh):
    placed = (
        P(("tile", "dev"), None, None),
        P(("tile", "dev")),
        P(("tile", "dev"), None),
        P(("tile", "dev")),
        P(("tile", "dev"), None, None),
        P(),
        P(),
    )
    return jax.shard_map(
        functools.partial(per_device, mesh.shape["tile"], mesh.shape["dev"]),
        mesh=mesh,
        in_specs=placed,
        out_specs=(P(("tile", "dev"), None, None), P(("tile", "dev"), None, None), P(), P()),
        check_vma=False,
    )
```

```python
import functools
import math

import jax
import jax.numpy as jnp
import numpy as np
from jax import lax
from jax.experimental import pallas as pl
from jax.experimental.pallas import tpu as pltpu
from jax.sharding import PartitionSpec as P

EDGE = 4
PLANE = EDGE * EDGE
BLK = 8
VOX = 64
CH = 128
RIM = 4
HALF = 27 * CH // 2
QUARTER = HALF // 4
TILES = QUARTER // 16
PIECE = 7 * 16
F32 = jnp.float32
BF16 = jnp.bfloat16
I32 = jnp.int32


def shift_matrix():
    result = np.zeros((9 * PLANE, 9 * PLANE), np.float32)
    for ky in range(3):
        for kz in range(3):
            for j in range(EDGE):
                for k in range(EDGE):
                    y, z = j + ky - 1, k + kz - 1
                    dy, dz = y // EDGE + 1, z // EDGE + 1
                    source = ((dy * 3 + dz) * EDGE + y % EDGE) * EDGE + z % EDGE
                    result[((ky * 3 + kz) * EDGE + j) * EDGE + k, source] = 1.0
    return result


def dot(left, right):
    return jnp.dot(left, right, preferred_element_type=F32)


def unit_kernel(
    n_tile,
    n_dev,
    scale,
    pos_in,
    nbr_in,
    rim_in,
    feat_in,
    cot_in,
    w1_in,
    w2_in,
    smat_in,
    out_output,
    out_grad,
    out_sums,
    pos,
    nbr,
    rim,
    feat,
    cot,
    w1,
    w2,
    smat,
    idxv,
    idxs,
    slotv,
    slots,
    labels,
    z_labels,
    z_slotv,
    z_slots,
    ring_0,
    ring_1,
    ring_2,
    ring_3,
    y_send,
    y_got,
    repacked,
    returned,
    tab_m,
    tab_c,
    tab_h,
    tab_p,
    own,
    leaving,
    rims,
    wt1,
    wt2,
    planes,
    y_m,
    y_c,
    y_x,
    pre_one,
    hidden_grad,
    grads,
    core_in,
    x_out,
    x_in,
    y_out,
    y_in,
    own_sum,
    z_out,
    z_in,
    final,
    sem_in,
    sem_local,
    sem_ring_s,
    sem_ring_r,
    sem_y,
    sem_z_lab,
    sem_lab,
    sem_back,
    sem_halo_s,
    sem_halo_r,
    sem_sum_s,
    sem_sum_r,
    sem_first,
    sem_core,
    sem_out,
):
    tile = lax.axis_index("tile")
    dev = lax.axis_index("dev")
    core = lax.rem(tile, 2)
    chip_x = tile // 2
    n_x = n_tile // 2

    def remote(src, dst, send, recv, **where):
        return pltpu.make_async_remote_copy(
            src_ref=src,
            dst_ref=dst,
            send_sem=send,
            recv_sem=recv,
            device_id=where,
            device_id_type=pl.DeviceIdType.MESH,
        )

    def await_bytes(ref, sem):
        pltpu.make_async_copy(ref, ref, sem).wait()

    operands = (pos_in, rim_in, feat_in, cot_in, w2_in, w1_in, smat_in, nbr_in)
    places = (pos, rim, feat, cot, w2, w1, smat, nbr)
    loads = [
        pltpu.make_async_copy(source, place, sem_in.at[i])
        for i, (source, place) in enumerate(zip(operands, places))
    ]
    load_pos, load_rim, load_feat, load_cot, load_w2, load_w1, load_smat, load_nbr = loads
    for load in loads:
        load.start()
    for table in (tab_m, tab_c, tab_h, tab_p):
        table[BLK + 2 * RIM :] = jnp.zeros((2 * RIM + 1, EDGE, PLANE, CH), BF16)
    barrier = pltpu.get_barrier_semaphore()

    @pl.loop(1, n_dev)
    def _(d):
        pl.semaphore_signal(barrier, inc=1, device_id={"dev": lax.rem(dev + d, n_dev)})

    @pl.loop(1, n_tile)
    def _(d):
        pl.semaphore_signal(barrier, inc=1, device_id={"tile": lax.rem(tile + d, n_tile)})

    sub = lax.broadcasted_iota(I32, (8, CH), 0)
    lane = lax.broadcasted_iota(I32, (8, CH), 1)
    load_pos.wait()
    posv = jnp.zeros((8, CH), I32)
    for r in range(BLK):
        posv = jnp.where(sub == r, pos[r], posv)
    owner = posv // BLK
    count = jnp.zeros((8, CH), I32)
    for r in range(BLK):
        count = count + jnp.where((owner == pos[r] // BLK) & (sub > r), 1, 0)
    slot_of_row = lax.rem(owner - dev + n_dev, n_dev) * 2 + count
    hit = lane == slot_of_row
    row_of_slot = jnp.min(jnp.where(hit, sub, BLK - 1), axis=0, keepdims=True)
    label_of_slot = jnp.min(jnp.where(hit, lax.rem(posv, BLK), BLK), axis=0, keepdims=True)
    idxv[0] = jnp.broadcast_to(row_of_slot, (8, CH))
    idxv[1] = jnp.minimum(slot_of_row, 2 * n_dev - 1)
    labels[0] = label_of_slot
    to_scalars = pltpu.make_async_copy(idxv, idxs, sem_local.at[0])
    to_scalars.start()

    def pack_rims(rows, which):
        for h in range(RIM):
            rims[which, h] = rows[rim[h]].reshape(EDGE, PLANE, CH)

    def halo_copies(which, table):
        result = []
        every, low, high = slice(None), pl.ds(0, PLANE // 2), pl.ds(PLANE // 2, PLANE // 2)
        for q, (where, part) in enumerate(
            (
                (dict(tile=lax.rem(tile + 1, n_tile)), (pl.ds(EDGE - 1, 1), every)),
                (dict(tile=lax.rem(tile + n_tile - 1, n_tile)), (pl.ds(0, 1), every)),
                (dict(dev=lax.rem(dev + 1, n_dev)), (every, high)),
                (dict(dev=lax.rem(dev + n_dev - 1, n_dev)), (every, low)),
            )
        ):
            result.append(
                remote(
                    rims.at[(which, every) + part],
                    table.at[(pl.ds(BLK + q * RIM, RIM),) + part],
                    sem_halo_s.at[which, q],
                    sem_halo_r.at[which, q],
                    **where,
                )
            )
        return result

    def finish_halo(copies, table):
        for copy in copies:
            copy.wait()
        edges = (tile == 0, tile == n_tile - 1, dev == 0, dev == n_dev - 1)
        for q, edge in enumerate(edges):

            @pl.when(edge)
            def _(q=q):
                table[BLK + q * RIM : BLK + (q + 1) * RIM] = jnp.zeros((RIM, EDGE, PLANE, CH), BF16)

    load_rim.wait()
    load_cot.wait()
    tab_c[0:BLK] = cot[...].reshape(BLK, EDGE, PLANE, CH)
    pack_rims(cot, 0)
    load_feat.wait()
    to_scalars.wait()

    rings = (ring_0, ring_1, ring_2, ring_3)
    for p, ring in enumerate(rings):
        ring[0:BLK] = feat[:, p * PLANE : (p + 1) * PLANE, :]
        ring[8 * BLK] = jnp.zeros((PLANE, CH), BF16)
    pos_lanes = jnp.zeros((1, CH), I32)
    for r in range(BLK):
        pos_lanes = jnp.where(lax.rem(lane[0:1], BLK) == r, pos[r], pos_lanes)
    z_labels[0] = pos_lanes

    y = lax.rem(dev, 4)
    z = dev // 4
    n_z = n_dev // 4

    def ring_copy(step, p, ahead):
        source = step - 1 if ahead else (9 - step) % 8
        target = step if ahead else 8 - step
        where = lax.rem(dev + (4 if ahead else n_dev - 4), n_dev)
        return remote(
            rings[p].at[pl.ds(source * BLK, BLK)],
            rings[p].at[pl.ds(target * BLK, BLK)],
            sem_ring_s.at[p],
            sem_ring_r.at[target, p],
            dev=where,
        )

    def ring_starts(step, p):
        if step < 4:
            return [ring_copy(step, p, True), ring_copy(step, p, False)]
        return [ring_copy(4, p, p < 2)]

    def ring_step(step):
        for p in range(4):
            arriving = ring_starts(step, p)
            leaving_now = ring_starts(step + 1, p)
            for copy in arriving:
                copy.wait_recv()
            for copy in leaving_now:
                copy.start()

    pl.semaphore_wait(barrier, n_dev + n_tile - 2)

    for k in range(1, n_z):
        where = lax.rem(dev + 4 * k, n_dev)
        remote(z_labels.at[0], z_labels.at[k], sem_z_lab.at[0], sem_z_lab.at[1], dev=where).start()
    for p in range(4):
        for copy in ring_starts(1, p):
            copy.start()
    halo_c = halo_copies(0, tab_c)
    for copy in halo_c:
        copy.start()

    @pl.loop(1, n_dev)
    def _(d):
        where = lax.rem(dev + d, n_dev)
        remote(labels.at[0], labels.at[d], sem_lab.at[0], sem_lab.at[1], dev=where).start()

    def flip_weights(source, target):
        for o in range(27):
            piece = source[o * CH : (o + 1) * CH, :].astype(F32)
            target[(26 - o) * CH : (27 - o) * CH, :] = piece.T.astype(BF16)

    def expand(table, y):
        for b in range(BLK):
            near = planes.at[b % 2]
            for i in range(6):
                dx = 0 if i == 0 else (2 if i == 5 else 1)
                row = (i + EDGE - 1) % EDGE
                for t in range(9):
                    near[t * PLANE : (t + 1) * PLANE, i * CH : (i + 1) * CH] = table[
                        nbr[b, dx * 9 + t], row
                    ]
            moved = dot(smat[...], near[...]).astype(BF16)
            for i in range(6):
                for t in range(9):
                    y[b, i, :, t * CH : (t + 1) * CH] = moved[
                        t * PLANE : (t + 1) * PLANE, i * CH : (i + 1) * CH
                    ]

    def columns(y, kx):
        return y[:, kx : kx + EDGE].reshape(BLK * VOX, 9 * CH)

    def conv(y, w):
        return (
            dot(columns(y, 0), w[0 : 9 * CH, :])
            + dot(columns(y, 1), w[9 * CH : 18 * CH, :])
            + dot(columns(y, 2), w[18 * CH : 27 * CH, :])
        )

    load_w2.wait()
    flip_weights(w2, wt2)
    load_w1.wait()
    flip_weights(w1, wt1)
    load_smat.wait()
    load_nbr.wait()
    ring_step(1)
    finish_halo(halo_c, tab_c)
    expand(tab_c, y_c)
    ring_step(2)
    hidden_grad[...] = conv(y_c, wt2)
    await_bytes(z_labels.at[pl.ds(1, n_z - 1)], sem_z_lab.at[1])
    z_pos = jnp.full((8, CH), -1, I32)
    for k in range(n_z):
        z_pos = jnp.where(lane // BLK == k, z_labels[k], z_pos)
    for dy in range(4):
        wanted = (z * 4 + lax.rem(y + dy, 4)) * BLK + sub
        found = jnp.min(jnp.where(z_pos == wanted, lane, 8 * BLK), axis=1, keepdims=True)
        z_slotv[dy] = jnp.broadcast_to(found, (8, CH))
    to_z_slots = pltpu.make_async_copy(z_slotv, z_slots, sem_local.at[0])
    to_z_slots.start()
    to_z_slots.wait()
    ring_step(3)

    def y_copy(p, dy):
        where = dict(dev=z * 4 + lax.rem(y + dy, 4))
        return remote(y_send.at[p, dy], y_got.at[p, dy - 1], sem_y.at[0, p], sem_y.at[1, p], **where)

    for p in (0, 2, 1, 3):
        for copy in ring_starts(4, p):
            copy.wait_recv()
        for dy in (2, 1, 3, 0):
            for s in range(BLK):
                y_send[p, dy, s] = rings[p][z_slots[dy, s, 0]]
            if dy:
                y_copy(p, dy).start()
    for p in (0, 2, 1, 3):
        await_bytes(y_got.at[p], sem_y.at[1, p])
        rows = y_send[p, 0].astype(F32)
        for dy in range(3):
            rows = rows + y_got[p, dy].astype(F32)
        own[0, :, p * PLANE : (p + 1) * PLANE, :] = rows.astype(BF16)
    tab_m[0:BLK] = own[0].reshape(BLK, EDGE, PLANE, CH)
    pack_rims(own.at[0], 1)
    halo_m = halo_copies(1, tab_m)
    for copy in halo_m:
        copy.start()
    await_bytes(labels.at[pl.ds(1, n_dev - 1)], sem_lab.at[1])
    label_at = jnp.zeros((8, CH), I32)
    for d in range(n_dev):
        label_at = jnp.where(lane // 2 == d, labels[d], label_at)
    slotv[0] = jnp.minimum(label_at, BLK - 1)
    to_slots = pltpu.make_async_copy(slotv, slots, sem_local.at[0])
    to_slots.start()
    to_slots.wait()
    finish_halo(halo_m, tab_m)
    expand(tab_m, y_m)
    pre = conv(y_m, w1)
    gate = jax.nn.sigmoid(pre)
    hidden = (pre * gate).astype(BF16)
    pre_grad = (hidden_grad[...] * gate * (1.0 + pre * (1.0 - gate))).astype(BF16)
    tab_h[0:BLK] = hidden.reshape(BLK, EDGE, PLANE, CH)
    tab_p[0:BLK] = pre_grad.reshape(BLK, EDGE, PLANE, CH)
    own[1] = hidden.reshape(BLK, VOX, CH)
    own[2] = pre_grad.reshape(BLK, VOX, CH)

    partner = dict(tile=tile + 1 - 2 * core)

    def core_copy(q, chunk):
        start = pl.multiple_of((1 - core) * HALF + chunk * QUARTER, 16)
        return remote(
            grads.at[q, pl.ds(start, QUARTER)],
            core_in.at[q, chunk],
            sem_sum_s.at[q, 0],
            sem_core.at[q, chunk],
            **partner,
        )

    dims = (("x", "y"), ("y", "x"))
    place = dict(x=chip_x, y=y)

    def start_core(q):
        for e in (2, 1, 3, 0):
            core_copy(q, lax.rem(place[dims[q][0]] + e, 4)).start()

    hidden_t = own[1].reshape(BLK * VOX, CH).astype(F32).T.astype(BF16)
    for kx in range(3):
        part = dot(hidden_t, columns(y_c, kx))
        for t in range(9):
            o = 26 - (kx * 9 + t)
            grads[1, o * CH : (o + 1) * CH, :] = part[:, t * CH : (t + 1) * CH]
    start_core(1)
    pack_rims(own.at[1], 2)
    pack_rims(own.at[2], 3)
    halo_h = halo_copies(2, tab_h)
    halo_p = halo_copies(3, tab_p)
    for copy in halo_h + halo_p:
        copy.start()
    pre_grad_t = own[2].reshape(BLK * VOX, CH).astype(F32).T.astype(BF16)
    for kx in range(3):
        part = dot(pre_grad_t, columns(y_m, kx))
        for t in range(9):
            o = kx * 9 + t
            grads[0, o * CH : (o + 1) * CH, :] = part[:, t * CH : (t + 1) * CH].T
    start_core(0)

    def peer(dim, e):
        if dim == "x":
            other = lax.rem(chip_x + e, n_x)
            return other, dict(tile=other * 2 + core)
        if dim == "y":
            other = lax.rem(y + e, 4)
            return other, dict(dev=z * 4 + other)
        other = lax.rem(z + e, n_z)
        return other, dict(dev=other * 4 + y)

    def sem(q, stage):
        return sem_sum_s.at[q, stage], sem_sum_r.at[q, stage]

    def both_cores(q, chunk):
        start = pl.multiple_of(core * HALF + chunk * QUARTER, 16)
        return grads[q, pl.ds(start, QUARTER), :] + core_in[q, chunk]

    def start_first(q):
        for e in (2, 1, 3):
            other, where = peer(dims[q][0], e)
            core_copy(q, other).wait_recv()
            x_out[q, other] = both_cores(q, other).astype(BF16)
            remote(x_out.at[q, other], x_in.at[q, e - 1], *sem(q, 1), **where).start()
        core_copy(q, place[dims[q][0]]).wait_recv()

    def start_second(q):
        await_bytes(x_in.at[q], sem_sum_r.at[q, 1])
        total = both_cores(q, place[dims[q][0]])
        for e in range(3):
            total = total + x_in[q, e].astype(F32)
        own_sum[q, 0:QUARTER] = total
        own_sum[q, QUARTER:] = jnp.zeros((4 * PIECE - QUARTER, CH), F32)
        for j in range(4):
            y_out[q, j] = own_sum[q, j * PIECE : (j + 1) * PIECE].astype(BF16)
        for e in (2, 1, 3):
            other, where = peer(dims[q][1], e)
            remote(y_out.at[q, other], y_in.at[q, e - 1], *sem(q, 2), **where).start()

    def start_third(q):
        await_bytes(y_in.at[q], sem_sum_r.at[q, 2])
        start = pl.multiple_of(place[dims[q][1]] * PIECE, 16)
        total = own_sum[q, pl.ds(start, PIECE), :]
        for e in range(3):
            total = total + y_in[q, e].astype(F32)
        z_out[q, 0:7] = total.reshape(7, 16, CH)
        z_out[q, 7] = jnp.zeros((16, CH), F32)
        for e in (4, 3, 5, 2, 6, 1, 7):
            other, where = peer("z", e)
            remote(z_out.at[q, other], z_in.at[q, e - 1], *sem(q, 3), **where).start()

    def start_gather_third(q):
        await_bytes(z_in.at[q], sem_sum_r.at[q, 3])
        total = z_out[q, z]
        for e in range(7):
            total = total + z_in[q, e]
        mine = final.at[q, core, place[dims[q][0]], place[dims[q][1]], z]
        mine[...] = (total * scale).astype(BF16)
        for e in (4, 3, 5, 2, 6, 1, 7):
            _, where = peer("z", e)
            remote(mine, mine, *sem(q, 4), **where).start()

    def start_gather_second(q):
        await_bytes(final.at[q, core, 0, 0, pl.ds(0, 7)], sem_sum_r.at[q, 4])
        mine = final.at[q, core, place[dims[q][0]], place[dims[q][1]], pl.ds(0, 7)]
        for e in (2, 1, 3):
            _, where = peer(dims[q][1], e)
            remote(mine, mine, *sem(q, 5), **where).start()

    def gather_core_copy(q, chunk):
        piece = final.at[q, core, chunk, :, pl.ds(0, 7)]
        return remote(piece, piece, *sem(q, 7), **partner)

    def exit_copy(q, chunk):
        return pltpu.make_async_copy(
            final.at[q, core, chunk], out_sums.at[q, core, chunk], sem_out.at[q, chunk]
        )

    def gather_first_copy(q, e):
        mine = final.at[q, core, place[dims[q][0]], :, pl.ds(0, 7)]
        _, where = peer(dims[q][0], e)
        return remote(mine, mine, sem_sum_s.at[q, 6], sem_first.at[q, e - 1], **where)

    def start_gather_first(q):
        await_bytes(final.at[q, core, 0, pl.ds(0, 3), pl.ds(0, 7)], sem_sum_r.at[q, 5])
        for e in (2, 1, 3):
            gather_first_copy(q, e).start()
        gather_core_copy(q, place[dims[q][0]]).start()
        exit_copy(q, place[dims[q][0]]).start()

    def start_gather_core(q):
        for e in (1, 3, 2):
            chunk = lax.rem(place[dims[q][0]] + 4 - e, 4)
            gather_first_copy(q, e).wait_recv()
            gather_core_copy(q, chunk).start()
            exit_copy(q, chunk).start()

    start_first(1)
    start_first(0)
    finish_halo(halo_h, tab_h)
    expand(tab_h, y_x)
    pre_two = conv(y_x, w2)
    leaving[0] = (
        (own[0].reshape(BLK * VOX, CH).astype(F32) + pre_two).astype(BF16).reshape(BLK, VOX, CH)
    )
    exit_output = pltpu.make_async_copy(leaving.at[0], out_output, sem_out.at[0, 5])
    exit_output.start()
    finish_halo(halo_p, tab_p)
    expand(tab_p, y_x)
    back = conv(y_x, wt1) + cot[...].reshape(BLK * VOX, CH).astype(F32)
    own[1] = back.astype(BF16).reshape(BLK, VOX, CH)

    @pl.loop(0, n_dev)
    def _(d):
        for c in range(2):
            repacked[d, c] = own[1, slots[0, 0, 2 * d + c]]

    returned[0] = repacked[0]

    order = [7 * i % n_dev for i in range(1, n_dev)]

    def send_back(offsets):
        for d in offsets:
            where = lax.rem(dev - d + n_dev, n_dev)
            remote(repacked.at[d], returned.at[d], sem_back.at[0], sem_back.at[1], dev=where).start()

    for stage, offsets in (
        (start_second, order[0:6]),
        (start_third, order[6:12]),
        (start_gather_third, order[12:18]),
        (start_gather_second, order[18:24]),
        (start_gather_first, order[24:]),
        (start_gather_core, []),
    ):
        stage(1)
        stage(0)
        send_back(offsets)
    await_bytes(returned.at[pl.ds(1, n_dev - 1)], sem_back.at[1])
    for r in range(BLK):
        linear = idxs[1, r, 0]
        leaving[1, r] = returned[linear // 2, lax.rem(linear, 2)]
    exit_grad = pltpu.make_async_copy(leaving.at[1], out_grad, sem_out.at[1, 5])
    exit_grad.start()

    await_bytes(labels.at[pl.ds(1, n_dev - 1)], sem_lab.at[0])
    await_bytes(z_labels.at[pl.ds(1, n_z - 1)], sem_z_lab.at[0])
    for p in range(4):
        await_bytes(rings[p].at[pl.ds(0, 7 * BLK)], sem_ring_s.at[p])
        await_bytes(y_got.at[p], sem_y.at[0, p])
    await_bytes(repacked.at[pl.ds(1, n_dev - 1)], sem_back.at[0])
    for q in (1, 0):
        await_bytes(final.at[q, 1 - core, :, :, pl.ds(0, 7)], sem_sum_r.at[q, 7])
        pltpu.make_async_copy(
            final.at[q, 1 - core], out_sums.at[q, 1 - core], sem_out.at[q, 4]
        ).start()
    for q in range(2):
        await_bytes(core_in.at[q], sem_sum_s.at[q, 0])
        await_bytes(x_in.at[q], sem_sum_s.at[q, 1])
        await_bytes(y_in.at[q], sem_sum_s.at[q, 2])
        await_bytes(z_in.at[q], sem_sum_s.at[q, 3])
        await_bytes(final.at[q, core, 0, 0, pl.ds(0, 7)], sem_sum_s.at[q, 4])
        await_bytes(final.at[q, core, 0, pl.ds(0, 3), pl.ds(0, 7)], sem_sum_s.at[q, 5])
        await_bytes(final.at[q, core, pl.ds(0, 3), :, pl.ds(0, 7)], sem_sum_s.at[q, 6])
        await_bytes(final.at[q, core, :, :, pl.ds(0, 7)], sem_sum_s.at[q, 7])
        for chunk in range(4):
            exit_copy(q, chunk).wait()
        pltpu.make_async_copy(
            final.at[q, 1 - core], out_sums.at[q, 1 - core], sem_out.at[q, 4]
        ).wait()
    exit_output.wait()
    exit_grad.wait()


def finish_kernel(
    sums, output_in, grad_in, output, grad, grad_one, grad_two, rows_held, held, wide, sem_load, sem_store, sem_pass
):
    passes = [
        pltpu.make_async_copy(output_in, rows_held.at[0], sem_pass.at[0]),
        pltpu.make_async_copy(grad_in, rows_held.at[1], sem_pass.at[1]),
    ]
    parts = [(q, c, j) for c in range(2) for j in range(4) for q in range(2)]
    loads = [pltpu.make_async_copy(sums.at[part], held.at[part], sem_load.at[part]) for part in parts]
    for copy in passes + loads:
        copy.start()
    stores = [
        pltpu.make_async_copy(rows_held.at[0], output, sem_pass.at[2]),
        pltpu.make_async_copy(rows_held.at[1], grad, sem_pass.at[3]),
    ]
    for copy, store in zip(passes, stores):
        copy.wait()
        store.start()
    for part, load in zip(parts, loads):
        q, c, j = part
        load.wait()
        rows = held[q, c, j, :, 0:7].reshape(4 * PIECE, CH)
        wide[q, c, j] = rows[0:QUARTER].astype(F32)
        target = (grad_one, grad_two)[q].at[pl.ds(c * HALF + j * QUARTER, QUARTER)]
        stores.append(pltpu.make_async_copy(wide.at[part], target, sem_store.at[part]))
        stores[-1].start()
    for copy in stores:
        copy.wait()


def per_device(
    n_tile, n_dev, features, morton_pos, neighbours, rim, cotangent, weight_one, weight_two
):
    blocks, voxels, channels = features.shape
    scale = 1.0 / math.sqrt(blocks * voxels * n_tile * n_dev)
    n_x = n_tile // 2
    hbm = pl.BlockSpec(memory_space=pltpu.HBM)
    dma = pltpu.SemaphoreType.DMA
    block_table = pltpu.VMEM((BLK + 4 * RIM + 1, EDGE, PLANE, CH), BF16)
    wide = pltpu.VMEM((BLK, 6, PLANE, 9 * CH), BF16)
    flat = pltpu.VMEM((BLK * VOX, CH), F32)
    ring = pltpu.VMEM((9 * BLK, PLANE, CH), BF16)
    slab = pltpu.VMEM((n_dev, 2, VOX, CH), BF16)
    output, input_grad, sums = pl.pallas_call(
        functools.partial(unit_kernel, n_tile, n_dev, scale),
        out_shape=(
            jax.ShapeDtypeStruct(features.shape, BF16),
            jax.ShapeDtypeStruct(features.shape, BF16),
            jax.ShapeDtypeStruct((2, 2, 4, 4, 8, 16, CH), BF16),
        ),
        in_specs=[hbm] * 8,
        out_specs=(hbm, hbm, hbm),
        scratch_shapes=[
            pltpu.SMEM(morton_pos.shape, I32),
            pltpu.SMEM(neighbours.shape, I32),
            pltpu.SMEM(rim.shape, I32),
            pltpu.VMEM(features.shape, BF16),
            pltpu.VMEM(cotangent.shape, BF16),
            pltpu.VMEM(weight_one.shape, BF16),
            pltpu.VMEM(weight_two.shape, BF16),
            pltpu.VMEM((9 * PLANE, 9 * PLANE), BF16),
            pltpu.VMEM((2, 8, CH), I32),
            pltpu.SMEM((2, 8, CH), I32),
            pltpu.VMEM((2, 8, CH), I32),
            pltpu.SMEM((2, 8, CH), I32),
            pltpu.VMEM((n_dev, 1, CH), I32),
            pltpu.VMEM((8, 1, CH), I32),
            pltpu.VMEM((4, 8, CH), I32),
            pltpu.SMEM((4, 8, CH), I32),
            ring,
            ring,
            ring,
            ring,
            pltpu.VMEM((4, 4, BLK, PLANE, CH), BF16),
            pltpu.VMEM((4, 3, BLK, PLANE, CH), BF16),
            slab,
            slab,
            block_table,
            block_table,
            block_table,
            block_table,
            pltpu.VMEM((3, BLK, VOX, CH), BF16),
            pltpu.VMEM((2, BLK, VOX, CH), BF16),
            pltpu.VMEM((4, RIM, EDGE, PLANE, CH), BF16),
            pltpu.VMEM((27 * CH, CH), BF16),
            pltpu.VMEM((27 * CH, CH), BF16),
            pltpu.VMEM((2, 9 * PLANE, 6 * CH), BF16),
            wide,
            wide,
            wide,
            flat,
            flat,
            pltpu.VMEM((2, 27 * CH, CH), F32),
            pltpu.VMEM((2, 4, QUARTER, CH), F32),
            pltpu.VMEM((2, 4, QUARTER, CH), BF16),
            pltpu.VMEM((2, 3, QUARTER, CH), BF16),
            pltpu.VMEM((2, 4, PIECE, CH), BF16),
            pltpu.VMEM((2, 3, PIECE, CH), BF16),
            pltpu.VMEM((2, 4 * PIECE, CH), F32),
            pltpu.VMEM((2, 8, 16, CH), F32),
            pltpu.VMEM((2, 7, 16, CH), F32),
            pltpu.VMEM((2, 2, 4, 4, 8, 16, CH), BF16),
            dma((8,)),
            dma((1,)),
            dma((4,)),
            dma((8, 4)),
            dma((2, 4)),
            dma((2,)),
            dma((2,)),
            dma((2,)),
            dma((4, 4)),
            dma((4, 4)),
            dma((2, 8)),
            dma((2, 8)),
            dma((2, 3)),
            dma((2, 4)),
            dma((2, 6)),
        ],
        compiler_params=pltpu.CompilerParams(
            collective_id=0, has_side_effects=True, vmem_limit_bytes=62 * 1024 * 1024
        ),
    )(
        morton_pos,
        neighbours,
        rim,
        features,
        cotangent,
        weight_one,
        weight_two,
        jnp.asarray(shift_matrix(), BF16),
    )
    kernel_shape = jax.ShapeDtypeStruct(weight_one.shape, F32)
    return pl.pallas_call(
        finish_kernel,
        out_shape=(
            jax.ShapeDtypeStruct(features.shape, BF16),
            jax.ShapeDtypeStruct(features.shape, BF16),
            kernel_shape,
            kernel_shape,
        ),
        in_specs=[hbm] * 3,
        out_specs=(hbm,) * 4,
        scratch_shapes=[
            pltpu.VMEM((2,) + features.shape, BF16),
            pltpu.VMEM((2, 2, 4, 4, 8, 16, CH), BF16),
            pltpu.VMEM((2, 2, 4, QUARTER, CH), F32),
            dma((2, 2, 4)),
            dma((2, 2, 4)),
            dma((4,)),
        ],
        compiler_params=pltpu.CompilerParams(vmem_limit_bytes=62 * 1024 * 1024),
    )(sums, output, input_grad)


def solution(mesh):
    placed = (
        P(("tile", "dev"), None, None),
        P(("tile", "dev")),
        P(("tile", "dev"), None),
        P(("tile", "dev")),
        P(("tile", "dev"), None, None),
        P(),
        P(),
    )
    return jax.shard_map(
        functools.partial(per_device, mesh.shape["tile"], mesh.shape["dev"]),
        mesh=mesh,
        in_specs=placed,
        out_specs=(P(("tile", "dev"), None, None), P(("tile", "dev"), None, None), P(), P()),
        check_vma=False,
    )
```
